512 devices in a mesh: rep: 4 (over y), blk: 32 (over z, core), tp: 4 (over x).
Axes of the slice: x: 4, y: 4, z: 16, core: 2. Of those that a mesh axis runs over, the one named last changes fastest.
Arguments:
- hidden: bfloat16 [16, 2048], P('rep', 'blk'), may hold values from -64 to 64
- ln_gain: float32 [2, 2048], P(None, 'blk'), may hold values from 0.1 to 1.9
- w_qkv: bfloat16 [2, 2048, 3, 2048], P(None, 'blk', None, 'tp'), may hold values from -0.125 to 0.125
- w_fc1: bfloat16 [2, 2048, 8192], P(None, 'blk', 'tp'), may hold values from -0.125 to 0.125
- w_out: bfloat16 [2, 2048, 2048], P(None, 'tp', 'blk'), may hold values from -0.125 to 0.125
- w_fc2: bfloat16 [2, 8192, 2048], P(None, 'tp', 'blk'), may hold values from -0.0625 to 0.0625
- caches: bfloat16 [2, 2, 1024, 32, 2048], P(None, None, ('rep', 'blk'), None, 'tp'), may hold values from -110 to 110
- page_owner: int32 [1024], P(('rep', 'blk')), may hold values from 0 to 15, as said below
- page_used: int32 [1024], P(('rep', 'blk')), may hold values from 0 to 1, as said below
- page_fill: int32 [1024], P(('rep', 'blk')), may hold values from 0 to 32, as said below
- page_tail: int32 [1024], P(('rep', 'blk')), may hold values from 0 to 1
- positions: int32 [16], P('rep'), may hold values from 0 to 4095
Outputs:
- hidden_out: bfloat16 [16, 2048], P('rep', 'blk')
- caches_out: bfloat16 [2, 2, 1024, 32, 2048], P(None, None, ('rep', 'blk'), None, 'tp')
The draws below stay inside these ranges and needn't reach their ends.
Inputs may be any that keep to these rules, and one draw needn't show every extreme that they name: `page_owner`: requests are numbered replica by replica, 4 to a replica. Each request has exactly one page with page_tail 1, which is used and lies among the pages of its own replica; other pages of a request may lie on any replica. `page_used`: every page with page_tail 1 is used. `page_fill`: A used page with page_tail 0 is full; a page with page_tail 1 holds fewer than 32 tokens; an unused page holds 0.
All inputs are finite; a program needn't handle non-finite values.
Results may differ from the reference program's by a relative error of at most 0.012.
The reference program's roundings to bfloat16 on the way (of `normed`, `mlp_act`, `queries` and `attended`) count: a program that leaves them out, or rounds other values in their place, can miss the bound.
Values may be sent and summed in bfloat16 or wider, within the bound.
No kernel may reach another device: no remote copies, remote signals or barrier semaphores. Data moves between devices by JAX's collectives and lax.ppermute only.
A program may use at most 64 MiB of HBM per device.

```python
import jax
import jax.numpy as jnp
from jax import lax

D = 2048
H = 32
HD = 64
ROT = 32
FF = 8192
LAYERS = 2
PAGE = 32
SLOTS = 8
REQ_REP = 4
REQS = 16
SLOTS_REP = 256
SLOTS_ALL = 1024


def page_layout(key):
    base = jax.random.fold_in(key, 11)
    keys = jax.random.split(base, 9)
    rep_total = SLOTS_ALL // SLOTS_REP
    slot_ids = jnp.arange(SLOTS_ALL, dtype=jnp.int32)
    slot_rep = slot_ids // SLOTS_REP
    rank_keys = jax.random.split(keys[0], rep_total)
    ranks = jax.vmap(lambda k: jnp.argsort(jax.random.permutation(k, SLOTS_REP), stable=True))(rank_keys)
    ranks = ranks.reshape(-1).astype(jnp.int32)
    tail = (ranks < REQ_REP).astype(jnp.int32)
    popular = jax.random.permutation(keys[1], REQ_REP).astype(jnp.int32)
    draw_a = jax.random.randint(keys[2], (SLOTS_ALL,), 0, REQ_REP)
    draw_b = jax.random.randint(keys[3], (SLOTS_ALL,), 0, REQ_REP)
    draw_c = jax.random.randint(keys[4], (SLOTS_ALL,), 0, REQ_REP)
    pick = popular[jnp.minimum(jnp.minimum(draw_a, draw_b), draw_c)]
    step_away = jax.random.randint(keys[6], (SLOTS_ALL,), 0, max(rep_total - 1, 1))
    owner_rep = (slot_rep + 1 + step_away) % rep_total
    owner = jnp.where(tail == 1, slot_rep * REQ_REP + ranks, owner_rep * REQ_REP + pick).astype(jnp.int32)
    used_rand = (jax.random.randint(keys[7], (SLOTS_ALL,), 0, 4) != 0).astype(jnp.int32)
    used_rand = jnp.where(ranks == REQ_REP, 0, used_rand)
    used = jnp.where(tail == 1, 1, used_rand).astype(jnp.int32)
    tail_fill = jax.random.randint(keys[8], (SLOTS_ALL,), 0, PAGE)
    fill = jnp.where(tail == 1, tail_fill, jnp.where(used == 1, PAGE, 0)).astype(jnp.int32)
    return (owner, used, fill, tail)


def draw_page_owner(key, part):
    return page_layout(key)[0]


def draw_page_used(key, part):
    return page_layout(key)[1]


def draw_page_fill(key, part):
    return page_layout(key)[2]


def draw_page_tail(key, part):
    return page_layout(key)[3]


def draw_hidden(key, part):
    keys = jax.random.split(jax.random.fold_in(key, 23), 2)
    column = jnp.arange(D, dtype=jnp.float32) / D
    rough = jax.random.uniform(keys[1], (D,), jnp.float32, 0.6, 1.6)
    scale_col = 0.5 * jnp.exp(jnp.log(3.0) * column) * rough
    values = jax.random.normal(keys[0], (REQS, D), jnp.float32) * scale_col[None, :]
    return jnp.clip(values, -64.0, 64.0).astype(jnp.bfloat16)


def draw_caches(key, part):
    keys = jax.random.split(jax.random.fold_in(key, 31), 1)
    shape = (LAYERS, 2, SLOTS_ALL, PAGE, H * HD)
    values = jnp.clip(jax.random.normal(keys[0], shape, jnp.float32), -6.0, 6.0)
    return values.astype(jnp.bfloat16)


def plant(entries, stream_key, least, top_value):
    index_at = [jax.random.randint(jax.random.fold_in(stream_key, axis), (), 0, length) for axis, length in enumerate(entries.shape)]
    main_axis = entries.shape.index(max(entries.shape))
    neighbour = index_at[:main_axis] + [(index_at[main_axis] + 1) % entries.shape[main_axis]] + index_at[main_axis + 1:]
    return entries.at[tuple(index_at)].set(least).at[tuple(neighbour)].set(top_value)


def shard_levels(own_key, shape, shards, smallest, high):
    def one(position, shards_of):
        heights = jax.random.uniform(jax.random.fold_in(jax.random.fold_in(own_key, 6), position), (shards_of,), jnp.float32, smallest / len(shards), high / len(shards))
        return jnp.repeat(jnp.exp(heights), shape[position] // shards_of).reshape((-1,) + (1,) * (len(shape) - position - 1))

    loudness = one(*shards[0])
    for cut in shards[1:]:
        loudness = loudness * one(*cut)
    return loudness


def normal_values(stream_key, extent, spread, most, shards=(), held_as=jnp.bfloat16):
    entries = jax.random.normal(stream_key, extent, jnp.float32) * spread
    if len(shards) > 0:
        entries = shard_levels(stream_key, extent, shards, -0.22, 0.18) * entries
    return jnp.clip(entries, min=-most, max=most).astype(held_as)


def setup_inputs(seed: int = 0) -> dict:
    splits = jax.random.split(jax.random.key(seed), 13)
    return {
        "hidden": draw_hidden(jax.random.fold_in(splits[12], 71), 0),
        "ln_gain": jnp.clip(1.0 + 0.18 * jax.random.normal(splits[1], (LAYERS, D), jnp.float32), 0.1, 1.9),
        "w_qkv": normal_values(splits[2], (LAYERS, D, 3, H * HD), D ** -0.5, 0.125, ((1, 32), (3, 4))),
        "w_fc1": normal_values(splits[3], (LAYERS, D, FF), D ** -0.5, 0.125, ((1, 32), (2, 4))),
        "w_out": normal_values(splits[4], (LAYERS, H * HD, D), (H * HD) ** -0.5, 0.125, ((1, 4), (2, 32))),
        "w_fc2": normal_values(splits[5], (LAYERS, FF, D), FF ** -0.5, 0.0625, ((1, 4), (2, 32))),
        "caches": draw_caches(jax.random.fold_in(splits[12], 71), 0),
        "page_owner": draw_page_owner(jax.random.fold_in(splits[12], 71), 0),
        "page_used": draw_page_used(jax.random.fold_in(splits[12], 71), 0),
        "page_fill": draw_page_fill(jax.random.fold_in(splits[12], 71), 0),
        "page_tail": draw_page_tail(jax.random.fold_in(splits[12], 71), 0),
        "positions": plant(jax.random.randint(splits[11], (REQS,), 0, 4096), jax.random.fold_in(splits[11], 1), 0, 4095).astype(jnp.int32),
    }


EPSILON = 1e-05
LOWEST = -1e+30

def rotate_heads(tensor, positions):
    half_rot = ROT // 2
    steps_f = jnp.arange(half_rot, dtype=jnp.float32)
    inverse = 10000.0 ** (-2.0 * steps_f / ROT)
    angles = positions.astype(jnp.float32)[:, None] * inverse[None, :]
    cosine = jnp.cos(angles)[:, None, :]
    sine_val = jnp.sin(angles)[:, None, :]
    first_half = tensor[..., :half_rot]
    second_half = tensor[..., half_rot:ROT]
    return jnp.concatenate([first_half * cosine - second_half * sine_val, second_half * cosine + first_half * sine_val, tensor[..., ROT:]], axis=-1)

def page_partials(items):
    query_rows, key_pages, value_pages, valid = items
    scores = jnp.einsum('shd,sphd->shp', query_rows.astype(jnp.float32), key_pages.astype(jnp.float32)) * HD ** (-0.5)
    scores = jnp.where(valid[:, None, :], scores, LOWEST)
    highest = lax.optimization_barrier(jnp.max(scores, axis=-1))
    weights = jnp.where(valid[:, None, :], jnp.exp(scores - highest[..., None]), 0.0)
    totals = lax.optimization_barrier(jnp.sum(weights, axis=-1))
    rounded = weights.astype(jnp.bfloat16)
    outputs = jnp.einsum('shp,sphd->shd', rounded.astype(jnp.float32), value_pages.astype(jnp.float32))
    return (highest, totals, outputs)

def reference(hidden, ln_gain, w_qkv, w_fc1, w_out, w_fc2, caches, page_owner, page_used, page_fill, page_tail, positions):
    width = H * HD
    offsets = jnp.arange(PAGE, dtype=jnp.int32)
    is_tail = page_tail == 1
    is_used = page_used == 1
    write_at = (offsets[None, :] == page_fill[:, None]) & is_tail[:, None]
    valid = is_used[:, None] & (offsets[None, :] < (page_fill + page_tail)[:, None])
    state = hidden
    cache_list = []
    for layer in range(LAYERS):
        resid = state.astype(jnp.float32)
        average = lax.optimization_barrier(jnp.mean(resid, axis=-1, keepdims=True))
        centered = resid - average
        variance = lax.optimization_barrier(jnp.mean(centered * centered, axis=-1, keepdims=True))
        normed = (centered * lax.rsqrt(variance + EPSILON) * ln_gain[layer][None, :]).astype(jnp.bfloat16)
        qkv = jnp.dot(normed, w_qkv[layer].reshape(D, 3 * width), preferred_element_type=jnp.float32).reshape(REQS, 3, H, HD)
        inner = jnp.dot(normed, w_fc1[layer], preferred_element_type=jnp.float32)
        mlp_act = jax.nn.gelu(inner, approximate=True).astype(jnp.bfloat16)
        queries = rotate_heads(qkv[:, 0], positions).astype(jnp.bfloat16).reshape(REQS, width)
        new_keys = rotate_heads(qkv[:, 1], positions).astype(jnp.bfloat16).reshape(REQS, width)
        new_values = qkv[:, 2].astype(jnp.bfloat16).reshape(REQS, width)
        key_pages = jnp.where(write_at[:, :, None], new_keys[page_owner][:, None, :], caches[layer, 0])
        value_pages = jnp.where(write_at[:, :, None], new_values[page_owner][:, None, :], caches[layer, 1])
        cache_list.append(jnp.stack([key_pages, value_pages]))
        query_rows = queries[page_owner]
        highest, totals, outputs = lax.map(page_partials, (query_rows.reshape(-1, SLOTS, H, HD), key_pages.reshape(-1, SLOTS, PAGE, H, HD), value_pages.reshape(-1, SLOTS, PAGE, H, HD), valid.reshape(-1, SLOTS, PAGE)))
        highest = highest.reshape(SLOTS_ALL, H)
        totals = totals.reshape(SLOTS_ALL, H)
        outputs = outputs.reshape(SLOTS_ALL, H, HD)
        masked_high = jnp.where(is_used[:, None], highest, LOWEST)
        request_high = jax.ops.segment_max(masked_high, page_owner, num_segments=REQS)
        scale_w = jnp.where(is_used[:, None], jnp.exp(highest - request_high[page_owner]), 0.0)
        denom = jax.ops.segment_sum(totals * scale_w, page_owner, num_segments=REQS)
        numer = jax.ops.segment_sum(outputs * scale_w[..., None], page_owner, num_segments=REQS)
        attended = (numer / denom[..., None]).reshape(REQS, width).astype(jnp.bfloat16)
        attn_part = jnp.dot(attended, w_out[layer], preferred_element_type=jnp.float32)
        mlp_part = jnp.dot(mlp_act, w_fc2[layer], preferred_element_type=jnp.float32)
        state = (resid + attn_part + mlp_part).astype(jnp.bfloat16)
    return (state, jnp.stack(cache_list))
```

```python
import jax
import jax.numpy as jnp
from jax import lax
from jax.sharding import PartitionSpec as P

D = 2048
HD = 64
ROT = 32
LAYERS = 2
PAGE = 32
EPSILON = 1e-05
LOWEST = -1e30
F32 = jnp.float32
BF16 = jnp.bfloat16


def exchange(value, axis, groups=None):
    return lax.all_to_all(value, axis, 0, 0, tiled=True, axis_index_groups=groups)


def spread(value, count, axis, groups=None):
    return exchange(jnp.broadcast_to(value[None], (count,) + value.shape), axis, groups)


def rope_tables(positions):
    lane = jnp.arange(128, dtype=jnp.int32) % HD
    steps_f = (lane % (ROT // 2)).astype(F32)
    inverse = 10000.0 ** (-2.0 * steps_f / ROT)
    angles = positions[:, None] * inverse[None, :]
    cosine = jnp.where(lane[None, :] < ROT, jnp.cos(angles), 1.0)
    sine = jnp.sin(angles)
    sine_up = jnp.where(lane[None, :] < ROT // 2, -sine, 0.0)
    sine_down = jnp.where((lane[None, :] >= ROT // 2) & (lane[None, :] < ROT), sine, 0.0)
    return cosine, sine_up, sine_down


def rotate(rows, tables):
    cosine, sine_up, sine_down = tables
    half = ROT // 2
    return (
        rows * cosine
        + jnp.roll(rows, -half, axis=-1) * sine_up
        + jnp.roll(rows, half, axis=-1) * sine_down
    )


def split_in_two(value):
    head = lax.reduce_precision(value, 8, 7)
    return head.astype(BF16), (value - head).astype(BF16)


def split_in_three(value):
    head = lax.reduce_precision(value, 8, 7)
    rest = value - head
    middle = lax.reduce_precision(rest, 8, 7)
    return head.astype(BF16), middle.astype(BF16), (rest - middle).astype(BF16)


def dot32(left, right):
    return jnp.dot(left, right, preferred_element_type=F32)


def merge(parts):
    high = parts[:, :, HD + 1 : HD + 2]
    top = jnp.max(high, axis=0)
    factor = jnp.exp(high - top[None])
    return jnp.sum(parts[:, :, : HD + 1] * factor, axis=0), top


def per_device(
    hidden,
    ln_gain,
    w_qkv,
    w_fc1,
    w_out,
    w_fc2,
    caches,
    page_owner,
    page_used,
    page_fill,
    page_tail,
    positions,
):
    rep = lax.axis_index("rep")
    blk = lax.axis_index("blk")
    zs = [[2 * z + c for z in range(16)] for c in range(2)]
    pairs = [[2 * z, 2 * z + 1] for z in range(16)]
    rep_core = [[r * 32 + 2 * z + c for r in range(4) for c in range(2)] for z in range(16)]

    offsets = jnp.arange(PAGE, dtype=jnp.int32)
    is_tail = page_tail == 1
    is_used = page_used == 1
    write_at = (offsets[None, :] == page_fill[:, None]) & is_tail[:, None]
    valid = is_used[:, None] & (offsets[None, :] < (page_fill + page_tail)[:, None])
    home_rows = page_owner - rep * 4
    pick_home = (
        (home_rows[:, None] == jnp.arange(4, dtype=jnp.int32)[None, :]) & is_tail[:, None]
    ).astype(BF16)
    pair_req = jnp.arange(128, dtype=jnp.int32) // 8
    allowed = (
        (pair_req[:, None, None] == page_owner[None, :, None]) & valid[None]
    ).reshape(128, 8 * PAGE)
    head_lane = (
        jnp.arange(512, dtype=jnp.int32)[None, :] // HD == jnp.arange(8, dtype=jnp.int32)[:, None]
    )

    first = jnp.concatenate(
        [
            hidden.astype(F32),
            jnp.broadcast_to(positions.astype(F32)[:, None], (4, 64)),
        ],
        axis=1,
    )
    first = spread(first, 4, "rep").reshape(16, 128)
    state = first[:, :64]
    all_pos = first[:, 64]
    q_rows = (blk % 8) * 2
    kv_row = rep * 4 + blk % 4
    fc_rows = rep * 4 + (blk % 2) * 2
    is_key = blk // 4 < 4
    rows_pos = jnp.concatenate(
        [
            lax.dynamic_slice_in_dim(all_pos, q_rows, 2),
            jnp.where(is_key, lax.dynamic_slice_in_dim(all_pos, kv_row, 1), 0.0),
        ]
    )
    tables = rope_tables(rows_pos)

    cache_list = []
    for layer in range(LAYERS):
        gain = ln_gain[layer][None, :]
        mean = jnp.mean(state, axis=1, keepdims=True)
        centered = state - mean
        square = jnp.sum(centered * centered, axis=1, keepdims=True)
        scaled_hi, scaled_lo = split_in_two(centered * gain)
        gain_parts = split_in_three(gain)
        rows = jnp.concatenate([scaled_hi, scaled_lo, *gain_parts], axis=0)
        own_hi = lax.dynamic_slice_in_dim(scaled_hi, rep * 4, 4)
        own_lo = lax.dynamic_slice_in_dim(scaled_lo, rep * 4, 4)
        own_mean = lax.dynamic_slice_in_dim(mean, rep * 4, 4)
        own_rows = jnp.concatenate([own_hi, own_lo, *gain_parts], axis=0)
        w_all = w_qkv[layer].reshape(64, 1536)
        q_prod = dot32(rows, w_all[:, :512])
        kv_prod = dot32(own_rows, w_all[:, 512:])
        fc_prod = dot32(own_rows, w_fc1[layer])
        q_col = jnp.sum(q_prod[32:], axis=0, keepdims=True)
        kv_col = jnp.sum(kv_prod[8:], axis=0, keepdims=True)
        fc_col = jnp.sum(fc_prod[8:], axis=0, keepdims=True)
        q_sum = q_prod[:16] + q_prod[16:32] + mean * q_col
        kv_sum = kv_prod[:4] + kv_prod[4:8] + own_mean * kv_col
        fc_sum = fc_prod[:4] + fc_prod[4:8] + own_mean * fc_col
        stats = jnp.concatenate([mean.reshape(1, 16), square.reshape(1, 16)], axis=1)
        send = jnp.concatenate(
            [
                q_sum.reshape(8, 2, 4, 128).transpose(2, 0, 1, 3).reshape(32, 256),
                kv_sum.reshape(4, 8, 128).transpose(1, 0, 2).reshape(32, 128),
                fc_sum.reshape(2, 2, 16, 128).transpose(2, 0, 1, 3).reshape(32, 256),
                jnp.repeat(q_col.reshape(4, 128), 8, axis=0),
                jnp.repeat(kv_col.reshape(8, 128), 4, axis=0),
                jnp.repeat(fc_col.reshape(16, 128), 2, axis=0),
                jnp.broadcast_to(jnp.pad(stats, ((0, 0), (0, 96))), (32, 128)),
            ],
            axis=1,
        )
        got = exchange(send, "blk")
        means = got[:, 1024:1040]
        squares = got[:, 1040:1056]
        average = jnp.mean(means, axis=0)
        variance = (
            jnp.sum(squares, axis=0) + 64.0 * jnp.sum((means - average[None]) ** 2, axis=0)
        ) / D
        rstd = lax.rsqrt(variance + EPSILON)
        total = jnp.sum(got[:, :1024], axis=0).reshape(8, 128)
        row_ids = jnp.concatenate(
            [q_rows + jnp.arange(2), kv_row[None], fc_rows + jnp.arange(2)]
        )
        pick = (row_ids[:, None] == jnp.arange(16)[None, :]).astype(F32)
        row_avg = jnp.sum(pick * average[None], axis=1, keepdims=True)
        row_rstd = jnp.sum(pick * rstd[None], axis=1, keepdims=True)
        columns = jnp.concatenate(
            [total[5:6], total[5:6], total[6:7], total[7:8], total[7:8]], axis=0
        )
        values = row_rstd * (total[:5] - row_avg * columns)
        turned = rotate(values[:3], tables)
        act = jax.nn.gelu(values[3:], approximate=True)
        packed = jnp.concatenate([turned, act], axis=0).astype(BF16).reshape(640)
        spread_out = spread(packed, 32, "blk")
        queries = (
            spread_out[:, :256].reshape(4, 8, 2, 128).transpose(1, 2, 0, 3).reshape(16, 512)
        )
        new_kv = spread_out[:, 256:384].reshape(8, 4, 128).transpose(1, 0, 2).reshape(4, 1024)
        mlp_act = (
            spread_out[:, 384:].reshape(16, 2, 2, 128).transpose(1, 2, 0, 3).reshape(4, 2048)
        )
        fresh = dot32(pick_home, new_kv).astype(BF16)
        key_pages = jnp.where(write_at[:, :, None], fresh[:, None, :512], caches[layer, 0])
        value_pages = jnp.where(write_at[:, :, None], fresh[:, None, 512:], caches[layer, 1])
        cache_list.append(jnp.stack([key_pages, value_pages]))
        wide = jnp.where(head_lane[None], queries[:, None, :], jnp.zeros((), BF16)).reshape(128, 512)
        scores = (
            lax.dot_general(
                wide,
                key_pages.reshape(256, 512),
                (((1,), (1,)), ((), ())),
                preferred_element_type=F32,
            )
            * HD ** (-0.5)
        )
        scores = jnp.where(allowed, scores, LOWEST)
        high = jnp.max(scores, axis=1, keepdims=True)
        weights = jnp.where(allowed, jnp.exp(scores - high), 0.0)
        sums = jnp.sum(weights, axis=1, keepdims=True)
        mixed = dot32(weights.astype(BF16), value_pages.reshape(256, 512))
        picked = jnp.sum(
            jnp.where(
                jnp.eye(8, dtype=bool)[None, :, :, None], mixed.reshape(16, 8, 8, 64), 0.0
            ),
            axis=2,
        ).reshape(128, 64)
        parts = jnp.concatenate([picked, sums, high, jnp.zeros((128, 62), F32)], axis=1)
        parts = exchange(parts.reshape(8, 16, 128), ("rep", "blk"), rep_core)
        sums_in, top = merge(parts)
        parts = jnp.concatenate([sums_in, top, jnp.zeros((16, 62), F32)], axis=1)
        parts = spread(parts, 16, "blk", zs)
        sums_in, _ = merge(parts)
        attended = (sums_in[:, :HD] / sums_in[:, HD:]).astype(BF16).reshape(2, 512)
        attended = lax.all_gather(attended, "blk", axis_index_groups=pairs, tiled=True)
        out_part = dot32(attended, w_out[layer]) + dot32(mlp_act, w_fc2[layer])
        if layer + 1 < LAYERS:
            everyone = spread(out_part.reshape(256), 16, ("rep", "tp")).reshape(4, 4, 4, 64)
            branch = jnp.sum(everyone, axis=1).reshape(16, 64)
            state = lax.reduce_precision(state + branch, 8, 7)
        else:
            branch = lax.psum(out_part, "tp")
            own = lax.dynamic_slice_in_dim(state, rep * 4, 4)
            result = (own + branch).astype(BF16)
    return (result, jnp.stack(cache_list))


def solution(mesh):
    in_specs = (
        P("rep", "blk"),
        P(None, "blk"),
        P(None, "blk", None, "tp"),
        P(None, "blk", "tp"),
        P(None, "tp", "blk"),
        P(None, "tp", "blk"),
        P(None, None, ("rep", "blk"), None, "tp"),
        P(("rep", "blk")),
        P(("rep", "blk")),
        P(("rep", "blk")),
        P(("rep", "blk")),
        P("rep"),
    )
    out_specs = (P("rep", "blk"), P(None, None, ("rep", "blk"), None, "tp"))
    return jax.shard_map(
        per_device, mesh=mesh, in_specs=in_specs, out_specs=out_specs, check_vma=False
    )
```

```python
import functools
import math

import jax
import jax.numpy as jnp
from jax import lax
from jax.experimental import pallas as pl
from jax.experimental.pallas import tpu as pltpu
from jax.sharding import PartitionSpec as P

D = 2048
HD = 64
ROT = 32
LAYERS = 2
PAGE = 32
EPSILON = 1e-05
LOWEST = -1e30
F32 = jnp.float32
BF16 = jnp.bfloat16
INTERPRET = False
WIRE = 10
BACK = 6


def exchange(value, axis, groups=None):
    return lax.all_to_all(value, axis, 0, 0, tiled=True, axis_index_groups=groups)


def spread(value, count, axis, groups=None):
    return exchange(jnp.broadcast_to(value[None], (count,) + value.shape), axis, groups)


def rope_tables(positions):
    lane = jnp.arange(128, dtype=jnp.int32) % HD
    steps_f = (lane % (ROT // 2)).astype(F32)
    inverse = 10000.0 ** (-2.0 * steps_f / ROT)
    angles = positions[:, None] * inverse[None, :]
    cosine = jnp.where(lane[None, :] < ROT, jnp.cos(angles), 1.0)
    sine = jnp.sin(angles)
    sine_up = jnp.where(lane[None, :] < ROT // 2, -sine, 0.0)
    sine_down = jnp.where((lane[None, :] >= ROT // 2) & (lane[None, :] < ROT), sine, 0.0)
    return jnp.concatenate([cosine, sine_up, sine_down], axis=0)


def iota(shape, axis):
    return lax.broadcasted_iota(jnp.int32, shape, axis)


def dot32(left, right):
    return jnp.dot(left, right, preferred_element_type=F32)


def parts_of(value, count):
    found = []
    for _ in range(count):
        part = value.astype(BF16).astype(F32)
        found.append(part)
        value = value - part
    return found


def project_kernel(with_branch, rep_ref, *refs):
    if with_branch:
        x_ref, gain_ref, wq_ref, wf_ref, branch_ref, send_ref, state_ref, wire = refs
        sums = []
        for rep in range(4):
            total = branch_ref[rep * 16 : rep * 16 + 4, :HD]
            for tp in range(1, 4):
                start = rep * 16 + tp * 4
                total = total + branch_ref[start : start + 4, :HD]
            sums.append(total)
        x = (x_ref[:, :HD] + jnp.concatenate(sums, axis=0)).astype(BF16).astype(F32)
    else:
        x_ref, gain_ref, wq_ref, wf_ref, send_ref, state_ref, wire = refs
        x = x_ref[:, :HD]
    state_ref[...] = jnp.concatenate([x, jnp.zeros_like(x)], axis=1)
    gain = gain_ref[...]
    mean = jnp.sum(x, axis=1, keepdims=True) * (1.0 / HD)
    centered = x - mean
    square = jnp.sum(centered * centered, axis=1, keepdims=True)
    scaled = centered * gain
    row = iota((48, 24), 0)
    col = iota((48, 24), 1)
    own = rep_ref[0] * 4
    within = row % 8
    want = jnp.where(
        row < 8,
        2 * within,
        jnp.where(
            row < 16,
            2 * within + 1,
            jnp.where(
                row < 24,
                own + within % 4,
                jnp.where(
                    row < 32,
                    own + 2 * (within % 2),
                    jnp.where(row < 40, own + 2 * (within % 2) + 1, 16),
                ),
            ),
        ),
    )
    choose = (col == want).astype(BF16)
    rows = jnp.concatenate([scaled, jnp.broadcast_to(gain, (8, HD))], axis=0)
    high, low = parts_of(rows, 2)
    left_high = dot32(choose, high.astype(BF16)).astype(BF16)
    left_low = dot32(choose, low.astype(BF16)).astype(BF16)

    def product(first, last, weights):
        return dot32(left_high[first:last], weights) + dot32(left_low[first:last], weights)

    wq = wq_ref[...]
    wf = wf_ref[0]
    every_q = product(0, 48, wq[:, :512])
    every_kv = product(16, 48, wq[:, 512:])
    every_fc = product(24, 48, wf)
    sub = iota((8, 128), 0)

    def stack_q(block):
        return jnp.concatenate([block[:, 128 * j : 128 * j + 128] for j in range(4)], axis=0)

    def stack_kv(block):
        return jnp.concatenate(
            [
                jnp.where(
                    sub < 4,
                    block[:, 256 * j : 256 * j + 128],
                    block[:, 256 * j + 128 : 256 * j + 256],
                )
                for j in range(4)
            ],
            axis=0,
        )

    def stack_fc(block):
        tiles = []
        for j in range(4):
            tile = block[:, 512 * j : 512 * j + 128]
            for k in range(1, 4):
                start = 512 * j + 128 * k
                tile = jnp.where(sub // 2 == k, block[:, start : start + 128], tile)
            tiles.append(tile)
        return jnp.concatenate(tiles, axis=0)

    lane = iota((16, 128), 1)
    request = iota((16, 128), 0)
    stats = jnp.zeros((16, 128), F32)
    for k, part in enumerate(parts_of(mean, 3) + parts_of(square, 3)):
        stats = jnp.where(lane == request + 16 * k, part, stats)
    stats = jnp.sum(stats, axis=0, keepdims=True)
    pieces = [
        stack_q(every_q[0:8]),
        stack_q(every_q[8:16]),
        stack_kv(every_kv[0:8]),
        stack_fc(every_fc[0:8]),
        stack_fc(every_fc[8:16]),
        stack_q(every_q[40:48]),
        stack_kv(every_kv[24:32]),
        stack_fc(every_fc[16:24]),
        jnp.broadcast_to(stats, (32, 128)),
        jnp.zeros((32, 128), F32),
    ]
    for k, piece in enumerate(pieces):
        wire[pl.ds(k, 32, stride=WIRE), :] = piece
    send_ref[...] = wire[...].astype(BF16)


def project(layer, rep, x, gain, wq, wf, branch=None):
    args = [rep, x, gain, wq, wf] + ([] if branch is None else [branch])
    full = lambda shape: pl.BlockSpec(shape, lambda i: (0,) * len(shape))
    specs = [
        pl.BlockSpec(memory_space=pltpu.SMEM),
        full((16, 128)),
        full((1, HD)),
        full((HD, 1536)),
        pl.BlockSpec((1, HD, D), lambda i: (layer, 0, 0)),
    ] + ([] if branch is None else [full((64, 128))])
    return pl.pallas_call(
        functools.partial(project_kernel, branch is not None),
        grid=(1,),
        in_specs=specs,
        out_specs=(full((32 * WIRE, 128)), full((16, 128))),
        out_shape=(
            jax.ShapeDtypeStruct((32 * WIRE, 128), BF16),
            jax.ShapeDtypeStruct((16, 128), F32),
        ),
        scratch_shapes=[pltpu.VMEM((32 * WIRE, 128), F32)],
        name="project",
        interpret=INTERPRET,
    )(*args)


def finish_kernel(rows_ref, got_ref, table_ref, out_ref, wire, back):
    wire[...] = got_ref[...].astype(F32)
    take = lambda k: wire[pl.ds(k, 32, stride=WIRE), :]
    stats = take(8)
    stats = stats + pltpu.roll(stats, 112, 1) + pltpu.roll(stats, 96, 1)
    average = jnp.sum(stats, axis=0, keepdims=True) * (1.0 / 32)
    offset = stats - average
    spread_sum = 64.0 * jnp.sum(offset * offset, axis=0, keepdims=True)
    square_sum = pltpu.roll(jnp.sum(stats, axis=0, keepdims=True), 80, 1)
    rstd = lax.rsqrt((square_sum + spread_sum) * (1.0 / D) + EPSILON)
    lane = iota((32, 128), 1)
    lane_one = iota((1, 128), 1)
    columns = [take(5), take(6), take(7)]
    half = ROT // 2
    for k, column in enumerate((0, 0, 1, 2, 2)):
        request = rows_ref[k]
        row_offset = jnp.sum(jnp.where(lane == request, offset, 0.0), axis=1, keepdims=True)
        row_rstd = jnp.sum(jnp.where(lane_one == request, rstd, 0.0), axis=1, keepdims=True)
        value = row_rstd * jnp.sum(take(k) + row_offset * columns[column], axis=0, keepdims=True)
        if k < 3:
            value = (
                value * table_ref[k : k + 1]
                + pltpu.roll(value, 128 - half, 1) * table_ref[3 + k : 4 + k]
                + pltpu.roll(value, half, 1) * table_ref[6 + k : 7 + k]
            )
        else:
            cubed = value * value * value
            value = (
                0.5 * value * (1.0 + jnp.tanh(math.sqrt(2.0 / math.pi) * (value + 0.044715 * cubed)))
            )
        back[pl.ds(k, 32, stride=BACK), :] = jnp.broadcast_to(value, (32, 128))
    back[pl.ds(5, 32, stride=BACK), :] = jnp.zeros((32, 128), F32)
    out_ref[...] = back[...].astype(BF16)


def finish(rows, got, table):
    return pl.pallas_call(
        finish_kernel,
        in_specs=[
            pl.BlockSpec(memory_space=pltpu.SMEM),
            pl.BlockSpec(memory_space=pltpu.VMEM),
            pl.BlockSpec(memory_space=pltpu.VMEM),
        ],
        out_specs=pl.BlockSpec(memory_space=pltpu.VMEM),
        out_shape=jax.ShapeDtypeStruct((32 * BACK, 128), BF16),
        scratch_shapes=[
            pltpu.VMEM((32 * WIRE, 128), F32),
            pltpu.VMEM((32 * BACK, 128), F32),
        ],
        name="finish",
        interpret=INTERPRET,
    )(rows, got, table)


def attend_kernel(aliased, meta_ref, got_ref, cache_ref, *refs):
    if aliased:
        _, pages_ref, out_ref, back, kv = refs
    else:
        pages_ref, out_ref, back, kv = refs
    back[...] = got_ref[...].astype(F32)
    take = lambda k: back[pl.ds(k, 32, stride=BACK), :]
    new = take(2)
    for j in range(4):
        for part in range(2):
            chunk = 2 * j + part
            kv[chunk // 4, :, 128 * (chunk % 4) : 128 * (chunk % 4) + 128] = new[
                8 * j + 4 * part : 8 * j + 4 * part + 4
            ]
    spot = iota((PAGE, 512), 0)
    for side in range(2):
        for page in range(8):
            home = jnp.clip(meta_ref[0, page] - meta_ref[4, 0], 0, 3)
            place = jnp.where(meta_ref[3, page] == 1, meta_ref[2, page], -1)
            fresh = kv[side, pl.ds(home, 1), :]
            old = cache_ref[0, side, page].astype(F32)
            pages_ref[0, side, page] = jnp.where(spot == place, fresh, old).astype(BF16)
    head_of = iota((8, 512), 1) // HD == iota((8, 512), 0)
    sides = []
    for k in range(2):
        tall = take(k)
        sides.append(jnp.concatenate([tall[8 * j : 8 * j + 8] for j in range(4)], axis=1))
    wide = jnp.concatenate(
        [
            jnp.where(head_of, jnp.broadcast_to(sides[k][p : p + 1], (8, 512)), 0.0)
            for p in range(8)
            for k in range(2)
        ],
        axis=0,
    ).astype(BF16)
    keys = pages_ref[0, 0].reshape(8 * PAGE, 512)
    values = pages_ref[0, 1].reshape(8 * PAGE, 512)
    scores = (
        lax.dot_general(wide, keys, (((1,), (1,)), ((), ())), preferred_element_type=F32)
        * HD ** (-0.5)
    )
    page_of = iota((1, 256), 1) // PAGE
    owner = jnp.zeros((1, 256), jnp.int32)
    limit = jnp.zeros((1, 256), jnp.int32)
    for page in range(8):
        length = jnp.where(meta_ref[1, page] == 1, meta_ref[2, page] + meta_ref[3, page], 0)
        owner = jnp.where(page_of == page, meta_ref[0, page], owner)
        limit = jnp.where(page_of == page, length, limit)
    owner = jnp.where(iota((1, 256), 1) % PAGE < limit, owner, -1)
    allowed = iota((128, 256), 0) // 8 == owner
    scores = jnp.where(allowed, scores, LOWEST)
    high = jnp.max(scores, axis=1, keepdims=True)
    weights = jnp.where(allowed, jnp.exp(scores - high), 0.0)
    total = jnp.sum(weights, axis=1, keepdims=True)
    mixed = dot32(weights.astype(BF16), values)
    head = iota((128, 128), 0) % 8
    lane = iota((128, 128), 1)
    picked = mixed[:, :128]
    for k in range(1, 4):
        picked = jnp.where(head // 2 == k, mixed[:, 128 * k : 128 * k + 128], picked)
    picked = jnp.where(head % 2 == 1, pltpu.roll(picked, HD, 1), picked)
    out_ref[...] = jnp.where(
        lane < HD, picked, jnp.where(lane == HD, total, jnp.where(lane == HD + 1, high, 0.0))
    )


def attend(layer, meta, got, caches, pages=None):
    block = pl.BlockSpec((1, 2, 8, PAGE, 512), lambda i: (layer, 0, 0, 0, 0))
    whole = lambda shape: pl.BlockSpec(shape, lambda i: (0,) * len(shape))
    specs = [pl.BlockSpec(memory_space=pltpu.SMEM), whole((32 * BACK, 128)), block]
    args = [meta, got, caches]
    aliases = {}
    if pages is not None:
        specs.append(pl.BlockSpec(memory_space=pl.ANY))
        args.append(pages)
        aliases = {3: 0}
    return pl.pallas_call(
        functools.partial(attend_kernel, pages is not None),
        grid=(1,),
        in_specs=specs,
        out_specs=(block, whole((128, 128))),
        out_shape=(
            jax.ShapeDtypeStruct(caches.shape, BF16),
            jax.ShapeDtypeStruct((128, 128), F32),
        ),
        scratch_shapes=[pltpu.VMEM((32 * BACK, 128), F32), pltpu.VMEM((2, 4, 512), F32)],
        input_output_aliases=aliases,
        name="attend",
        interpret=INTERPRET,
    )(*args)


def join_kernel(got_ref, out_ref):
    got = got_ref[...]
    high = got[:, :, HD + 1 : HD + 2]
    top = jnp.max(high, axis=0)
    total = jnp.sum(got * jnp.exp(high - top[None]), axis=0)
    lane = iota((16, 128), 1)
    out = jnp.where(lane < HD, total, 0.0)
    extra = parts_of(total[:, HD : HD + 1], 3) + parts_of(top, 3)
    for k, part in enumerate(extra):
        out = jnp.where(lane == HD + k, part, out)
    out_ref[...] = jnp.broadcast_to(out.astype(BF16)[None], (16, 16, 128))


def join(got):
    return pl.pallas_call(
        join_kernel,
        out_shape=jax.ShapeDtypeStruct((16, 16, 128), BF16),
        name="join",
        interpret=INTERPRET,
    )(got)


def settle_kernel(got_ref, out_ref):
    got = got_ref[...].astype(F32)
    sums = got[:, :, HD : HD + 1] + got[:, :, HD + 1 : HD + 2] + got[:, :, HD + 2 : HD + 3]
    high = got[:, :, HD + 3 : HD + 4] + got[:, :, HD + 4 : HD + 5] + got[:, :, HD + 5 : HD + 6]
    factor = jnp.exp(high - jnp.max(high, axis=0)[None])
    total = jnp.sum(sums * factor, axis=0)
    mixed = jnp.sum(got * factor, axis=0)
    out_ref[...] = jnp.where(iota((16, 128), 1) < HD, mixed / total, 0.0).astype(BF16)


def settle(got):
    return pl.pallas_call(
        settle_kernel,
        out_shape=jax.ShapeDtypeStruct((16, 128), BF16),
        name="settle",
        interpret=INTERPRET,
    )(got)


def output_kernel(copies, att_ref, got_ref, wo_ref, wf_ref, out_ref, back):
    back[...] = got_ref[...].astype(F32)
    att = att_ref[...].astype(F32)
    att = att + pltpu.roll(att, HD, 1)
    att = jnp.concatenate([att] * 4, axis=1)
    own = iota((32, 512), 1) // HD == iota((32, 512), 0) % 8
    by_head = dot32(jnp.where(own, att, 0.0).astype(BF16), wo_ref[0])
    chunk = iota((32, D), 1) // 128 == iota((32, D), 0) // 2
    mlp = []
    for k in range(2):
        act = back[pl.ds(3 + k, 32, stride=BACK), :]
        act = jnp.concatenate([act] * 16, axis=1)
        mlp.append(dot32(jnp.where(chunk, act, 0.0).astype(BF16), wf_ref[0]))
    odd = iota((32, HD), 0) % 2
    rows = []
    for i in range(4):
        from_mlp = jnp.sum(jnp.where(odd == i // 2, mlp[i % 2], 0.0), axis=0, keepdims=True)
        from_att = jnp.sum(by_head[8 * i : 8 * i + 8], axis=0, keepdims=True)
        rows.append(from_att + from_mlp)
    tile = jnp.concatenate(rows, axis=0)
    tile = jnp.concatenate([tile, jnp.zeros_like(tile)], axis=1)
    for k in range(copies):
        out_ref[4 * k : 4 * k + 4] = tile


def output(layer, copies, att, got, w_out, w_fc2):
    whole = lambda shape: pl.BlockSpec(shape, lambda i: (0,) * len(shape))
    return pl.pallas_call(
        functools.partial(output_kernel, copies),
        grid=(1,),
        in_specs=[
            whole((32, 128)),
            whole((32 * BACK, 128)),
            pl.BlockSpec((1, 512, HD), lambda i: (layer, 0, 0)),
            pl.BlockSpec((1, D, HD), lambda i: (layer, 0, 0)),
        ],
        out_specs=whole((4 * copies, 128)),
        out_shape=jax.ShapeDtypeStruct((4 * copies, 128), F32),
        scratch_shapes=[pltpu.VMEM((32 * BACK, 128), F32)],
        name="output",
        interpret=INTERPRET,
    )(att, got, w_out, w_fc2)


def per_device(
    hidden,
    ln_gain,
    w_qkv,
    w_fc1,
    w_out,
    w_fc2,
    caches,
    page_owner,
    page_used,
    page_fill,
    page_tail,
    positions,
):
    rep = lax.axis_index("rep")
    blk = lax.axis_index("blk")
    zs = [[2 * z + c for z in range(16)] for c in range(2)]
    pairs = [[2 * z, 2 * z + 1] for z in range(16)]
    rep_core = [[r * 32 + 2 * z + c for r in range(4) for c in range(2)] for z in range(16)]

    first = jnp.concatenate(
        [hidden.astype(F32), jnp.broadcast_to(positions.astype(F32)[:, None], (4, 64))], axis=1
    )
    first = spread(first, 4, "rep").reshape(16, 128)
    q_row = (blk % 8) * 2
    kv_row = rep * 4 + blk % 4
    fc_row = rep * 4 + (blk % 2) * 2
    rows = jnp.stack([q_row, q_row + 1, kv_row, fc_row, fc_row + 1])
    pick = rows[:3, None] == jnp.arange(16)[None, :]
    pick = pick & ((jnp.arange(3) < 2) | (blk // 4 < 4))[:, None]
    table = rope_tables(jnp.sum(jnp.where(pick, first[:, 64][None], 0.0), axis=1))
    meta = jnp.stack(
        [page_owner, page_used, page_fill, page_tail, jnp.full((8,), rep * 4, jnp.int32)]
    )
    rep_one = rep.reshape(1)
    weights = [w_qkv[layer].reshape(HD, 1536) for layer in range(LAYERS)]
    gains = [ln_gain[layer : layer + 1] for layer in range(LAYERS)]

    state, branch, pages = first, None, None
    for layer in range(LAYERS):
        send, state = project(layer, rep_one, state, gains[layer], weights[layer], w_fc1, branch)
        got = exchange(send.reshape(32, WIRE // 2, 2, 128), "blk").reshape(32 * WIRE, 128)
        back = finish(rows, got, table)
        got = exchange(back.reshape(32, BACK // 2, 2, 128), "blk").reshape(32 * BACK, 128)
        pages, parts = attend(layer, meta, got, caches, pages)
        parts = exchange(parts.reshape(8, 16, 128), ("rep", "blk"), rep_core)
        parts = exchange(join(parts), "blk", zs)
        att = lax.all_gather(settle(parts), "blk", axis_index_groups=pairs, tiled=True)
        if layer + 1 < LAYERS:
            out = output(layer, 16, att, got, w_out, w_fc2).reshape(16, 4, 128)
            branch = exchange(out, ("rep", "tp")).reshape(64, 128)
        else:
            out = output(layer, 4, att, got, w_out, w_fc2).reshape(4, 4, 128)
            branch = jnp.sum(exchange(out, "tp"), axis=0)[:, :HD]
            own = lax.dynamic_slice(state, (rep * 4, 0), (4, HD))
            result = (own + branch).astype(BF16)
    return (result, pages)


def solution(mesh):
    in_specs = (
        P("rep", "blk"),
        P(None, "blk"),
        P(None, "blk", None, "tp"),
        P(None, "blk", "tp"),
        P(None, "tp", "blk"),
        P(None, "tp", "blk"),
        P(None, None, ("rep", "blk"), None, "tp"),
        P(("rep", "blk")),
        P(("rep", "blk")),
        P(("rep", "blk")),
        P(("rep", "blk")),
        P("rep"),
    )
    out_specs = (P("rep", "blk"), P(None, None, ("rep", "blk"), None, "tp"))
    return jax.shard_map(
        per_device, mesh=mesh, in_specs=in_specs, out_specs=out_specs, check_vma=False
    )
```

```python
import functools
import math

import jax
import jax.numpy as jnp
from jax import lax
from jax.experimental import pallas as pl
from jax.experimental.pallas import tpu as pltpu
from jax.sharding import PartitionSpec as P

D = 2048
HD = 64
ROT = 32
LAYERS = 2
PAGE = 32
EPSILON = 1e-05
LOWEST = -1e30
F32 = jnp.float32
BF16 = jnp.bfloat16
INTERPRET = False
WIRE = 10
BACK = 6


def exchange(value, axis, groups=None):
    return lax.all_to_all(value, axis, 0, 0, tiled=True, axis_index_groups=groups)


def spread(value, count, axis, groups=None):
    return exchange(jnp.broadcast_to(value[None], (count,) + value.shape), axis, groups)


def rope_tables(positions):
    lane = jnp.arange(128, dtype=jnp.int32) % HD
    steps_f = (lane % (ROT // 2)).astype(F32)
    inverse = 10000.0 ** (-2.0 * steps_f / ROT)
    angles = positions[:, None] * inverse[None, :]
    cosine = jnp.where(lane[None, :] < ROT, jnp.cos(angles), 1.0)
    sine = jnp.sin(angles)
    sine_up = jnp.where(lane[None, :] < ROT // 2, -sine, 0.0)
    sine_down = jnp.where((lane[None, :] >= ROT // 2) & (lane[None, :] < ROT), sine, 0.0)
    return jnp.concatenate([cosine, sine_up, sine_down], axis=0)


def near(value):
    return value if INTERPRET else pltpu.with_memory_space_constraint(value, pltpu.VMEM)


def near_out(shape, dtype):
    return jax.ShapeDtypeStruct(shape, dtype) if INTERPRET else pltpu.VMEM(shape, dtype)


def iota(shape, axis):
    return lax.broadcasted_iota(jnp.int32, shape, axis)


def dot32(left, right):
    return jnp.dot(left, right, preferred_element_type=F32)


def dot_t(left, right):
    return lax.dot_general(left, right, (((1,), (1,)), ((), ())), preferred_element_type=F32)


def parts_of(value, count):
    found = []
    for _ in range(count):
        part = value.astype(BF16).astype(F32)
        found.append(part)
        value = value - part
    return found


def project_kernel(with_branch, rep_ref, *refs):
    if with_branch:
        x_ref, gain_ref, wq_ref, wf_ref, branch_ref, send_ref, state_ref, wire = refs
        sums = []
        for rep in range(4):
            total = branch_ref[rep * 16 : rep * 16 + 4, :HD]
            for tp in range(1, 4):
                start = rep * 16 + tp * 4
                total = total + branch_ref[start : start + 4, :HD]
            sums.append(total)
        x = (x_ref[:, :HD] + jnp.concatenate(sums, axis=0)).astype(BF16).astype(F32)
    else:
        x_ref, gain_ref, wq_ref, wf_ref, send_ref, state_ref, wire = refs
        x = x_ref[:, :HD]
    state_ref[...] = jnp.concatenate([x, jnp.zeros_like(x)], axis=1)
    gain = gain_ref[...]
    mean = jnp.sum(x, axis=1, keepdims=True) * (1.0 / HD)
    centered = x - mean
    square = jnp.sum(centered * centered, axis=1, keepdims=True)
    scaled = centered * gain
    row = iota((48, 24), 0)
    col = iota((48, 24), 1)
    own = rep_ref[0] * 4
    within = row % 8
    want = jnp.where(
        row < 8,
        2 * within,
        jnp.where(
            row < 16,
            2 * within + 1,
            jnp.where(
                row < 24,
                own + within % 4,
                jnp.where(
                    row < 32,
                    own + 2 * (within % 2),
                    jnp.where(row < 40, own + 2 * (within % 2) + 1, 16),
                ),
            ),
        ),
    )
    choose = (col == want).astype(BF16)
    rows = jnp.concatenate([scaled, jnp.broadcast_to(gain, (8, HD))], axis=0)
    high, low = parts_of(rows, 2)
    left_high = dot32(choose, high.astype(BF16)).astype(BF16)
    left_low = dot32(choose, low.astype(BF16)).astype(BF16)

    def product(first, last, weights):
        return dot32(left_high[first:last], weights) + dot32(left_low[first:last], weights)

    wf = wf_ref[0]
    every_q = product(0, 48, wq_ref[0, 0])
    every_kv = jnp.concatenate([product(16, 48, wq_ref[0, k]) for k in (1, 2)], axis=1)
    every_fc = product(24, 48, wf)
    sub = iota((8, 128), 0)

    def stack_q(block):
        return jnp.concatenate([block[:, 128 * j : 128 * j + 128] for j in range(4)], axis=0)

    def stack_kv(block):
        return jnp.concatenate(
            [
                jnp.where(
                    sub < 4,
                    block[:, 256 * j : 256 * j + 128],
                    block[:, 256 * j + 128 : 256 * j + 256],
                )
                for j in range(4)
            ],
            axis=0,
        )

    def stack_fc(block):
        tiles = []
        for j in range(4):
            tile = block[:, 512 * j : 512 * j + 128]
            for k in range(1, 4):
                start = 512 * j + 128 * k
                tile = jnp.where(sub // 2 == k, block[:, start : start + 128], tile)
            tiles.append(tile)
        return jnp.concatenate(tiles, axis=0)

    lane = iota((16, 128), 1)
    request = iota((16, 128), 0)
    stats = jnp.zeros((16, 128), F32)
    for k, part in enumerate(parts_of(mean, 3) + parts_of(square, 3)):
        stats = jnp.where(lane == request + 16 * k, part, stats)
    stats = jnp.sum(stats, axis=0, keepdims=True)
    pieces = [
        stack_q(every_q[0:8]),
        stack_q(every_q[8:16]),
        stack_kv(every_kv[0:8]),
        stack_fc(every_fc[0:8]),
        stack_fc(every_fc[8:16]),
        stack_q(every_q[40:48]),
        stack_kv(every_kv[24:32]),
        stack_fc(every_fc[16:24]),
        jnp.broadcast_to(stats, (32, 128)),
        jnp.zeros((32, 128), F32),
    ]
    for k, piece in enumerate(pieces):
        wire[pl.ds(k, 32, stride=WIRE), :] = piece
    send_ref[...] = wire[...].astype(BF16)


def project(layer, rep, x, gain, wq, wf, branch=None):
    args = [rep, near(x), near(gain), wq, wf] + ([] if branch is None else [near(branch)])
    full = lambda shape: pl.BlockSpec(shape, lambda i: (0,) * len(shape))
    specs = [
        pl.BlockSpec(memory_space=pltpu.SMEM),
        full((16, 128)),
        full((1, HD)),
        pl.BlockSpec((1, 3, HD, 512), lambda i: (layer, 0, 0, 0)),
        pl.BlockSpec((1, HD, D), lambda i: (layer, 0, 0)),
    ] + ([] if branch is None else [full((64, 128))])
    return pl.pallas_call(
        functools.partial(project_kernel, branch is not None),
        grid=(1,),
        in_specs=specs,
        out_specs=(full((32 * WIRE, 128)), full((16, 128))),
        out_shape=(
            near_out((32 * WIRE, 128), BF16),
            near_out((16, 128), F32),
        ),
        scratch_shapes=[pltpu.VMEM((32 * WIRE, 128), F32)],
        name="project",
        interpret=INTERPRET,
    )(*args)


def finish_kernel(rows_ref, got_ref, table_ref, out_ref, wire, back):
    wire[...] = got_ref[...].astype(F32)
    take = lambda k: wire[pl.ds(k, 32, stride=WIRE), :]
    stats = take(8)
    stats = stats + pltpu.roll(stats, 112, 1) + pltpu.roll(stats, 96, 1)
    average = jnp.sum(stats, axis=0, keepdims=True) * (1.0 / 32)
    offset = stats - average
    spread_sum = 64.0 * jnp.sum(offset * offset, axis=0, keepdims=True)
    square_sum = pltpu.roll(jnp.sum(stats, axis=0, keepdims=True), 80, 1)
    rstd = lax.rsqrt((square_sum + spread_sum) * (1.0 / D) + EPSILON)
    lane = iota((32, 128), 1)
    lane_one = iota((1, 128), 1)
    columns = [take(5), take(6), take(7)]
    half = ROT // 2
    for k, column in enumerate((0, 0, 1, 2, 2)):
        request = rows_ref[k]
        row_offset = jnp.sum(jnp.where(lane == request, offset, 0.0), axis=1, keepdims=True)
        row_rstd = jnp.sum(jnp.where(lane_one == request, rstd, 0.0), axis=1, keepdims=True)
        value = row_rstd * jnp.sum(take(k) + row_offset * columns[column], axis=0, keepdims=True)
        if k < 3:
            value = (
                value * table_ref[k : k + 1]
                + pltpu.roll(value, 128 - half, 1) * table_ref[3 + k : 4 + k]
                + pltpu.roll(value, half, 1) * table_ref[6 + k : 7 + k]
            )
        else:
            cubed = value * value * value
            value = (
                0.5 * value * (1.0 + jnp.tanh(math.sqrt(2.0 / math.pi) * (value + 0.044715 * cubed)))
            )
        back[pl.ds(k, 32, stride=BACK), :] = jnp.broadcast_to(value, (32, 128))
    back[pl.ds(5, 32, stride=BACK), :] = jnp.zeros((32, 128), F32)
    out_ref[...] = back[...].astype(BF16)


def finish(rows, got, table):
    return pl.pallas_call(
        finish_kernel,
        in_specs=[
            pl.BlockSpec(memory_space=pltpu.SMEM),
            pl.BlockSpec(memory_space=pltpu.VMEM),
            pl.BlockSpec(memory_space=pltpu.VMEM),
        ],
        out_specs=pl.BlockSpec(memory_space=pltpu.VMEM),
        out_shape=near_out((32 * BACK, 128), BF16),
        scratch_shapes=[
            pltpu.VMEM((32 * WIRE, 128), F32),
            pltpu.VMEM((32 * BACK, 128), F32),
        ],
        name="finish",
        interpret=INTERPRET,
    )(rows, near(got), near(table))


def attend_kernel(aliased, meta_ref, got_ref, cache_ref, *refs):
    if aliased:
        _, pages_ref, out_ref, back, kv = refs
    else:
        pages_ref, out_ref, back, kv = refs
    back[...] = got_ref[...].astype(F32)
    take = lambda k: back[pl.ds(k, 32, stride=BACK), :]
    new = take(2)
    for j in range(4):
        for part in range(2):
            chunk = 2 * j + part
            kv[chunk // 4, :, 128 * (chunk % 4) : 128 * (chunk % 4) + 128] = new[
                8 * j + 4 * part : 8 * j + 4 * part + 4
            ]
    spot = iota((PAGE, 512), 0)
    for side in range(2):
        for page in range(8):
            home = jnp.clip(meta_ref[0, page] - meta_ref[4, 0], 0, 3)
            place = jnp.where(meta_ref[3, page] == 1, meta_ref[2, page], -1)
            fresh = kv[side, pl.ds(home, 1), :]
            old = cache_ref[0, side, page].astype(F32)
            pages_ref[0, side, page] = jnp.where(spot == place, fresh, old).astype(BF16)
    head_of = iota((8, 512), 1) // HD == iota((8, 512), 0)
    sides = []
    for k in range(2):
        tall = take(k)
        sides.append(jnp.concatenate([tall[8 * j : 8 * j + 8] for j in range(4)], axis=1))
    wide = jnp.concatenate(
        [
            jnp.where(head_of, jnp.broadcast_to(sides[k][p : p + 1], (8, 512)), 0.0)
            for p in range(8)
            for k in range(2)
        ],
        axis=0,
    ).astype(BF16)
    keys = pages_ref[0, 0].reshape(8 * PAGE, 512)
    values = pages_ref[0, 1].reshape(8 * PAGE, 512)
    scores = dot_t(wide, keys) * HD ** (-0.5)
    page_of = iota((1, 256), 1) // PAGE
    owner = jnp.zeros((1, 256), jnp.int32)
    limit = jnp.zeros((1, 256), jnp.int32)
    for page in range(8):
        length = jnp.where(meta_ref[1, page] == 1, meta_ref[2, page] + meta_ref[3, page], 0)
        owner = jnp.where(page_of == page, meta_ref[0, page], owner)
        limit = jnp.where(page_of == page, length, limit)
    owner = jnp.where(iota((1, 256), 1) % PAGE < limit, owner, -1)
    allowed = iota((128, 256), 0) // 8 == owner
    scores = jnp.where(allowed, scores, LOWEST)
    high = jnp.max(scores, axis=1, keepdims=True)
    weights = jnp.where(allowed, jnp.exp(scores - high), 0.0)
    total = jnp.sum(weights, axis=1, keepdims=True)
    mixed = dot32(weights.astype(BF16), values)
    head = iota((128, 128), 0) % 8
    lane = iota((128, 128), 1)
    picked = mixed[:, :128]
    for k in range(1, 4):
        picked = jnp.where(head // 2 == k, mixed[:, 128 * k : 128 * k + 128], picked)
    picked = jnp.where(head % 2 == 1, pltpu.roll(picked, HD, 1), picked)
    out_ref[...] = jnp.where(
        lane < HD, picked, jnp.where(lane == HD, total, jnp.where(lane == HD + 1, high, 0.0))
    )


def attend(layer, meta, got, caches, pages=None):
    block = pl.BlockSpec((1, 2, 8, PAGE, 512), lambda i: (layer, 0, 0, 0, 0))
    whole = lambda shape: pl.BlockSpec(shape, lambda i: (0,) * len(shape))
    specs = [pl.BlockSpec(memory_space=pltpu.SMEM), whole((32 * BACK, 128)), block]
    args = [meta, near(got), caches]
    aliases = {}
    if pages is not None:
        specs.append(pl.BlockSpec(memory_space=pl.ANY))
        args.append(pages)
        aliases = {3: 0}
    return pl.pallas_call(
        functools.partial(attend_kernel, pages is not None),
        grid=(1,),
        in_specs=specs,
        out_specs=(block, whole((128, 128))),
        out_shape=(
            jax.ShapeDtypeStruct(caches.shape, BF16),
            near_out((128, 128), F32),
        ),
        scratch_shapes=[pltpu.VMEM((32 * BACK, 128), F32), pltpu.VMEM((2, 4, 512), F32)],
        input_output_aliases=aliases,
        name="attend",
        interpret=INTERPRET,
    )(*args)


def join_kernel(got_ref, out_ref):
    got = got_ref[...]
    high = got[:, :, HD + 1 : HD + 2]
    top = jnp.max(high, axis=0)
    total = jnp.sum(got * jnp.exp(high - top[None]), axis=0)
    lane = iota((16, 128), 1)
    out = jnp.where(lane < HD, total, 0.0)
    extra = parts_of(total[:, HD : HD + 1], 3) + parts_of(top, 3)
    for k, part in enumerate(extra):
        out = jnp.where(lane == HD + k, part, out)
    out_ref[...] = jnp.broadcast_to(out.astype(BF16)[None], (16, 16, 128))


def join(got):
    return pl.pallas_call(
        join_kernel,
        out_shape=near_out((16, 16, 128), BF16),
        name="join",
        interpret=INTERPRET,
    )(near(got))


def settle_kernel(got_ref, out_ref):
    got = got_ref[...].astype(F32)
    sums = got[:, :, HD : HD + 1] + got[:, :, HD + 1 : HD + 2] + got[:, :, HD + 2 : HD + 3]
    high = got[:, :, HD + 3 : HD + 4] + got[:, :, HD + 4 : HD + 5] + got[:, :, HD + 5 : HD + 6]
    factor = jnp.exp(high - jnp.max(high, axis=0)[None])
    total = jnp.sum(sums * factor, axis=0)
    mixed = jnp.sum(got * factor, axis=0)
    out_ref[...] = jnp.where(iota((16, 128), 1) < HD, mixed / total, 0.0).astype(BF16)


def settle(got):
    return pl.pallas_call(
        settle_kernel,
        out_shape=near_out((16, 128), BF16),
        name="settle",
        interpret=INTERPRET,
    )(near(got))


def output_kernel(copies, att_ref, got_ref, wo_ref, wf_ref, out_ref, back):
    back[...] = got_ref[...].astype(F32)
    att = att_ref[...].astype(F32)
    att = att + pltpu.roll(att, HD, 1)
    att = jnp.concatenate([att] * 4, axis=1)
    own = iota((32, 512), 1) // HD == iota((32, 512), 0) % 8
    by_head = dot_t(jnp.where(own, att, 0.0).astype(BF16), wo_ref[0])
    chunk = iota((32, D), 1) // 128 == iota((32, D), 0) // 2
    mlp = []
    for k in range(2):
        act = back[pl.ds(3 + k, 32, stride=BACK), :]
        act = jnp.concatenate([act] * 16, axis=1)
        mlp.append(dot_t(jnp.where(chunk, act, 0.0).astype(BF16), wf_ref[0]))
    odd = iota((32, HD), 0) % 2
    rows = []
    for i in range(4):
        from_mlp = jnp.sum(jnp.where(odd == i // 2, mlp[i % 2], 0.0), axis=0, keepdims=True)
        from_att = jnp.sum(by_head[8 * i : 8 * i + 8], axis=0, keepdims=True)
        rows.append(from_att + from_mlp)
    tile = jnp.concatenate(rows, axis=0)
    tile = jnp.concatenate([tile, jnp.zeros_like(tile)], axis=1)
    for k in range(copies):
        out_ref[4 * k : 4 * k + 4] = tile


def output(layer, copies, att, got, w_out, w_fc2):
    whole = lambda shape: pl.BlockSpec(shape, lambda i: (0,) * len(shape))
    return pl.pallas_call(
        functools.partial(output_kernel, copies),
        grid=(1,),
        in_specs=[
            whole((32, 128)),
            whole((32 * BACK, 128)),
            pl.BlockSpec((1, HD, 512), lambda i: (layer, 0, 0)),
            pl.BlockSpec((1, HD, D), lambda i: (layer, 0, 0)),
        ],
        out_specs=whole((4 * copies, 128)),
        out_shape=near_out((4 * copies, 128), F32),
        scratch_shapes=[pltpu.VMEM((32 * BACK, 128), F32)],
        name="output",
        interpret=INTERPRET,
    )(near(att), near(got), w_out, w_fc2)


def per_device(
    hidden,
    ln_gain,
    w_qkv,
    w_fc1,
    w_out,
    w_fc2,
    caches,
    page_owner,
    page_used,
    page_fill,
    page_tail,
    positions,
):
    rep = lax.axis_index("rep")
    blk = lax.axis_index("blk")
    zs = [[2 * z + c for z in range(16)] for c in range(2)]
    pairs = [[2 * z, 2 * z + 1] for z in range(16)]
    rep_core = [[r * 32 + 2 * z + c for r in range(4) for c in range(2)] for z in range(16)]

    first = jnp.concatenate(
        [hidden.astype(F32), jnp.broadcast_to(positions.astype(F32)[:, None], (4, 64))], axis=1
    )
    first = spread(first, 4, "rep").reshape(16, 128)
    q_row = (blk % 8) * 2
    kv_row = rep * 4 + blk % 4
    fc_row = rep * 4 + (blk % 2) * 2
    rows = jnp.stack([q_row, q_row + 1, kv_row, fc_row, fc_row + 1])
    pick = rows[:3, None] == jnp.arange(16)[None, :]
    pick = pick & ((jnp.arange(3) < 2) | (blk // 4 < 4))[:, None]
    table = rope_tables(jnp.sum(jnp.where(pick, first[:, 64][None], 0.0), axis=1))
    meta = jnp.stack(
        [page_owner, page_used, page_fill, page_tail, jnp.full((8,), rep * 4, jnp.int32)]
    )
    rep_one = rep.reshape(1)
    w_qkv = w_qkv.transpose(0, 2, 1, 3)
    w_out = w_out.transpose(0, 2, 1)
    w_fc2 = w_fc2.transpose(0, 2, 1)
    gains = [ln_gain[layer : layer + 1] for layer in range(LAYERS)]

    state, branch, pages = first, None, None
    for layer in range(LAYERS):
        send, state = project(layer, rep_one, state, gains[layer], w_qkv, w_fc1, branch)
        got = exchange(send.reshape(32, WIRE // 2, 2, 128), "blk").reshape(32 * WIRE, 128)
        back = finish(rows, got, table)
        got = exchange(back.reshape(32, BACK // 2, 2, 128), "blk").reshape(32 * BACK, 128)
        pages, parts = attend(layer, meta, got, caches, pages)
        parts = exchange(parts.reshape(8, 16, 128), ("rep", "blk"), rep_core)
        parts = exchange(join(parts), "blk", zs)
        att = lax.all_gather(settle(parts), "blk", axis_index_groups=pairs, tiled=True)
        if layer + 1 < LAYERS:
            out = output(layer, 16, att, got, w_out, w_fc2).reshape(16, 4, 128)
            branch = exchange(out, ("rep", "tp")).reshape(64, 128)
        else:
            out = output(layer, 4, att, got, w_out, w_fc2).reshape(4, 4, 128)
            branch = jnp.sum(exchange(out, "tp"), axis=0)[:, :HD]
            own = lax.dynamic_slice(state, (rep * 4, 0), (4, HD))
            result = (own + branch).astype(BF16)
    return (result, pages)


def solution(mesh):
    in_specs = (
        P("rep", "blk"),
        P(None, "blk"),
        P(None, "blk", None, "tp"),
        P(None, "blk", "tp"),
        P(None, "tp", "blk"),
        P(None, "tp", "blk"),
        P(None, None, ("rep", "blk"), None, "tp"),
        P(("rep", "blk")),
        P(("rep", "blk")),
        P(("rep", "blk")),
        P(("rep", "blk")),
        P("rep"),
    )
    out_specs = (P("rep", "blk"), P(None, None, ("rep", "blk"), None, "tp"))
    return jax.shard_map(
        per_device, mesh=mesh, in_specs=in_specs, out_specs=out_specs, check_vma=False
    )
```

```python
import functools
import math

import jax
import jax.numpy as jnp
from jax import lax
from jax.experimental import pallas as pl
from jax.experimental.pallas import tpu as pltpu
from jax.sharding import PartitionSpec as P

D = 2048
HD = 64
ROT = 32
LAYERS = 2
PAGE = 32
EPSILON = 1e-05
LOWEST = -1e30
F32 = jnp.float32
BF16 = jnp.bfloat16
INTERPRET = False
WIRE = 10
BACK = 6


def exchange(value, axis, groups=None):
    return lax.all_to_all(value, axis, 0, 0, tiled=True, axis_index_groups=groups)


def spread(value, count, axis, groups=None):
    return exchange(jnp.broadcast_to(value[None], (count,) + value.shape), axis, groups)


def rope_factors(positions):
    lane = jnp.arange(64, dtype=jnp.int32)
    steps_f = (lane % (ROT // 2)).astype(F32)
    angles = positions.astype(F32)[:, None] * (10000.0 ** (-2.0 * steps_f / ROT))[None, :]
    sine = jnp.sin(angles)
    return jnp.where(lane < 32, jnp.cos(angles), jnp.where(lane < 48, -sine, sine))


def near(value):
    return value if INTERPRET else pltpu.with_memory_space_constraint(value, pltpu.VMEM)


def near_out(shape, dtype):
    return jax.ShapeDtypeStruct(shape, dtype) if INTERPRET else pltpu.VMEM(shape, dtype)


def iota(shape, axis):
    return lax.broadcasted_iota(jnp.int32, shape, axis)


def dot32(left, right):
    return jnp.dot(left, right, preferred_element_type=F32)


def dot_t(left, right):
    return lax.dot_general(left, right, (((1,), (1,)), ((), ())), preferred_element_type=F32)


def parts_of(value, count):
    found = []
    for _ in range(count):
        part = value.astype(BF16).astype(F32)
        found.append(part)
        value = value - part
    return found


def project_kernel(layer, with_branch, meta_ref, *refs):
    if with_branch:
        x_ref, gain_ref, wq_ref, wf_ref, branch_ref, send_ref, state_ref, wire = refs
        sums = []
        for rep in range(4):
            total = branch_ref[rep * 16 : rep * 16 + 4, :HD]
            for tp in range(1, 4):
                start = rep * 16 + tp * 4
                total = total + branch_ref[start : start + 4, :HD]
            sums.append(total)
        x = (x_ref[:, :HD] + jnp.concatenate(sums, axis=0)).astype(BF16).astype(F32)
    else:
        x_ref, gain_ref, wq_ref, wf_ref, send_ref, state_ref, wire = refs
        x = x_ref[:, :HD]
    state_ref[...] = jnp.concatenate([x, jnp.zeros_like(x)], axis=1)
    gain = gain_ref[layer : layer + 1]
    mean = jnp.sum(x, axis=1, keepdims=True) * (1.0 / HD)
    centered = x - mean
    square = jnp.sum(centered * centered, axis=1, keepdims=True)
    scaled = centered * gain
    row = iota((48, 24), 0)
    col = iota((48, 24), 1)
    own = meta_ref[4, 0] * 4
    within = row % 8
    want = jnp.where(
        row < 8,
        2 * within,
        jnp.where(
            row < 16,
            2 * within + 1,
            jnp.where(
                row < 24,
                own + within % 4,
                jnp.where(
                    row < 32,
                    own + 2 * (within % 2),
                    jnp.where(row < 40, own + 2 * (within % 2) + 1, 16),
                ),
            ),
        ),
    )
    choose = (col == want).astype(BF16)
    rows = jnp.concatenate([scaled, jnp.broadcast_to(gain, (8, HD))], axis=0)
    high, low = parts_of(rows, 2)
    left_high = dot32(choose, high.astype(BF16)).astype(BF16)
    left_low = dot32(choose, low.astype(BF16)).astype(BF16)

    def product(first, last, weights):
        return dot32(left_high[first:last], weights) + dot32(left_low[first:last], weights)

    wf = wf_ref[layer]
    every_q = product(0, 48, wq_ref[layer, 0])
    every_kv = jnp.concatenate([product(16, 48, wq_ref[layer, k]) for k in (1, 2)], axis=1)
    every_fc = product(24, 48, wf)
    sub = iota((8, 128), 0)

    def stack_q(block):
        return jnp.concatenate([block[:, 128 * j : 128 * j + 128] for j in range(4)], axis=0)

    def stack_kv(block):
        return jnp.concatenate(
            [
                jnp.where(
                    sub < 4,
                    block[:, 256 * j : 256 * j + 128],
                    block[:, 256 * j + 128 : 256 * j + 256],
                )
                for j in range(4)
            ],
            axis=0,
        )

    def stack_fc(block):
        tiles = []
        for j in range(4):
            tile = block[:, 512 * j : 512 * j + 128]
            for k in range(1, 4):
                start = 512 * j + 128 * k
                tile = jnp.where(sub // 2 == k, block[:, start : start + 128], tile)
            tiles.append(tile)
        return jnp.concatenate(tiles, axis=0)

    lane = iota((16, 128), 1)
    request = iota((16, 128), 0)
    stats = jnp.zeros((16, 128), F32)
    for k, part in enumerate(parts_of(mean, 3) + parts_of(square, 3)):
        stats = jnp.where(lane == request + 16 * k, part, stats)
    stats = jnp.sum(stats, axis=0, keepdims=True)
    pieces = [
        stack_q(every_q[0:8]),
        stack_q(every_q[8:16]),
        stack_kv(every_kv[0:8]),
        stack_fc(every_fc[0:8]),
        stack_fc(every_fc[8:16]),
        stack_q(every_q[40:48]),
        stack_kv(every_kv[24:32]),
        stack_fc(every_fc[16:24]),
        jnp.broadcast_to(stats, (32, 128)),
        jnp.zeros((32, 128), F32),
    ]
    for k, piece in enumerate(pieces):
        wire[pl.ds(k, 32, stride=WIRE), :] = piece
    send_ref[...] = wire[...].astype(BF16)


def call(kernel, name, outs, scratch, meta, *args, aliases=None):
    specs = [pl.BlockSpec(memory_space=pltpu.SMEM)]
    specs += [pl.BlockSpec(memory_space=pltpu.VMEM) for _ in args]
    place = pl.BlockSpec(memory_space=pltpu.VMEM)
    return pl.pallas_call(
        kernel,
        in_specs=specs,
        out_specs=jax.tree.map(lambda _: place, outs, is_leaf=lambda x: hasattr(x, "shape")),
        out_shape=outs,
        scratch_shapes=scratch,
        input_output_aliases=aliases or {},
        compiler_params=pltpu.CompilerParams(vmem_limit_bytes=24 * 2**20),
        name=name,
        interpret=INTERPRET,
    )(meta, *[near(arg) for arg in args])


def project(layer, meta, x, gain, wq, wf, branch=None):
    args = [x, gain, wq, wf] + ([] if branch is None else [branch])
    return call(
        functools.partial(project_kernel, layer, branch is not None),
        "project",
        (near_out((32 * WIRE, 128), BF16), near_out((16, 128), F32)),
        [pltpu.VMEM((32 * WIRE, 128), F32)],
        meta,
        *args,
    )


def finish_kernel(meta_ref, got_ref, first_ref, out_ref, wire, back):
    rep, blk = meta_ref[4, 0], meta_ref[4, 1]
    q_row = (blk % 8) * 2
    fc_row = rep * 4 + (blk % 2) * 2
    requests = (q_row, q_row + 1, rep * 4 + blk % 4, fc_row, fc_row + 1)
    wire[...] = got_ref[...].astype(F32)
    take = lambda k: wire[pl.ds(k, 32, stride=WIRE), :]
    stats = take(8)
    stats = stats + pltpu.roll(stats, 112, 1) + pltpu.roll(stats, 96, 1)
    average = jnp.sum(stats, axis=0, keepdims=True) * (1.0 / 32)
    offset = stats - average
    spread_sum = 64.0 * jnp.sum(offset * offset, axis=0, keepdims=True)
    square_sum = pltpu.roll(jnp.sum(stats, axis=0, keepdims=True), 80, 1)
    rstd = lax.rsqrt((square_sum + spread_sum) * (1.0 / D) + EPSILON)
    lane = iota((32, 128), 1)
    lane_one = iota((1, 128), 1)
    columns = [take(5), take(6), take(7)]
    half = ROT // 2
    for k, column in enumerate((0, 0, 1, 2, 2)):
        request = requests[k]
        row_offset = jnp.sum(jnp.where(lane == request, offset, 0.0), axis=1, keepdims=True)
        row_rstd = jnp.sum(jnp.where(lane_one == request, rstd, 0.0), axis=1, keepdims=True)
        value = row_rstd * jnp.sum(take(k) + row_offset * columns[column], axis=0, keepdims=True)
        if k < 3:
            factors = first_ref[pl.ds(request, 1), :]
            place = lane_one % HD
            turned = place < ROT if k < 2 else (place < ROT) & (blk < 16)
            left = lane_one < HD
            cosine = jnp.where(left, pltpu.roll(factors, 64, 1), factors)
            sine = jnp.where(left, pltpu.roll(factors, 32, 1), pltpu.roll(factors, 96, 1))
            other = jnp.where(
                place < half, pltpu.roll(value, 128 - half, 1), pltpu.roll(value, half, 1)
            )
            value = jnp.where(turned, value * cosine + other * sine, value)
        else:
            cubed = value * value * value
            value = (
                0.5 * value * (1.0 + jnp.tanh(math.sqrt(2.0 / math.pi) * (value + 0.044715 * cubed)))
            )
        back[pl.ds(k, 32, stride=BACK), :] = jnp.broadcast_to(value, (32, 128))
    back[pl.ds(5, 32, stride=BACK), :] = jnp.zeros((32, 128), F32)
    out_ref[...] = back[...].astype(BF16)


def finish(meta, got, first):
    return call(
        finish_kernel,
        "finish",
        near_out((32 * BACK, 128), BF16),
        [pltpu.VMEM((32 * WIRE, 128), F32), pltpu.VMEM((32 * BACK, 128), F32)],
        meta,
        got,
        first,
    )


def attend_kernel(layer, aliased, meta_ref, got_ref, cache_ref, *refs):
    if aliased:
        _, pages_ref, out_ref, back, kv = refs
    else:
        pages_ref, out_ref, back, kv = refs
    back[...] = got_ref[...].astype(F32)
    take = lambda k: back[pl.ds(k, 32, stride=BACK), :]
    new = take(2)
    for j in range(4):
        for part in range(2):
            chunk = 2 * j + part
            kv[chunk // 4, :, 128 * (chunk % 4) : 128 * (chunk % 4) + 128] = new[
                8 * j + 4 * part : 8 * j + 4 * part + 4
            ]
    spot = iota((PAGE, 512), 0)
    for side in range(2):
        for page in range(8):
            home = jnp.clip(meta_ref[0, page] - meta_ref[4, 0] * 4, 0, 3)
            place = jnp.where(meta_ref[3, page] == 1, meta_ref[2, page], -1)
            fresh = kv[side, pl.ds(home, 1), :]
            old = cache_ref[layer, side, page].astype(F32)
            pages_ref[layer, side, page] = jnp.where(spot == place, fresh, old).astype(BF16)
    head_of = iota((8, 512), 1) // HD == iota((8, 512), 0)
    sides = []
    for k in range(2):
        tall = take(k)
        sides.append(jnp.concatenate([tall[8 * j : 8 * j + 8] for j in range(4)], axis=1))
    wide = jnp.concatenate(
        [
            jnp.where(head_of, jnp.broadcast_to(sides[k][p : p + 1], (8, 512)), 0.0)
            for p in range(8)
            for k in range(2)
        ],
        axis=0,
    ).astype(BF16)
    keys = pages_ref[layer, 0].reshape(8 * PAGE, 512)
    values = pages_ref[layer, 1].reshape(8 * PAGE, 512)
    scores = dot_t(wide, keys) * HD ** (-0.5)
    page_of = iota((1, 256), 1) // PAGE
    owner = jnp.zeros((1, 256), jnp.int32)
    limit = jnp.zeros((1, 256), jnp.int32)
    for page in range(8):
        length = jnp.where(meta_ref[1, page] == 1, meta_ref[2, page] + meta_ref[3, page], 0)
        owner = jnp.where(page_of == page, meta_ref[0, page], owner)
        limit = jnp.where(page_of == page, length, limit)
    owner = jnp.where(iota((1, 256), 1) % PAGE < limit, owner, -1)
    allowed = iota((128, 256), 0) // 8 == owner
    scores = jnp.where(allowed, scores, LOWEST)
    high = jnp.max(scores, axis=1, keepdims=True)
    weights = jnp.where(allowed, jnp.exp(scores - high), 0.0)
    total = jnp.sum(weights, axis=1, keepdims=True)
    mixed = dot32(weights.astype(BF16), values)
    head = iota((128, 128), 0) % 8
    lane = iota((128, 128), 1)
    picked = mixed[:, :128]
    for k in range(1, 4):
        picked = jnp.where(head // 2 == k, mixed[:, 128 * k : 128 * k + 128], picked)
    picked = jnp.where(head % 2 == 1, pltpu.roll(picked, HD, 1), picked)
    out_ref[...] = jnp.where(
        lane < HD, picked, jnp.where(lane == HD, total, jnp.where(lane == HD + 1, high, 0.0))
    )


def attend(layer, meta, got, caches, pages=None):
    args = [got, caches] + ([] if pages is None else [pages])
    return call(
        functools.partial(attend_kernel, layer, pages is not None),
        "attend",
        (near_out(caches.shape, BF16), near_out((128, 128), F32)),
        [pltpu.VMEM((32 * BACK, 128), F32), pltpu.VMEM((2, 4, 512), F32)],
        meta,
        *args,
        aliases={} if pages is None else {3: 0},
    )


def join_kernel(got_ref, out_ref):
    got = got_ref[...]
    high = got[:, :, HD + 1 : HD + 2]
    top = jnp.max(high, axis=0)
    total = jnp.sum(got * jnp.exp(high - top[None]), axis=0)
    lane = iota((16, 128), 1)
    out = jnp.where(lane < HD, total, 0.0)
    extra = parts_of(total[:, HD : HD + 1], 3) + parts_of(top, 3)
    for k, part in enumerate(extra):
        out = jnp.where(lane == HD + k, part, out)
    out_ref[...] = jnp.broadcast_to(out.astype(BF16)[None], (16, 16, 128))


def join(got):
    return pl.pallas_call(
        join_kernel,
        out_shape=near_out((16, 16, 128), BF16),
        name="join",
        interpret=INTERPRET,
    )(near(got))


def settle_kernel(got_ref, out_ref):
    got = got_ref[...].astype(F32)
    sums = got[:, :, HD : HD + 1] + got[:, :, HD + 1 : HD + 2] + got[:, :, HD + 2 : HD + 3]
    high = got[:, :, HD + 3 : HD + 4] + got[:, :, HD + 4 : HD + 5] + got[:, :, HD + 5 : HD + 6]
    factor = jnp.exp(high - jnp.max(high, axis=0)[None])
    total = jnp.sum(sums * factor, axis=0)
    mixed = jnp.sum(got * factor, axis=0)
    out_ref[...] = jnp.where(iota((16, 128), 1) < HD, mixed / total, 0.0).astype(BF16)


def settle(got):
    return pl.pallas_call(
        settle_kernel,
        out_shape=near_out((16, 128), BF16),
        name="settle",
        interpret=INTERPRET,
    )(near(got))


def output_kernel(layer, copies, meta_ref, att_ref, got_ref, wo_ref, wf_ref, out_ref, back):
    back[...] = got_ref[...].astype(F32)
    att = att_ref[...].astype(F32)
    att = att + pltpu.roll(att, HD, 1)
    att = jnp.concatenate([att] * 4, axis=1)
    own = iota((32, 512), 1) // HD == iota((32, 512), 0) % 8
    by_head = dot_t(jnp.where(own, att, 0.0).astype(BF16), wo_ref[layer])
    chunk = iota((32, D), 1) // 128 == iota((32, D), 0) // 2
    mlp = []
    for k in range(2):
        act = back[pl.ds(3 + k, 32, stride=BACK), :]
        act = jnp.concatenate([act] * 16, axis=1)
        mlp.append(dot_t(jnp.where(chunk, act, 0.0).astype(BF16), wf_ref[layer]))
    odd = iota((32, HD), 0) % 2
    rows = []
    for i in range(4):
        from_mlp = jnp.sum(jnp.where(odd == i // 2, mlp[i % 2], 0.0), axis=0, keepdims=True)
        from_att = jnp.sum(by_head[8 * i : 8 * i + 8], axis=0, keepdims=True)
        rows.append(from_att + from_mlp)
    tile = jnp.concatenate(rows, axis=0)
    tile = jnp.concatenate([tile, jnp.zeros_like(tile)], axis=1)
    for k in range(copies):
        out_ref[4 * k : 4 * k + 4] = tile


def output(layer, copies, meta, att, got, w_out, w_fc2):
    return call(
        functools.partial(output_kernel, layer, copies),
        "output",
        near_out((4 * copies, 128), F32),
        [pltpu.VMEM((32 * BACK, 128), F32)],
        meta,
        att,
        got,
        w_out,
        w_fc2,
    )


def per_device(
    hidden,
    ln_gain,
    w_qkv,
    w_fc1,
    w_out,
    w_fc2,
    caches,
    page_owner,
    page_used,
    page_fill,
    page_tail,
    positions,
):
    rep = lax.axis_index("rep")
    blk = lax.axis_index("blk")
    zs = [[2 * z + c for z in range(16)] for c in range(2)]
    pairs = [[2 * z, 2 * z + 1] for z in range(16)]
    rep_core = [[r * 32 + 2 * z + c for r in range(4) for c in range(2)] for z in range(16)]

    first = jnp.concatenate([hidden.astype(F32), rope_factors(positions)], axis=1)
    first = spread(first, 4, "rep").reshape(16, 128)
    place = jnp.where(jnp.arange(8) == 0, rep, blk).astype(jnp.int32)
    meta = jnp.stack([page_owner, page_used, page_fill, page_tail, place])
    w_qkv = w_qkv.transpose(0, 2, 1, 3)
    w_out = w_out.transpose(0, 2, 1)
    w_fc2 = w_fc2.transpose(0, 2, 1)

    state, branch, pages = first, None, None
    for layer in range(LAYERS):
        send, state = project(layer, meta, state, ln_gain, w_qkv, w_fc1, branch)
        got = exchange(send.reshape(32, WIRE // 2, 2, 128), "blk").reshape(32 * WIRE, 128)
        back = finish(meta, got, first)
        got = exchange(back.reshape(32, BACK // 2, 2, 128), "blk").reshape(32 * BACK, 128)
        pages, parts = attend(layer, meta, got, caches, pages)
        parts = exchange(parts.reshape(8, 16, 128), ("rep", "blk"), rep_core)
        parts = exchange(join(parts), "blk", zs)
        att = lax.all_gather(settle(parts), "blk", axis_index_groups=pairs, tiled=True)
        if layer + 1 < LAYERS:
            out = output(layer, 16, meta, att, got, w_out, w_fc2).reshape(16, 4, 128)
            branch = exchange(out, ("rep", "tp")).reshape(64, 128)
        else:
            out = output(layer, 4, meta, att, got, w_out, w_fc2).reshape(4, 4, 128)
            branch = jnp.sum(exchange(out, "tp"), axis=0)[:, :HD]
            own = lax.dynamic_slice(state, (rep * 4, 0), (4, HD))
            result = (own + branch).astype(BF16)
    return (result, pages)


def solution(mesh):
    in_specs = (
        P("rep", "blk"),
        P(None, "blk"),
        P(None, "blk", None, "tp"),
        P(None, "blk", "tp"),
        P(None, "tp", "blk"),
        P(None, "tp", "blk"),
        P(None, None, ("rep", "blk"), None, "tp"),
        P(("rep", "blk")),
        P(("rep", "blk")),
        P(("rep", "blk")),
        P(("rep", "blk")),
        P("rep"),
    )
    out_specs = (P("rep", "blk"), P(None, None, ("rep", "blk"), None, "tp"))
    return jax.shard_map(
        per_device, mesh=mesh, in_specs=in_specs, out_specs=out_specs, check_vma=False
    )
```

```python
import functools
import math

import jax
import jax.numpy as jnp
from jax import lax
from jax.experimental import pallas as pl
from jax.experimental.pallas import tpu as pltpu
from jax.sharding import PartitionSpec as P

D = 2048
HD = 64
ROT = 32
LAYERS = 2
PAGE = 32
EPSILON = 1e-05
LOWEST = -1e30
F32 = jnp.float32
BF16 = jnp.bfloat16
INTERPRET = False
WIRE = 10
CUT = 896
BACK = 6


def exchange(value, axis, groups=None):
    return lax.all_to_all(value, axis, 0, 0, tiled=True, axis_index_groups=groups)


def spread(value, count, axis, groups=None):
    return exchange(jnp.broadcast_to(value[None], (count,) + value.shape), axis, groups)


def rope_factors(positions):
    lane = jnp.arange(64, dtype=jnp.int32)
    steps_f = (lane % (ROT // 2)).astype(F32)
    angles = positions.astype(F32)[:, None] * (10000.0 ** (-2.0 * steps_f / ROT))[None, :]
    sine = jnp.sin(angles)
    return jnp.where(lane < 32, jnp.cos(angles), jnp.where(lane < 48, -sine, sine))


def near(value):
    return value if INTERPRET else pltpu.with_memory_space_constraint(value, pltpu.VMEM)


def near_out(shape, dtype):
    return jax.ShapeDtypeStruct(shape, dtype) if INTERPRET else pltpu.VMEM(shape, dtype)


def iota(shape, axis):
    return lax.broadcasted_iota(jnp.int32, shape, axis)


def dot32(left, right):
    return jnp.dot(left, right, preferred_element_type=F32)


def dot_t(left, right):
    return lax.dot_general(left, right, (((1,), (1,)), ((), ())), preferred_element_type=F32)


def parts_of(value, count):
    found = []
    for _ in range(count):
        part = value.astype(BF16).astype(F32)
        found.append(part)
        value = value - part
    return found


def rope(value, factors, turned):
    lane = iota(value.shape, 1)
    left = lane < HD
    half = ROT // 2
    cosine = jnp.where(left, pltpu.roll(factors, 64, 1), factors)
    sine = jnp.where(left, pltpu.roll(factors, 32, 1), pltpu.roll(factors, 96, 1))
    other = jnp.where(
        lane % HD < half, pltpu.roll(value, 128 - half, 1), pltpu.roll(value, half, 1)
    )
    return jnp.where(turned & (lane % HD < ROT), value * cosine + other * sine, value)


def gelu(value):
    cubed = value * value * value
    return 0.5 * value * (1.0 + jnp.tanh(math.sqrt(2.0 / math.pi) * (value + 0.044715 * cubed)))


def project_kernel(meta_ref, x_ref, gain_ref, wq_ref, wf_ref, send_ref, cut_ref, wire):
    layer = 0
    quarter = pl.multiple_of(meta_ref[4, 0] * 128, 128)
    for k in range(3):
        cut_ref[:, 128 * k : 128 * k + 128] = wq_ref[1, k, :, pl.ds(quarter, 128)]
    cut_ref[:, 384:] = wf_ref[1, :, pl.ds(pl.multiple_of(meta_ref[4, 0] * 512, 512), 512)]
    x = x_ref[:, :HD]
    gain = gain_ref[layer : layer + 1]
    mean = jnp.sum(x, axis=1, keepdims=True) * (1.0 / HD)
    centered = x - mean
    square = jnp.sum(centered * centered, axis=1, keepdims=True)
    scaled = centered * gain
    row = iota((48, 24), 0)
    col = iota((48, 24), 1)
    own = meta_ref[4, 0] * 4
    within = row % 8
    want = jnp.where(
        row < 8,
        2 * within,
        jnp.where(
            row < 16,
            2 * within + 1,
            jnp.where(
                row < 24,
                own + within % 4,
                jnp.where(
                    row < 32,
                    own + 2 * (within % 2),
                    jnp.where(row < 40, own + 2 * (within % 2) + 1, 16),
                ),
            ),
        ),
    )
    choose = (col == want).astype(BF16)
    rows = jnp.concatenate([scaled, jnp.broadcast_to(gain, (8, HD))], axis=0)
    high, low = parts_of(rows, 2)
    left_high = dot32(choose, high.astype(BF16)).astype(BF16)
    left_low = dot32(choose, low.astype(BF16)).astype(BF16)

    def product(first, last, weights):
        return dot32(left_high[first:last], weights) + dot32(left_low[first:last], weights)

    wf = wf_ref[layer]
    every_q = product(0, 48, wq_ref[layer, 0])
    every_kv = jnp.concatenate([product(16, 48, wq_ref[layer, k]) for k in (1, 2)], axis=1)
    every_fc = product(24, 48, wf)
    sub = iota((8, 128), 0)

    def stack_q(block):
        return jnp.concatenate([block[:, 128 * j : 128 * j + 128] for j in range(4)], axis=0)

    def stack_kv(block):
        return jnp.concatenate(
            [
                jnp.where(
                    sub < 4,
                    block[:, 256 * j : 256 * j + 128],
                    block[:, 256 * j + 128 : 256 * j + 256],
                )
                for j in range(4)
            ],
            axis=0,
        )

    def stack_fc(block):
        tiles = []
        for j in range(4):
            tile = block[:, 512 * j : 512 * j + 128]
            for k in range(1, 4):
                start = 512 * j + 128 * k
                tile = jnp.where(sub // 2 == k, block[:, start : start + 128], tile)
            tiles.append(tile)
        return jnp.concatenate(tiles, axis=0)

    lane = iota((16, 128), 1)
    request = iota((16, 128), 0)
    stats = jnp.zeros((16, 128), F32)
    for k, part in enumerate(parts_of(mean, 3) + parts_of(square, 3)):
        stats = jnp.where(lane == request + 16 * k, part, stats)
    stats = jnp.sum(stats, axis=0, keepdims=True)
    later = jnp.concatenate(parts_of(gain_ref[1:2], 2), axis=1)
    pieces = [
        stack_q(every_q[0:8]),
        stack_q(every_q[8:16]),
        stack_kv(every_kv[0:8]),
        stack_fc(every_fc[0:8]),
        stack_fc(every_fc[8:16]),
        stack_q(every_q[40:48]),
        stack_kv(every_kv[24:32]),
        stack_fc(every_fc[16:24]),
        jnp.broadcast_to(stats, (32, 128)),
        jnp.broadcast_to(later, (32, 128)),
    ]
    for k, piece in enumerate(pieces):
        wire[pl.ds(k, 32, stride=WIRE), :] = piece
    send_ref[...] = wire[...].astype(BF16)


def call(kernel, name, outs, scratch, meta, *args, aliases=None):
    specs = [pl.BlockSpec(memory_space=pltpu.SMEM)]
    specs += [pl.BlockSpec(memory_space=pltpu.VMEM) for _ in args]
    place = pl.BlockSpec(memory_space=pltpu.VMEM)
    return pl.pallas_call(
        kernel,
        in_specs=specs,
        out_specs=jax.tree.map(lambda _: place, outs, is_leaf=lambda x: hasattr(x, "shape")),
        out_shape=outs,
        scratch_shapes=scratch,
        input_output_aliases=aliases or {},
        compiler_params=pltpu.CompilerParams(vmem_limit_bytes=24 * 2**20),
        name=name,
        interpret=INTERPRET,
    )(meta, *[near(arg) for arg in args])


def project(meta, x, gain, wq, wf):
    return call(
        project_kernel,
        "project",
        (near_out((32 * WIRE, 128), BF16), near_out((HD, CUT), BF16)),
        [pltpu.VMEM((32 * WIRE, 128), F32)],
        meta,
        x,
        gain,
        wq,
        wf,
    )


def finish_kernel(meta_ref, got_ref, first_ref, out_ref, gain_ref, wire, back):
    rep, blk = meta_ref[4, 0], meta_ref[4, 1]
    q_row = (blk % 8) * 2
    fc_row = rep * 4 + (blk % 2) * 2
    requests = (q_row, q_row + 1, rep * 4 + blk % 4, fc_row, fc_row + 1)
    wire[...] = got_ref[...].astype(F32)
    take = lambda k: wire[pl.ds(k, 32, stride=WIRE), :]
    stats = take(8)
    stats = stats + pltpu.roll(stats, 112, 1) + pltpu.roll(stats, 96, 1)
    average = jnp.sum(stats, axis=0, keepdims=True) * (1.0 / 32)
    offset = stats - average
    spread_sum = 64.0 * jnp.sum(offset * offset, axis=0, keepdims=True)
    square_sum = pltpu.roll(jnp.sum(stats, axis=0, keepdims=True), 80, 1)
    rstd = lax.rsqrt((square_sum + spread_sum) * (1.0 / D) + EPSILON)
    lane = iota((32, 128), 1)
    lane_one = iota((1, 128), 1)
    columns = [take(5), take(6), take(7)]
    for k, column in enumerate((0, 0, 1, 2, 2)):
        request = requests[k]
        row_offset = jnp.sum(jnp.where(lane == request, offset, 0.0), axis=1, keepdims=True)
        row_rstd = jnp.sum(jnp.where(lane_one == request, rstd, 0.0), axis=1, keepdims=True)
        value = row_rstd * jnp.sum(take(k) + row_offset * columns[column], axis=0, keepdims=True)
        if k < 3:
            turned = jnp.full((1, 128), True) if k < 2 else jnp.full((1, 128), blk) < 16
            value = rope(value, first_ref[pl.ds(request, 1), :], turned)
        else:
            value = gelu(value)
        back[pl.ds(k, 32, stride=BACK), :] = jnp.broadcast_to(value, (32, 128))
    back[pl.ds(5, 32, stride=BACK), :] = jnp.zeros((32, 128), F32)
    out_ref[...] = back[...].astype(BF16)
    later = take(9)
    later = later + pltpu.roll(later, HD, 1)
    for z in range(16):
        gain_ref[:, 128 * z : 128 * z + 128] = jnp.where(
            lane_one < HD, later[2 * z : 2 * z + 1], later[2 * z + 1 : 2 * z + 2]
        )


def finish(meta, got, first):
    return call(
        finish_kernel,
        "finish",
        (near_out((32 * BACK, 128), BF16), near_out((1, D), F32)),
        [pltpu.VMEM((32 * WIRE, 128), F32), pltpu.VMEM((32 * BACK, 128), F32)],
        meta,
        got,
        first,
    )


def renew_kernel(meta_ref, x_ref, branch_ref, out_ref, state_ref):
    sums = []
    for rep in range(4):
        total = branch_ref[rep * 16 : rep * 16 + 4]
        for tp in range(1, 4):
            start = rep * 16 + tp * 4
            total = total + branch_ref[start : start + 4]
        sums.append(total)
    x = (x_ref[...] + jnp.concatenate(sums, axis=0)).astype(BF16).astype(F32)
    state_ref[...] = x
    packed = jnp.where(iota((8, 128), 1) < HD, x[:8], pltpu.roll(x[8:], HD, 1)).astype(BF16)
    out_ref[...] = jnp.broadcast_to(packed[None], (32, 8, 128))


def renew(meta, x, branch):
    return call(
        renew_kernel,
        "renew",
        (near_out((32, 8, 128), BF16), near_out((16, 128), F32)),
        [],
        meta,
        x,
        branch,
    )


def deepen_kernel(meta_ref, got_ref, gain_ref, deep_ref, out_ref):
    left = iota((8, 128), 1) < HD
    tiles = []
    for z in range(16):
        even = got_ref[2 * z].astype(F32)
        odd = got_ref[2 * z + 1].astype(F32)
        top = jnp.where(left, even, pltpu.roll(odd, HD, 1))
        bottom = jnp.where(left, pltpu.roll(even, HD, 1), odd)
        tiles.append(jnp.concatenate([top, bottom], axis=0))
    x = jnp.concatenate(tiles, axis=1)
    average = jnp.sum(x, axis=1, keepdims=True) * (1.0 / D)
    centered = x - average
    variance = jnp.sum(centered * centered, axis=1, keepdims=True) * (1.0 / D)
    normed = centered * lax.rsqrt(variance + EPSILON) * gain_ref[...]
    low = iota((16, 128), 1) < HD
    first_core = jnp.full((16, 128), meta_ref[4, 1] % 2) == 0
    tiles = []
    for pair in range(8):
        one = normed[:, 256 * pair : 256 * pair + 128]
        two = normed[:, 256 * pair + 128 : 256 * pair + 256]
        tiles.append(
            jnp.where(
                first_core,
                jnp.where(low, one, pltpu.roll(two, HD, 1)),
                jnp.where(low, pltpu.roll(one, HD, 1), two),
            )
        )
    mixed = dot32(jnp.concatenate(tiles, axis=1).astype(BF16), deep_ref[...])
    for rep in range(4):
        rows = mixed[4 * rep : 4 * rep + 4]
        parts = [mixed[:, :128]] + [rows[:, 128 * k : 128 * k + 128] for k in range(1, 7)]
        block = jnp.concatenate(parts, axis=0).astype(BF16)
        for core in range(2):
            out_ref[2 * rep + core] = block


def deepen(meta, got, gain, deep):
    return call(
        deepen_kernel, "deepen", near_out((8, 40, 128), BF16), [], meta, got, gain, deep
    )


def gather_shallow(got_ref, back, kv):
    back[...] = got_ref[...].astype(F32)
    take = lambda k: back[pl.ds(k, 32, stride=BACK), :]
    new = take(2)
    for chunk in range(8):
        kv[chunk // 4, :, 128 * (chunk % 4) : 128 * (chunk % 4) + 128] = new[
            4 * chunk : 4 * chunk + 4
        ]
    sides = []
    for k in range(2):
        tall = take(k)
        sides.append(jnp.concatenate([tall[8 * j : 8 * j + 8] for j in range(4)], axis=1))
    return [sides[i % 2][i // 2 : i // 2 + 1] for i in range(16)]


def gather_deep(meta_ref, got_ref, first_ref, kv):
    own = first_ref[pl.ds(meta_ref[4, 0] * 4, 4), :]
    tiles = []
    for r in range(4):
        both = got_ref[2 * r, :24].astype(F32) + got_ref[2 * r + 1, :24].astype(F32)
        tiles.append(rope(both[:16], first_ref[...], jnp.full((16, 128), True)))
        kv[0, :, 128 * r : 128 * r + 128] = rope(both[16:20], own, jnp.full((4, 128), True))
        kv[1, :, 128 * r : 128 * r + 128] = both[20:24]
    queries = jnp.concatenate(tiles, axis=1)
    return [queries[i : i + 1] for i in range(16)]


def attend_kernel(layer, meta_ref, got_ref, cache_ref, *refs):
    if layer == 0:
        pages_ref, out_ref, back, kv = refs
        queries = gather_shallow(got_ref, back, kv)
    else:
        first_ref, _, pages_ref, out_ref, kv = refs
        queries = gather_deep(meta_ref, got_ref, first_ref, kv)
    spot = iota((PAGE, 512), 0)
    for side in range(2):
        for page in range(8):
            home = jnp.clip(meta_ref[0, page] - meta_ref[4, 0] * 4, 0, 3)
            place = jnp.where(meta_ref[3, page] == 1, meta_ref[2, page], -1)
            fresh = kv[side, pl.ds(home, 1), :]
            old = cache_ref[layer, side, page].astype(F32)
            pages_ref[layer, side, page] = jnp.where(spot == place, fresh, old).astype(BF16)
    head_of = iota((8, 512), 1) // HD == iota((8, 512), 0)
    wide = jnp.concatenate(
        [jnp.where(head_of, jnp.broadcast_to(row, (8, 512)), 0.0) for row in queries], axis=0
    ).astype(BF16)
    keys = pages_ref[layer, 0].reshape(8 * PAGE, 512)
    values = pages_ref[layer, 1].reshape(8 * PAGE, 512)
    scores = dot_t(wide, keys) * HD ** (-0.5)
    page_of = iota((1, 256), 1) // PAGE
    owner = jnp.zeros((1, 256), jnp.int32)
    limit = jnp.zeros((1, 256), jnp.int32)
    for page in range(8):
        length = jnp.where(meta_ref[1, page] == 1, meta_ref[2, page] + meta_ref[3, page], 0)
        owner = jnp.where(page_of == page, meta_ref[0, page], owner)
        limit = jnp.where(page_of == page, length, limit)
    owner = jnp.where(iota((1, 256), 1) % PAGE < limit, owner, -1)
    allowed = iota((128, 256), 0) // 8 == owner
    scores = jnp.where(allowed, scores, LOWEST)
    high = jnp.max(scores, axis=1, keepdims=True)
    weights = jnp.where(allowed, jnp.exp(scores - high), 0.0)
    total = jnp.sum(weights, axis=1, keepdims=True)
    mixed = dot32(weights.astype(BF16), values)
    head = iota((128, 128), 0) % 8
    lane = iota((128, 128), 1)
    picked = mixed[:, :128]
    for k in range(1, 4):
        picked = jnp.where(head // 2 == k, mixed[:, 128 * k : 128 * k + 128], picked)
    picked = jnp.where(head % 2 == 1, pltpu.roll(picked, HD, 1), picked)
    out_ref[...] = jnp.where(
        lane < HD, picked, jnp.where(lane == HD, total, jnp.where(lane == HD + 1, high, 0.0))
    )


def attend(layer, meta, got, caches, *more):
    back = [pltpu.VMEM((32 * BACK, 128), F32)] if layer == 0 else []
    return call(
        functools.partial(attend_kernel, layer),
        "attend",
        (near_out(caches.shape, BF16), near_out((128, 128), F32)),
        back + [pltpu.VMEM((2, 4, 512), F32)],
        meta,
        got,
        caches,
        *more,
        aliases={} if layer == 0 else {4: 0},
    )


def join_kernel(got_ref, out_ref):
    got = got_ref[...]
    high = got[:, :, HD + 1 : HD + 2]
    top = jnp.max(high, axis=0)
    total = jnp.sum(got * jnp.exp(high - top[None]), axis=0)
    lane = iota((16, 128), 1)
    out = jnp.where(lane < HD, total, 0.0)
    extra = parts_of(total[:, HD : HD + 1], 3) + parts_of(top, 3)
    for k, part in enumerate(extra):
        out = jnp.where(lane == HD + k, part, out)
    out_ref[...] = jnp.broadcast_to(out.astype(BF16)[None], (16, 16, 128))


def join(got):
    return pl.pallas_call(
        join_kernel,
        out_shape=near_out((16, 16, 128), BF16),
        name="join",
        interpret=INTERPRET,
    )(near(got))


def settle_kernel(got_ref, out_ref):
    got = got_ref[...].astype(F32)
    sums = got[:, :, HD : HD + 1] + got[:, :, HD + 1 : HD + 2] + got[:, :, HD + 2 : HD + 3]
    high = got[:, :, HD + 3 : HD + 4] + got[:, :, HD + 4 : HD + 5] + got[:, :, HD + 5 : HD + 6]
    factor = jnp.exp(high - jnp.max(high, axis=0)[None])
    total = jnp.sum(sums * factor, axis=0)
    mixed = jnp.sum(got * factor, axis=0)
    out_ref[...] = jnp.where(iota((16, 128), 1) < HD, mixed / total, 0.0).astype(BF16)


def settle(got):
    return pl.pallas_call(
        settle_kernel,
        out_shape=near_out((16, 128), BF16),
        name="settle",
        interpret=INTERPRET,
    )(near(got))


def output_kernel(layer, copies, meta_ref, att_ref, got_ref, wo_ref, wf_ref, out_ref, *scratch):
    att = att_ref[...].astype(F32)
    att = att + pltpu.roll(att, HD, 1)
    att = jnp.concatenate([att] * 4, axis=1)
    own = iota((32, 512), 1) // HD == iota((32, 512), 0) % 8
    by_head = dot_t(jnp.where(own, att, 0.0).astype(BF16), wo_ref[layer])
    rows = [jnp.sum(by_head[8 * i : 8 * i + 8], axis=0, keepdims=True) for i in range(4)]
    if layer == 0:
        back = scratch[0]
        back[...] = got_ref[...].astype(F32)
        chunk = iota((32, D), 1) // 128 == iota((32, D), 0) // 2
        mlp = []
        for k in range(2):
            act = back[pl.ds(3 + k, 32, stride=BACK), :]
            act = jnp.concatenate([act] * 16, axis=1)
            mlp.append(dot_t(jnp.where(chunk, act, 0.0).astype(BF16), wf_ref[layer]))
        odd = iota((32, HD), 0) % 2
        rows = [
            rows[i] + jnp.sum(jnp.where(odd == i // 2, mlp[i % 2], 0.0), axis=0, keepdims=True)
            for i in range(4)
        ]
    else:
        tiles = []
        for r in range(4):
            both = got_ref[2 * r, 24:].astype(F32) + got_ref[2 * r + 1, 24:].astype(F32)
            tiles += [gelu(both[4 * k : 4 * k + 4]) for k in range(4)]
        mlp = dot_t(jnp.concatenate(tiles, axis=1).astype(BF16), wf_ref[layer])
        rows = [rows[i] + mlp[i : i + 1] for i in range(4)]
    tile = jnp.concatenate(rows, axis=0)
    tile = jnp.concatenate([tile, jnp.zeros_like(tile)], axis=1)
    for k in range(copies):
        out_ref[4 * k : 4 * k + 4] = tile


def output(layer, copies, meta, att, got, w_out, w_fc2):
    return call(
        functools.partial(output_kernel, layer, copies),
        "output",
        near_out((4 * copies, 128), F32),
        [pltpu.VMEM((32 * BACK, 128), F32)] if layer == 0 else [],
        meta,
        att,
        got,
        w_out,
        w_fc2,
    )


def per_device(
    hidden,
    ln_gain,
    w_qkv,
    w_fc1,
    w_out,
    w_fc2,
    caches,
    page_owner,
    page_used,
    page_fill,
    page_tail,
    positions,
):
    rep = lax.axis_index("rep")
    blk = lax.axis_index("blk")
    zs = [[2 * z + c for z in range(16)] for c in range(2)]
    pairs = [[2 * z, 2 * z + 1] for z in range(16)]
    rep_core = [[r * 32 + 2 * z + c for r in range(4) for c in range(2)] for z in range(16)]

    first = jnp.concatenate([hidden.astype(F32), rope_factors(positions)], axis=1)
    first = spread(first, 4, "rep").reshape(16, 128)
    place = jnp.where(jnp.arange(8) == 0, rep, blk).astype(jnp.int32)
    meta = jnp.stack([page_owner, page_used, page_fill, page_tail, place])
    w_qkv = w_qkv.transpose(0, 2, 1, 3)
    w_out = w_out.transpose(0, 2, 1)
    w_fc2 = w_fc2.transpose(0, 2, 1)

    def combine(parts):
        parts = exchange(parts.reshape(8, 16, 128), ("rep", "blk"), rep_core)
        parts = exchange(join(parts), "blk", zs)
        return lax.all_gather(settle(parts), "blk", axis_index_groups=pairs, tiled=True)

    send, cut = project(meta, first, ln_gain, w_qkv, w_fc1)
    deep = lax.all_gather(cut, "blk", axis_index_groups=zs, tiled=True)
    got = exchange(send.reshape(32, WIRE // 2, 2, 128), "blk").reshape(32 * WIRE, 128)
    back, gain = finish(meta, got, first)
    got = exchange(back.reshape(32, BACK // 2, 2, 128), "blk").reshape(32 * BACK, 128)
    pages, parts = attend(0, meta, got, caches)
    out = output(0, 16, meta, combine(parts), got, w_out, w_fc2).reshape(16, 4, 128)
    branch = exchange(out, ("rep", "tp")).reshape(64, 128)

    piece, state = renew(meta, first, branch)
    got = exchange(deepen(meta, exchange(piece, "blk"), gain, deep), ("rep", "blk"), rep_core)
    pages, parts = attend(1, meta, got, caches, first, pages)
    out = output(1, 4, meta, combine(parts), got, w_out, w_fc2).reshape(4, 4, 128)
    branch = jnp.sum(exchange(out, "tp"), axis=0)[:, :HD]
    own = lax.dynamic_slice(state, (rep * 4, 0), (4, HD))
    return ((own + branch).astype(BF16), pages)


def solution(mesh):
    in_specs = (
        P("rep", "blk"),
        P(None, "blk"),
        P(None, "blk", None, "tp"),
        P(None, "blk", "tp"),
        P(None, "tp", "blk"),
        P(None, "tp", "blk"),
        P(None, None, ("rep", "blk"), None, "tp"),
        P(("rep", "blk")),
        P(("rep", "blk")),
        P(("rep", "blk")),
        P(("rep", "blk")),
        P("rep"),
    )
    out_specs = (P("rep", "blk"), P(None, None, ("rep", "blk"), None, "tp"))
    return jax.shard_map(
        per_device, mesh=mesh, in_specs=in_specs, out_specs=out_specs, check_vma=False
    )
```

```python
import functools
import math

import jax
import jax.numpy as jnp
from jax import lax
from jax.experimental import pallas as pl
from jax.experimental.pallas import tpu as pltpu
from jax.sharding import PartitionSpec as P

D = 2048
HD = 64
ROT = 32
LAYERS = 2
PAGE = 32
EPSILON = 1e-05
LOWEST = -1e30
F32 = jnp.float32
BF16 = jnp.bfloat16
INTERPRET = False
HALF = 296
FLOW = 64
JOIN = 18


def exchange(value, axis, groups=None):
    return lax.all_to_all(value, axis, 0, 0, tiled=True, axis_index_groups=groups)


def spread(value, count, axis, groups=None):
    return exchange(jnp.broadcast_to(value[None], (count,) + value.shape), axis, groups)


def rope_factors(positions):
    lane = jnp.arange(64, dtype=jnp.int32)
    steps_f = (lane % (ROT // 2)).astype(F32)
    angles = positions.astype(F32)[:, None] * (10000.0 ** (-2.0 * steps_f / ROT))[None, :]
    sine = jnp.sin(angles)
    return jnp.where(lane < 32, jnp.cos(angles), jnp.where(lane < 48, -sine, sine))


def near(value):
    return value if INTERPRET else pltpu.with_memory_space_constraint(value, pltpu.VMEM)


def near_out(shape, dtype):
    return jax.ShapeDtypeStruct(shape, dtype) if INTERPRET else pltpu.VMEM(shape, dtype)


def iota(shape, axis):
    return lax.broadcasted_iota(jnp.int32, shape, axis)


def dot32(left, right):
    return jnp.dot(left, right, preferred_element_type=F32)


def dot_t(left, right):
    return lax.dot_general(left, right, (((1,), (1,)), ((), ())), preferred_element_type=F32)


def parts_of(value, count):
    found = []
    for _ in range(count):
        part = value.astype(BF16).astype(F32)
        found.append(part)
        value = value - part
    return found


def rope(value, factors):
    lane = iota(value.shape, 1)
    left = lane < HD
    half = ROT // 2
    cosine = jnp.where(left, pltpu.roll(factors, 64, 1), factors)
    sine = jnp.where(left, pltpu.roll(factors, 32, 1), pltpu.roll(factors, 96, 1))
    other = jnp.where(
        lane % HD < half, pltpu.roll(value, 128 - half, 1), pltpu.roll(value, half, 1)
    )
    return jnp.where(lane % HD < ROT, value * cosine + other * sine, value)


def gelu(value):
    cubed = value * value * value
    return 0.5 * value * (1.0 + jnp.tanh(math.sqrt(2.0 / math.pi) * (value + 0.044715 * cubed)))


def column_of(row, first, period, shape):
    mine = iota(shape, 1) == first + iota(shape, 0) % period
    return jnp.sum(jnp.where(mine, row, 0.0), axis=1, keepdims=True)


def project_kernel(layer, with_branch, meta_ref, x_ref, gain_ref, wq_ref, wf_ref, *refs):
    if with_branch:
        branch_ref, out_ref, state_ref = refs
        sums = []
        for rep in range(4):
            total = branch_ref[rep * 16 : rep * 16 + 4]
            for tp in range(1, 4):
                start = rep * 16 + tp * 4
                total = total + branch_ref[start : start + 4]
            sums.append(total)
        state_ref[...] = (x_ref[...] + jnp.concatenate(sums, axis=0)).astype(BF16).astype(F32)
    else:
        out_ref, state_ref = refs
        state_ref[...] = x_ref[...]
    own = state_ref[pl.ds(meta_ref[4, 0] * 4, 4), :]
    x = jnp.concatenate([state_ref[...], own], axis=0)[:, :HD]
    gain = gain_ref[layer : layer + 1]
    mean = jnp.sum(x, axis=1, keepdims=True) * (1.0 / HD)
    centered = x - mean
    square = jnp.sum(centered * centered, axis=1, keepdims=True)
    rows = jnp.concatenate([centered * gain, jnp.broadcast_to(gain, (4, HD))], axis=0)
    high, low = parts_of(rows, 2)
    high, low = high.astype(BF16), low.astype(BF16)
    for k in range(3):
        every = dot32(high, wq_ref[layer, k]) + dot32(low, wq_ref[layer, k])
        for j in range(4):
            tile = every[:, 128 * j : 128 * j + 128]
            if k == 0:
                out_ref[24 * j : 24 * j + 24] = tile
            else:
                start = 96 + 8 * (4 * (k - 1) + j)
                out_ref[start : start + 8] = tile[16:]
    every = dot32(high[16:], wf_ref[layer]) + dot32(low[16:], wf_ref[layer])
    for j in range(16):
        out_ref[160 + 8 * j : 168 + 8 * j] = every[:, 128 * j : 128 * j + 128]
    lane = iota((16, 128), 1)
    request = iota((16, 128), 0)
    stats = jnp.where(
        lane == request, mean[:16], jnp.where(lane == request + 16, square[:16], 0.0)
    )
    out_ref[288:296] = jnp.broadcast_to(jnp.sum(stats, axis=0, keepdims=True), (8, 128))


def call(kernel, name, outs, scratch, meta, *args, aliases=None):
    specs = [pl.BlockSpec(memory_space=pltpu.SMEM)]
    specs += [pl.BlockSpec(memory_space=pltpu.VMEM) for _ in args]
    place = pl.BlockSpec(memory_space=pltpu.VMEM)
    return pl.pallas_call(
        kernel,
        in_specs=specs,
        out_specs=jax.tree.map(lambda _: place, outs, is_leaf=lambda x: hasattr(x, "shape")),
        out_shape=outs,
        scratch_shapes=scratch,
        input_output_aliases=aliases or {},
        compiler_params=pltpu.CompilerParams(vmem_limit_bytes=24 * 2**20),
        name=name,
        interpret=INTERPRET,
    )(meta, *[near(arg) for arg in args])


def project(layer, meta, x, gain, wq, wf, *branch):
    return call(
        functools.partial(project_kernel, layer, len(branch) > 0),
        "project",
        (near_out((HALF, 128), F32), near_out((16, 128), F32)),
        [],
        meta,
        x,
        gain,
        wq,
        wf,
        *branch,
    )


def pool_kernel(meta_ref, got_ref, out_ref):
    core = meta_ref[4, 1] % 2
    first = meta_ref[4, 0] * 4
    means = [got_ref[s, 288:289] for s in range(2)]
    center = 0.5 * (means[0] + means[1])
    moves = [mean - center for mean in means]
    square = pltpu.roll(means[0] + means[1], 112, 1) + 64.0 * (
        moves[0] * moves[0] + moves[1] * moves[1]
    )
    shift_all = [column_of(move, 0, 16, (16, 128)) for move in moves]
    upper = iota((8, 1), 0) < 4
    shift_own = [jnp.where(upper, column_of(move, first, 4, (8, 128)), 0.0) for move in moves]

    def block(start):
        total = 0.0
        for s in range(2):
            part = got_ref[s, pl.ds(pl.multiple_of(start, 8), 8), :]
            total = total + part + shift_own[s] * part[4:5]
        return total

    common = []
    columns = []
    for j in range(2):
        start = 48 * core + 24 * j
        total, column = 0.0, 0.0
        for s in range(2):
            part = got_ref[s, pl.ds(pl.multiple_of(start, 8), 24), :]
            total = total + part[:16] + shift_all[s] * part[20:21]
            column = column + part[20:21]
        common.append(total)
        columns.append(column)
    for base in (96, 128):
        one = block(base + 16 * core)
        two = block(base + 16 * core + 8)
        common.append(jnp.where(upper, one, pltpu.roll(two, 4, 0)))
        columns += [one[4:5], two[4:5]]
    lane = iota((16, 128), 1)
    request = iota((16, 128), 0)
    stats = jnp.zeros((16, 128), F32)
    both = parts_of(column_of(center, 0, 16, (16, 128)), 3)
    both += parts_of(column_of(square, 0, 16, (16, 128)), 3)
    for k, part in enumerate(both):
        stats = jnp.where(lane == request + 16 * k, part, stats)
    columns.append(jnp.sum(stats, axis=0, keepdims=True))
    tail = jnp.zeros((8, 128), F32)
    for k, column in enumerate(columns):
        tail = jnp.where(iota((8, 128), 0) == k, column, tail)
    common.append(tail)
    shared = jnp.concatenate(common, axis=0)
    for m in range(8):
        whole = jnp.concatenate([shared, block(160 + 64 * core + 8 * m)], axis=0).astype(BF16)
        out_ref[2 * m] = whole
        out_ref[2 * m + 1] = whole


def pool(meta, got):
    return call(pool_kernel, "pool", near_out((16, FLOW, 128), BF16), [], meta, got)


def finish_kernel(meta_ref, got_ref, first_ref, out_ref, act_ref, own_scratch):
    first = meta_ref[4, 0] * 4
    tails = [got_ref[z, 48:].astype(F32) for z in range(16)]
    stats = jnp.concatenate([tail[6:7] for tail in tails], axis=0)
    stats = stats + pltpu.roll(stats, 112, 1) + pltpu.roll(stats, 96, 1)
    average = jnp.sum(stats, axis=0, keepdims=True) * (1.0 / 16)
    offset = stats - average
    spread_sum = 128.0 * jnp.sum(offset * offset, axis=0, keepdims=True)
    square_sum = pltpu.roll(jnp.sum(stats, axis=0, keepdims=True), 80, 1)
    rstd = lax.rsqrt((square_sum + spread_sum) * (1.0 / D) + EPSILON)
    upper = iota((8, 128), 0) < 4
    sums = [0.0] * 5
    for z in range(16):
        tail = tails[z]
        move = offset[z : z + 1]
        every = column_of(move, 0, 16, (16, 128))
        mine = column_of(move, first, 4, (8, 128))
        for j in range(2):
            part = got_ref[z, 16 * j : 16 * j + 16].astype(F32)
            sums[j] = sums[j] + part + every * tail[j : j + 1]
            part = got_ref[z, 32 + 8 * j : 40 + 8 * j].astype(F32)
            column = jnp.where(upper, tail[2 + 2 * j : 3 + 2 * j], tail[3 + 2 * j : 4 + 2 * j])
            sums[2 + j] = sums[2 + j] + part + mine * column
        sums[4] = sums[4] + tail[8:] + mine * tail[12:13]
    every = column_of(rstd, 0, 16, (16, 128))
    mine = column_of(rstd, first, 4, (8, 128))
    own_scratch[:4] = first_ref[pl.ds(first, 4), :]
    own_scratch[4:] = first_ref[pl.ds(first, 4), :]
    queries = [rope(every * sums[j], first_ref[...]) for j in range(2)]
    keys = rope(mine * sums[2], own_scratch[...])
    out_ref[...] = jnp.concatenate(queries + [keys, mine * sums[3]], axis=0).astype(BF16)
    act_ref[...] = gelu(mine * sums[4])


def finish(meta, got, first):
    return call(
        finish_kernel,
        "finish",
        (near_out((48, 128), BF16), near_out((8, 128), F32)),
        [pltpu.VMEM((8, 128), F32)],
        meta,
        got,
        first,
    )


def attend_kernel(layer, meta_ref, got_ref, cache_ref, *refs):
    pages_ref, out_ref, kv = refs[-3:]
    tiles = []
    for tile in range(4):
        start = 48 * (tile // 2)
        rows = start + 16 * (tile % 2)
        tiles.append(got_ref[rows : rows + 16].astype(F32))
        new = got_ref[start + 32 : start + 48].astype(F32)
        for side in range(2):
            rows = 8 * side + 4 * (tile % 2)
            kv[side, :, 128 * tile : 128 * tile + 128] = new[rows : rows + 4]
    queries = jnp.concatenate(tiles, axis=1)
    queries = [queries[i : i + 1] for i in range(16)]
    spot = iota((PAGE, 512), 0)
    for side in range(2):
        for page in range(8):
            home = jnp.clip(meta_ref[0, page] - meta_ref[4, 0] * 4, 0, 3)
            place = jnp.where(meta_ref[3, page] == 1, meta_ref[2, page], -1)
            fresh = kv[side, pl.ds(home, 1), :]
            old = cache_ref[layer, side, page].astype(F32)
            pages_ref[layer, side, page] = jnp.where(spot == place, fresh, old).astype(BF16)
    head_of = iota((8, 512), 1) // HD == iota((8, 512), 0)
    wide = jnp.concatenate(
        [jnp.where(head_of, jnp.broadcast_to(row, (8, 512)), 0.0) for row in queries], axis=0
    ).astype(BF16)
    keys = pages_ref[layer, 0].reshape(8 * PAGE, 512)
    values = pages_ref[layer, 1].reshape(8 * PAGE, 512)
    scores = dot_t(wide, keys) * HD ** (-0.5)
    page_of = iota((1, 256), 1) // PAGE
    owner = jnp.zeros((1, 256), jnp.int32)
    limit = jnp.zeros((1, 256), jnp.int32)
    for page in range(8):
        length = jnp.where(meta_ref[1, page] == 1, meta_ref[2, page] + meta_ref[3, page], 0)
        owner = jnp.where(page_of == page, meta_ref[0, page], owner)
        limit = jnp.where(page_of == page, length, limit)
    owner = jnp.where(iota((1, 256), 1) % PAGE < limit, owner, -1)
    allowed = iota((128, 256), 0) // 8 == owner
    scores = jnp.where(allowed, scores, LOWEST)
    high = jnp.max(scores, axis=1, keepdims=True)
    weights = jnp.where(allowed, jnp.exp(scores - high), 0.0)
    total = jnp.sum(weights, axis=1, keepdims=True)
    mixed = dot32(weights.astype(BF16), values)
    head = iota((128, 128), 0) % 8
    lane = iota((128, 128), 1)
    picked = mixed[:, :128]
    for k in range(1, 4):
        picked = jnp.where(head // 2 == k, mixed[:, 128 * k : 128 * k + 128], picked)
    picked = jnp.where(head % 2 == 1, pltpu.roll(picked, HD, 1), picked)
    out_ref[...] = jnp.where(
        lane < HD, picked, jnp.where(lane == HD, total, jnp.where(lane == HD + 1, high, 0.0))
    )


def attend(layer, meta, got, caches, *pages):
    return call(
        functools.partial(attend_kernel, layer),
        "attend",
        (near_out(caches.shape, BF16), near_out((128, 128), F32)),
        [pltpu.VMEM((2, 4, 512), F32)],
        meta,
        got,
        caches,
        *pages,
        aliases={3: 0} if pages else {},
    )


def join_kernel(meta_ref, got_ref, act_ref, out_ref, wire):
    got = got_ref[...]
    high = got[:, :, HD + 1 : HD + 2]
    top = jnp.max(high, axis=0)
    total = jnp.sum(got * jnp.exp(high - top[None]), axis=0)
    lane = iota((16, 128), 1)
    out = jnp.where(lane < HD, total, 0.0)
    extra = parts_of(total[:, HD : HD + 1], 3) + parts_of(top, 3)
    for k, part in enumerate(extra):
        out = jnp.where(lane == HD + k, part, out)
    even = jnp.full((2, 128), (meta_ref[4, 1] // 2) % 2) == 0
    act = jnp.where(even, act_ref[0:2], act_ref[2:4])
    for z in range(16):
        wire[JOIN * z : JOIN * z + 16] = out
        wire[JOIN * z + 16 : JOIN * z + 18] = act
    out_ref[...] = wire[...].astype(BF16)


def join(meta, got, act):
    return call(
        join_kernel,
        "join",
        near_out((16 * JOIN, 128), BF16),
        [pltpu.VMEM((16 * JOIN, 128), F32)],
        meta,
        got,
        act,
    )


def settle_kernel(meta_ref, got_ref, out_ref, wire, back):
    wire[...] = got_ref[...].astype(F32)
    parts = [wire[JOIN * z : JOIN * z + 16] for z in range(16)]
    take = lambda part, k: part[:, HD + k : HD + k + 1]
    highs = [take(part, 3) + take(part, 4) + take(part, 5) for part in parts]
    top = functools.reduce(jnp.maximum, highs)
    total, mixed = 0.0, 0.0
    for part, high in zip(parts, highs):
        factor = jnp.exp(high - top)
        total = total + (take(part, 0) + take(part, 1) + take(part, 2)) * factor
        mixed = mixed + part * factor
    back[:16] = jnp.where(iota((16, 128), 1) < HD, mixed / total, 0.0)
    for k in range(2):
        back[pl.ds(16 + k, 16, stride=2), :] = wire[pl.ds(16 + k, 16, stride=JOIN), :]
    out_ref[...] = back[...].astype(BF16)


def settle(meta, got):
    return call(
        settle_kernel,
        "settle",
        near_out((48, 128), BF16),
        [pltpu.VMEM((16 * JOIN, 128), F32), pltpu.VMEM((48, 128), F32)],
        meta,
        got,
    )


def output_kernel(layer, copies, meta_ref, got_ref, wo_ref, wf_ref, out_ref):
    att = jnp.concatenate([got_ref[:16], got_ref[48:64]], axis=0).astype(F32)
    att = att + pltpu.roll(att, HD, 1)
    att = jnp.concatenate([att] * 4, axis=1)
    own = iota((32, 512), 1) // HD == iota((32, 512), 0) % 8
    by_head = dot_t(jnp.where(own, att, 0.0).astype(BF16), wo_ref[layer])
    tiles = []
    for core in range(2):
        act = got_ref[48 * core + 16 : 48 * core + 48].astype(F32)
        tiles += [act[4 * m : 4 * m + 4] for m in range(8)]
    mlp = dot_t(jnp.concatenate(tiles, axis=1).astype(BF16), wf_ref[layer])
    rows = [
        jnp.sum(by_head[8 * i : 8 * i + 8], axis=0, keepdims=True) + mlp[i : i + 1]
        for i in range(4)
    ]
    tile = jnp.concatenate(rows, axis=0)
    tile = jnp.concatenate([tile, jnp.zeros_like(tile)], axis=1)
    for k in range(copies):
        out_ref[4 * k : 4 * k + 4] = tile


def output(layer, copies, meta, got, w_out, w_fc2):
    return call(
        functools.partial(output_kernel, layer, copies),
        "output",
        near_out((4 * copies, 128), F32),
        [],
        meta,
        got,
        w_out,
        w_fc2,
    )


def per_device(
    hidden,
    ln_gain,
    w_qkv,
    w_fc1,
    w_out,
    w_fc2,
    caches,
    page_owner,
    page_used,
    page_fill,
    page_tail,
    positions,
):
    rep = lax.axis_index("rep")
    blk = lax.axis_index("blk")
    zs = [[2 * z + c for z in range(16)] for c in range(2)]
    pairs = [[2 * z, 2 * z + 1] for z in range(16)]
    rep_core = [[r * 32 + 2 * z + c for r in range(4) for c in range(2)] for z in range(16)]

    first = jnp.concatenate([hidden.astype(F32), rope_factors(positions)], axis=1)
    first = spread(first, 4, "rep").reshape(16, 128)
    place = jnp.where(jnp.arange(8) == 0, rep, blk).astype(jnp.int32)
    meta = jnp.stack([page_owner, page_used, page_fill, page_tail, place])
    w_qkv = w_qkv.transpose(0, 2, 1, 3)
    w_out = w_out.transpose(0, 2, 1)
    w_fc2 = w_fc2.transpose(0, 2, 1)

    state, branch, pages = first, (), ()
    for layer in range(LAYERS):
        parts, state = project(layer, meta, state, ln_gain, w_qkv, w_fc1, *branch)
        parts = lax.all_gather(parts, "blk", axis_index_groups=pairs)
        got = exchange(pool(meta, parts), "blk", zs)
        packed, act = finish(meta, got, first)
        got = lax.all_gather(packed, "blk", axis_index_groups=pairs, tiled=True)
        fresh, parts = attend(layer, meta, got, caches, *pages)
        pages = (fresh,)
        parts = exchange(parts.reshape(8, 16, 128), ("rep", "blk"), rep_core)
        got = exchange(join(meta, parts, act).reshape(16, JOIN // 2, 2, 128), "blk", zs)
        got = settle(meta, got.reshape(16 * JOIN, 128))
        got = lax.all_gather(got, "blk", axis_index_groups=pairs, tiled=True)
        if layer + 1 < LAYERS:
            out = output(layer, 16, meta, got, w_out, w_fc2).reshape(16, 4, 128)
            branch = (exchange(out, ("rep", "tp")).reshape(64, 128),)
    out = output(layer, 4, meta, got, w_out, w_fc2).reshape(4, 4, 128)
    total = jnp.sum(exchange(out, "tp"), axis=0)[:, :HD]
    own = lax.dynamic_slice(state, (rep * 4, 0), (4, HD))
    return ((own + total).astype(BF16), fresh)


def solution(mesh):
    in_specs = (
        P("rep", "blk"),
        P(None, "blk"),
        P(None, "blk", None, "tp"),
        P(None, "blk", "tp"),
        P(None, "tp", "blk"),
        P(None, "tp", "blk"),
        P(None, None, ("rep", "blk"), None, "tp"),
        P(("rep", "blk")),
        P(("rep", "blk")),
        P(("rep", "blk")),
        P(("rep", "blk")),
        P("rep"),
    )
    out_specs = (P("rep", "blk"), P(None, None, ("rep", "blk"), None, "tp"))
    return jax.shard_map(
        per_device, mesh=mesh, in_specs=in_specs, out_specs=out_specs, check_vma=False
    )
```

```python
import functools
import math

import jax
import jax.numpy as jnp
from jax import lax
from jax.experimental import pallas as pl
from jax.experimental.pallas import tpu as pltpu
from jax.sharding import PartitionSpec as P

D = 2048
HD = 64
ROT = 32
LAYERS = 2
PAGE = 32
EPSILON = 1e-05
LOWEST = -1e30
F32 = jnp.float32
BF16 = jnp.bfloat16
INTERPRET = False
HALF = 232
FLOW = 34
JOIN = 18


def exchange(value, axis, groups=None):
    return lax.all_to_all(value, axis, 0, 0, tiled=True, axis_index_groups=groups)


def rope_factors(positions):
    lane = jnp.arange(64, dtype=jnp.int32)
    steps_f = (lane % (ROT // 2)).astype(F32)
    angles = positions.astype(F32)[:, None] * (10000.0 ** (-2.0 * steps_f / ROT))[None, :]
    sine = jnp.sin(angles)
    return jnp.where(lane < 32, jnp.cos(angles), jnp.where(lane < 48, -sine, sine))


def near(value):
    return value if INTERPRET else pltpu.with_memory_space_constraint(value, pltpu.VMEM)


def near_out(shape, dtype):
    return jax.ShapeDtypeStruct(shape, dtype) if INTERPRET else pltpu.VMEM(shape, dtype)


def iota(shape, axis):
    return lax.broadcasted_iota(jnp.int32, shape, axis)


def dot32(left, right):
    return jnp.dot(left, right, preferred_element_type=F32)


def dot_t(left, right):
    return lax.dot_general(left, right, (((1,), (1,)), ((), ())), preferred_element_type=F32)


def parts_of(value, count):
    found = []
    for _ in range(count):
        part = value.astype(BF16).astype(F32)
        found.append(part)
        value = value - part
    return found


def rope(value, factors):
    lane = iota(value.shape, 1)
    left = lane < HD
    half = ROT // 2
    cosine = jnp.where(left, pltpu.roll(factors, 64, 1), factors)
    sine = jnp.where(left, pltpu.roll(factors, 32, 1), pltpu.roll(factors, 96, 1))
    other = jnp.where(
        lane % HD < half, pltpu.roll(value, 128 - half, 1), pltpu.roll(value, half, 1)
    )
    return jnp.where(lane % HD < ROT, value * cosine + other * sine, value)


def gelu(value):
    cubed = value * value * value
    return 0.5 * value * (1.0 + jnp.tanh(math.sqrt(2.0 / math.pi) * (value + 0.044715 * cubed)))


def column_of(row, first, period, shape):
    mine = iota(shape, 1) == first + iota(shape, 0) % period
    return jnp.sum(jnp.where(mine, row, 0.0), axis=1, keepdims=True)


def project_kernel(layer, meta_ref, x_ref, gain_ref, wq_ref, wf_ref, *refs):
    out_ref, state_ref = refs[-2:]
    if layer == 0:
        x = x_ref[...].astype(F32)
    else:
        branch_ref = refs[0]
        x = x_ref[...] + branch_ref[0:4] + branch_ref[4:8] + branch_ref[8:12] + branch_ref[12:16]
        x = x.astype(BF16).astype(F32)[:, :HD]
    state_ref[...] = jnp.concatenate([x, jnp.zeros_like(x)], axis=1)
    gain = gain_ref[layer : layer + 1]
    mean = jnp.sum(x, axis=1, keepdims=True) * (1.0 / HD)
    centered = x - mean
    square = jnp.sum(centered * centered, axis=1, keepdims=True)
    rows = jnp.concatenate([centered * gain, jnp.broadcast_to(gain, (4, HD))], axis=0)
    high, low = parts_of(rows, 2)
    high, low = high.astype(BF16), low.astype(BF16)
    for k in range(3):
        every = dot32(high, wq_ref[layer, k]) + dot32(low, wq_ref[layer, k])
        for j in range(4):
            start = 8 * (4 * k + j)
            out_ref[start : start + 8] = every[:, 128 * j : 128 * j + 128]
    every = dot32(high, wf_ref[layer]) + dot32(low, wf_ref[layer])
    for j in range(16):
        out_ref[96 + 8 * j : 104 + 8 * j] = every[:, 128 * j : 128 * j + 128]
    lane = iota((4, 128), 1)
    request = iota((4, 128), 0)
    stats = jnp.where(lane == request, mean, jnp.where(lane == request + 16, square, 0.0))
    out_ref[224:232] = jnp.broadcast_to(jnp.sum(stats, axis=0, keepdims=True), (8, 128))


def call(kernel, name, outs, scratch, meta, *args, aliases=None):
    specs = [pl.BlockSpec(memory_space=pltpu.SMEM)]
    specs += [pl.BlockSpec(memory_space=pltpu.VMEM) for _ in args]
    place = pl.BlockSpec(memory_space=pltpu.VMEM)
    return pl.pallas_call(
        kernel,
        in_specs=specs,
        out_specs=jax.tree.map(lambda _: place, outs, is_leaf=lambda x: hasattr(x, "shape")),
        out_shape=outs,
        scratch_shapes=scratch,
        input_output_aliases=aliases or {},
        compiler_params=pltpu.CompilerParams(vmem_limit_bytes=24 * 2**20),
        name=name,
        interpret=INTERPRET,
    )(meta, *[near(arg) for arg in args])


def project(layer, meta, x, gain, wq, wf, *branch):
    return call(
        functools.partial(project_kernel, layer),
        "project",
        (near_out((HALF, 128), F32), near_out((4, 128), F32)),
        [],
        meta,
        x,
        gain,
        wq,
        wf,
        *branch,
    )


def pool_kernel(meta_ref, got_ref, out_ref, wire):
    core = meta_ref[4, 1] % 2
    means = [got_ref[s, 224:225] for s in range(2)]
    center = 0.5 * (means[0] + means[1])
    moves = [mean - center for mean in means]
    square = pltpu.roll(means[0] + means[1], 112, 1) + 64.0 * (
        moves[0] * moves[0] + moves[1] * moves[1]
    )
    upper = iota((8, 1), 0) < 4
    shift = [jnp.where(upper, column_of(move, 0, 4, (8, 128)), 0.0) for move in moves]

    def block(start):
        total = 0.0
        for s in range(2):
            part = got_ref[s, pl.ds(pl.multiple_of(start, 8), 8), :]
            total = total + part + shift[s] * part[4:5]
        return total

    common = []
    columns = []
    for base in (0, 32, 64):
        one = block(base + 16 * core)
        two = block(base + 16 * core + 8)
        common.append(jnp.where(upper, one, pltpu.roll(two, 4, 0)))
        columns += [one[4:5], two[4:5]]
    lane = iota((4, 128), 1)
    request = iota((4, 128), 0)
    stats = jnp.zeros((4, 128), F32)
    both = parts_of(column_of(center, 0, 4, (4, 128)), 3)
    both += parts_of(column_of(square, 0, 4, (4, 128)), 3)
    for k, part in enumerate(both):
        stats = jnp.where(lane == request + 16 * k, part, stats)
    columns.append(jnp.sum(stats, axis=0, keepdims=True))
    row = iota((8, 128), 0)
    tail = jnp.zeros((8, 128), F32)
    for k, column in enumerate(columns):
        tail = jnp.where(row == k, column, tail)
    shared = jnp.concatenate(common, axis=0)
    for m in range(8):
        last = block(96 + 64 * core + 8 * m)
        whole = jnp.concatenate([shared, jnp.where(row == 7, last[4:5], tail)], axis=0)
        for k in range(2):
            start = FLOW * (2 * m + k)
            wire[start : start + 32] = whole
            wire[start + 32 : start + 34] = last[2 * k : 2 * k + 2]
    out_ref[...] = wire[...].astype(BF16)


def pool(meta, got):
    return call(
        pool_kernel,
        "pool",
        near_out((16 * FLOW, 128), BF16),
        [pltpu.VMEM((16 * FLOW, 128), F32)],
        meta,
        got,
    )


def finish_kernel(meta_ref, got_ref, factor_ref, out_ref, act_ref, wire):
    wire[...] = got_ref[...].astype(F32)
    stats = wire[pl.ds(30, 16, stride=FLOW), :]
    stats = stats + pltpu.roll(stats, 112, 1) + pltpu.roll(stats, 96, 1)
    average = jnp.sum(stats, axis=0, keepdims=True) * (1.0 / 16)
    offset = stats - average
    spread_sum = 128.0 * jnp.sum(offset * offset, axis=0, keepdims=True)
    square_sum = pltpu.roll(jnp.sum(stats, axis=0, keepdims=True), 80, 1)
    rstd = lax.rsqrt((square_sum + spread_sum) * (1.0 / D) + EPSILON)
    upper = iota((8, 128), 0) < 4
    pair = 2 * ((meta_ref[4, 1] // 2) % 2)
    sums = [0.0] * 4
    for z in range(16):
        base = FLOW * z
        move = offset[z : z + 1]
        mine = column_of(move, 0, 4, (8, 128))
        tail = wire[base + 24 : base + 32]
        for k in range(3):
            part = wire[base + 8 * k : base + 8 * k + 8]
            column = jnp.where(upper, tail[2 * k : 2 * k + 1], tail[2 * k + 1 : 2 * k + 2])
            sums[k] = sums[k] + part + mine * column
        part = wire[base + 32 : base + 34]
        sums[3] = sums[3] + part + column_of(move, pair, 2, (2, 128)) * tail[7:8]
    mine = column_of(rstd, 0, 4, (8, 128))
    factors = jnp.concatenate([factor_ref[...], factor_ref[...]], axis=0)
    packed = [rope(mine * sums[k], factors) for k in range(2)] + [mine * sums[2]]
    packed = jnp.concatenate(packed, axis=0).astype(BF16)
    for k in range(8):
        out_ref[k] = packed
    act_ref[...] = gelu(column_of(rstd, pair, 2, (2, 128)) * sums[3])


def finish(meta, got, factors):
    return call(
        finish_kernel,
        "finish",
        (near_out((8, 24, 128), BF16), near_out((2, 128), F32)),
        [pltpu.VMEM((16 * FLOW, 128), F32)],
        meta,
        got,
        factors,
    )


def attend_kernel(layer, meta_ref, got_ref, cache_ref, *refs):
    pages_ref, out_ref, kv = refs[-3:]
    tiles = []
    for tile in range(4):
        core, rows = tile // 2, 4 * (tile % 2)
        parts = [got_ref[2 * r + core, :8].astype(F32)[rows : rows + 4] for r in range(4)]
        tiles.append(jnp.concatenate(parts, axis=0))
        new = got_ref[2 * meta_ref[4, 0] + core].astype(F32)
        for side in range(2):
            start = 8 + 8 * side + rows
            kv[side, :, 128 * tile : 128 * tile + 128] = new[start : start + 4]
    queries = jnp.concatenate(tiles, axis=1)
    queries = [queries[i : i + 1] for i in range(16)]
    spot = iota((PAGE, 512), 0)
    for side in range(2):
        for page in range(8):
            home = jnp.clip(meta_ref[0, page] - meta_ref[4, 0] * 4, 0, 3)
            place = jnp.where(meta_ref[3, page] == 1, meta_ref[2, page], -1)
            fresh = kv[side, pl.ds(home, 1), :]
            old = cache_ref[layer, side, page].astype(F32)
            pages_ref[layer, side, page] = jnp.where(spot == place, fresh, old).astype(BF16)
    head_of = iota((8, 512), 1) // HD == iota((8, 512), 0)
    wide = jnp.concatenate(
        [jnp.where(head_of, jnp.broadcast_to(row, (8, 512)), 0.0) for row in queries], axis=0
    ).astype(BF16)
    keys = pages_ref[layer, 0].reshape(8 * PAGE, 512)
    values = pages_ref[layer, 1].reshape(8 * PAGE, 512)
    scores = dot_t(wide, keys) * HD ** (-0.5)
    page_of = iota((1, 256), 1) // PAGE
    owner = jnp.zeros((1, 256), jnp.int32)
    limit = jnp.zeros((1, 256), jnp.int32)
    for page in range(8):
        length = jnp.where(meta_ref[1, page] == 1, meta_ref[2, page] + meta_ref[3, page], 0)
        owner = jnp.where(page_of == page, meta_ref[0, page], owner)
        limit = jnp.where(page_of == page, length, limit)
    owner = jnp.where(iota((1, 256), 1) % PAGE < limit, owner, -1)
    allowed = iota((128, 256), 0) // 8 == owner
    scores = jnp.where(allowed, scores, LOWEST)
    high = jnp.max(scores, axis=1, keepdims=True)
    weights = jnp.where(allowed, jnp.exp(scores - high), 0.0)
    total = jnp.sum(weights, axis=1, keepdims=True)
    mixed = dot32(weights.astype(BF16), values)
    head = iota((128, 128), 0) % 8
    lane = iota((128, 128), 1)
    picked = mixed[:, :128]
    for k in range(1, 4):
        picked = jnp.where(head // 2 == k, mixed[:, 128 * k : 128 * k + 128], picked)
    picked = jnp.where(head % 2 == 1, pltpu.roll(picked, HD, 1), picked)
    out_ref[...] = jnp.where(
        lane < HD, picked, jnp.where(lane == HD, total, jnp.where(lane == HD + 1, high, 0.0))
    )


def attend(layer, meta, got, caches, *pages):
    return call(
        functools.partial(attend_kernel, layer),
        "attend",
        (near_out(caches.shape, BF16), near_out((128, 128), F32)),
        [pltpu.VMEM((2, 4, 512), F32)],
        meta,
        got,
        caches,
        *pages,
        aliases={3: 0} if pages else {},
    )


def join_kernel(meta_ref, got_ref, act_ref, out_ref, wire):
    got = got_ref[...]
    high = got[:, :, HD + 1 : HD + 2]
    top = jnp.max(high, axis=0)
    total = jnp.sum(got * jnp.exp(high - top[None]), axis=0)
    lane = iota((16, 128), 1)
    out = jnp.where(lane < HD, total, 0.0)
    extra = parts_of(total[:, HD : HD + 1], 3) + parts_of(top, 3)
    for k, part in enumerate(extra):
        out = jnp.where(lane == HD + k, part, out)
    act = act_ref[...]
    for z in range(16):
        wire[JOIN * z : JOIN * z + 16] = out
        wire[JOIN * z + 16 : JOIN * z + 18] = act
    out_ref[...] = wire[...].astype(BF16)


def join(meta, got, act):
    return call(
        join_kernel,
        "join",
        near_out((16 * JOIN, 128), BF16),
        [pltpu.VMEM((16 * JOIN, 128), F32)],
        meta,
        got,
        act,
    )


def settle_kernel(meta_ref, got_ref, out_ref, wire, back):
    wire[...] = got_ref[...].astype(F32)
    parts = [wire[JOIN * z : JOIN * z + 16] for z in range(16)]
    take = lambda part, k: part[:, HD + k : HD + k + 1]
    highs = [take(part, 3) + take(part, 4) + take(part, 5) for part in parts]
    top = functools.reduce(jnp.maximum, highs)
    total, mixed = 0.0, 0.0
    for part, high in zip(parts, highs):
        factor = jnp.exp(high - top)
        total = total + (take(part, 0) + take(part, 1) + take(part, 2)) * factor
        mixed = mixed + part * factor
    back[:16] = jnp.where(iota((16, 128), 1) < HD, mixed / total, 0.0)
    for k in range(2):
        back[pl.ds(16 + k, 16, stride=2), :] = wire[pl.ds(16 + k, 16, stride=JOIN), :]
    out_ref[...] = back[...].astype(BF16)


def settle(meta, got):
    return call(
        settle_kernel,
        "settle",
        near_out((48, 128), BF16),
        [pltpu.VMEM((16 * JOIN, 128), F32), pltpu.VMEM((48, 128), F32)],
        meta,
        got,
    )


def output_kernel(layer, meta_ref, got_ref, wo_ref, wf_ref, out_ref):
    att = jnp.concatenate([got_ref[:16], got_ref[48:64]], axis=0).astype(F32)
    att = att + pltpu.roll(att, HD, 1)
    att = jnp.concatenate([att] * 4, axis=1)
    own = iota((32, 512), 1) // HD == iota((32, 512), 0) % 8
    by_head = dot_t(jnp.where(own, att, 0.0).astype(BF16), wo_ref[layer])
    tiles = []
    for core in range(2):
        act = got_ref[48 * core + 16 : 48 * core + 48].astype(F32)
        tiles += [act[4 * m : 4 * m + 4] for m in range(8)]
    mlp = dot_t(jnp.concatenate(tiles, axis=1).astype(BF16), wf_ref[layer])
    rows = [
        jnp.sum(by_head[8 * i : 8 * i + 8], axis=0, keepdims=True) + mlp[i : i + 1]
        for i in range(4)
    ]
    tile = jnp.concatenate(rows, axis=0)
    tile = jnp.concatenate([tile, jnp.zeros_like(tile)], axis=1)
    for k in range(4):
        out_ref[4 * k : 4 * k + 4] = tile


def output(layer, meta, got, w_out, w_fc2):
    return call(
        functools.partial(output_kernel, layer),
        "output",
        near_out((16, 128), F32),
        [],
        meta,
        got,
        w_out,
        w_fc2,
    )


def per_device(
    hidden,
    ln_gain,
    w_qkv,
    w_fc1,
    w_out,
    w_fc2,
    caches,
    page_owner,
    page_used,
    page_fill,
    page_tail,
    positions,
):
    rep = lax.axis_index("rep")
    blk = lax.axis_index("blk")
    zs = [[2 * z + c for z in range(16)] for c in range(2)]
    pairs = [[2 * z, 2 * z + 1] for z in range(16)]
    rep_core = [[r * 32 + 2 * z + c for r in range(4) for c in range(2)] for z in range(16)]

    factors = rope_factors(positions)
    factors = jnp.concatenate([factors, factors], axis=1)
    place = jnp.where(jnp.arange(8) == 0, rep, blk).astype(jnp.int32)
    meta = jnp.stack([page_owner, page_used, page_fill, page_tail, place])
    w_qkv = w_qkv.transpose(0, 2, 1, 3)
    w_out = w_out.transpose(0, 2, 1)
    w_fc2 = w_fc2.transpose(0, 2, 1)

    state, branch, pages = hidden, (), ()
    for layer in range(LAYERS):
        parts, state = project(layer, meta, state, ln_gain, w_qkv, w_fc1, *branch)
        parts = lax.all_gather(parts, "blk", axis_index_groups=pairs)
        got = exchange(pool(meta, parts).reshape(16, FLOW // 2, 2, 128), "blk", zs)
        packed, act = finish(meta, got.reshape(16 * FLOW, 128), factors)
        got = exchange(packed, ("rep", "blk"), rep_core)
        fresh, parts = attend(layer, meta, got, caches, *pages)
        pages = (fresh,)
        parts = exchange(parts.reshape(8, 16, 128), ("rep", "blk"), rep_core)
        got = exchange(join(meta, parts, act).reshape(16, JOIN // 2, 2, 128), "blk", zs)
        got = settle(meta, got.reshape(16 * JOIN, 128))
        got = lax.all_gather(got, "blk", axis_index_groups=pairs, tiled=True)
        out = output(layer, meta, got, w_out, w_fc2).reshape(4, 4, 128)
        out = exchange(out, "tp")
        branch = (out.reshape(16, 128),)
    result = (state[:, :HD] + jnp.sum(out, axis=0)[:, :HD]).astype(BF16)
    return (result, fresh)


def solution(mesh):
    in_specs = (
        P("rep", "blk"),
        P(None, "blk"),
        P(None, "blk", None, "tp"),
        P(None, "blk", "tp"),
        P(None, "tp", "blk"),
        P(None, "tp", "blk"),
        P(None, None, ("rep", "blk"), None, "tp"),
        P(("rep", "blk")),
        P(("rep", "blk")),
        P(("rep", "blk")),
        P(("rep", "blk")),
        P("rep"),
    )
    out_specs = (P("rep", "blk"), P(None, None, ("rep", "blk"), None, "tp"))
    return jax.shard_map(
        per_device, mesh=mesh, in_specs=in_specs, out_specs=out_specs, check_vma=False
    )
```

```python
import functools
import math

import jax
import jax.numpy as jnp
from jax import lax
from jax.experimental import pallas as pl
from jax.experimental.pallas import tpu as pltpu
from jax.sharding import PartitionSpec as P

D = 2048
HD = 64
ROT = 32
LAYERS = 2
PAGE = 32
EPSILON = 1e-05
LOWEST = -1e30
F32 = jnp.float32
BF16 = jnp.bfloat16
INTERPRET = False
HALF = 232
FLOW = 34
JOIN = 18


def exchange(value, axis, groups=None):
    return lax.all_to_all(value, axis, 0, 0, tiled=True, axis_index_groups=groups)


def rope_factors(positions):
    lane = jnp.arange(64, dtype=jnp.int32)
    steps_f = (lane % (ROT // 2)).astype(F32)
    angles = positions.astype(F32)[:, None] * (10000.0 ** (-2.0 * steps_f / ROT))[None, :]
    sine = jnp.sin(angles)
    return jnp.where(lane < 32, jnp.cos(angles), jnp.where(lane < 48, -sine, sine))


def near(value):
    return value if INTERPRET else pltpu.with_memory_space_constraint(value, pltpu.VMEM)


def away(value):
    return value if INTERPRET else pltpu.with_memory_space_constraint(value, pltpu.HBM)


def near_out(shape, dtype):
    return jax.ShapeDtypeStruct(shape, dtype) if INTERPRET else pltpu.VMEM(shape, dtype)


def iota(shape, axis):
    return lax.broadcasted_iota(jnp.int32, shape, axis)


def dot32(left, right):
    return jnp.dot(left, right, preferred_element_type=F32)


def dot_t(left, right):
    return lax.dot_general(left, right, (((1,), (1,)), ((), ())), preferred_element_type=F32)


def parts_of(value, count):
    found = []
    for _ in range(count):
        part = value.astype(BF16).astype(F32)
        found.append(part)
        value = value - part
    return found


def rope(value, factors):
    lane = iota(value.shape, 1)
    left = lane < HD
    half = ROT // 2
    cosine = jnp.where(left, pltpu.roll(factors, 64, 1), factors)
    sine = jnp.where(left, pltpu.roll(factors, 32, 1), pltpu.roll(factors, 96, 1))
    other = jnp.where(
        lane % HD < half, pltpu.roll(value, 128 - half, 1), pltpu.roll(value, half, 1)
    )
    return jnp.where(lane % HD < ROT, value * cosine + other * sine, value)


def gelu(value):
    cubed = value * value * value
    return 0.5 * value * (1.0 + jnp.tanh(math.sqrt(2.0 / math.pi) * (value + 0.044715 * cubed)))


def column_of(row, first, period, shape):
    mine = iota(shape, 1) == first + iota(shape, 0) % period
    return jnp.sum(jnp.where(mine, row, 0.0), axis=1, keepdims=True)


def project_kernel(layer, x_ref, gain_ref, wq_ref, wf_ref, *refs):
    if layer == 0:
        out_ref, state_ref, q_held, f_held, x_held, gain_held, sems = refs
        copies = [
            pltpu.make_async_copy(x_ref, x_held, sems.at[0]),
            pltpu.make_async_copy(gain_ref, gain_held, sems.at[1]),
            pltpu.make_async_copy(wq_ref.at[0], q_held, sems.at[2]),
            pltpu.make_async_copy(wf_ref.at[0], f_held, sems.at[3]),
        ]
        for copy in copies:
            copy.start()
        copies[0].wait()
        copies[1].wait()
        x = x_held[...].astype(F32)
        gain_ref = gain_held
    else:
        branch_ref, out_ref, state_ref = refs
        x = x_ref[...] + branch_ref[0:4] + branch_ref[4:8] + branch_ref[8:12] + branch_ref[12:16]
        x = x.astype(BF16).astype(F32)[:, :HD]
    state_ref[...] = jnp.concatenate([x, jnp.zeros_like(x)], axis=1)
    gain = gain_ref[layer : layer + 1]
    mean = jnp.sum(x, axis=1, keepdims=True) * (1.0 / HD)
    centered = x - mean
    square = jnp.sum(centered * centered, axis=1, keepdims=True)
    rows = jnp.concatenate([centered * gain, jnp.broadcast_to(gain, (4, HD))], axis=0)
    high, low = parts_of(rows, 2)
    high, low = high.astype(BF16), low.astype(BF16)
    if layer == 0:
        copies[2].wait()
    for k in range(3):
        weights = q_held[k] if layer == 0 else wq_ref[layer, k]
        every = dot32(high, weights) + dot32(low, weights)
        for j in range(4):
            start = 8 * (4 * k + j)
            out_ref[start : start + 8] = every[:, 128 * j : 128 * j + 128]
    if layer == 0:
        copies[3].wait()
    weights = f_held[...] if layer == 0 else wf_ref[layer]
    every = dot32(high, weights) + dot32(low, weights)
    for j in range(16):
        out_ref[96 + 8 * j : 104 + 8 * j] = every[:, 128 * j : 128 * j + 128]
    lane = iota((4, 128), 1)
    request = iota((4, 128), 0)
    stats = jnp.where(lane == request, mean, jnp.where(lane == request + 16, square, 0.0))
    out_ref[224:232] = jnp.broadcast_to(jnp.sum(stats, axis=0, keepdims=True), (8, 128))


def call(kernel, name, outs, scratch, tables, *args, far=(), far_outs=(), aliases=None):
    near_spec = pl.BlockSpec(memory_space=pltpu.VMEM)
    far_spec = pl.BlockSpec(memory_space=pl.ANY)
    specs = [pl.BlockSpec(memory_space=pltpu.SMEM) for _ in tables]
    specs += [far_spec if k in far else near_spec for k in range(len(args))]
    args = [away(arg) if k in far else near(arg) for k, arg in enumerate(args)]
    return pl.pallas_call(
        kernel,
        in_specs=specs,
        out_specs=tuple(far_spec if k in far_outs else near_spec for k in range(len(outs))),
        out_shape=tuple(outs),
        scratch_shapes=scratch,
        input_output_aliases=aliases or {},
        compiler_params=pltpu.CompilerParams(vmem_limit_bytes=24 * 2**20),
        name=name,
        interpret=INTERPRET,
    )(*tables, *args)


def project(layer, x, gain, wq, wf, *branch):
    scratch = [
        pltpu.VMEM(wq.shape[1:], BF16),
        pltpu.VMEM(wf.shape[1:], BF16),
        pltpu.VMEM(x.shape, x.dtype),
        pltpu.VMEM(gain.shape, F32),
        pltpu.SemaphoreType.DMA((4,)),
    ]
    return call(
        functools.partial(project_kernel, layer),
        "project",
        (near_out((HALF, 128), F32), near_out((4, 128), F32)),
        scratch if layer == 0 else [],
        (),
        x,
        gain,
        wq,
        wf,
        *branch,
        far=(0, 1, 2, 3) if layer == 0 else (),
    )


def pool_kernel(got_ref, out_ref, wire):
    core = lax.axis_index("blk") % 2
    means = [got_ref[s, 224:225] for s in range(2)]
    center = 0.5 * (means[0] + means[1])
    moves = [mean - center for mean in means]
    square = pltpu.roll(means[0] + means[1], 112, 1) + 64.0 * (
        moves[0] * moves[0] + moves[1] * moves[1]
    )
    upper = iota((8, 1), 0) < 4
    shift = [jnp.where(upper, column_of(move, 0, 4, (8, 128)), 0.0) for move in moves]

    def block(start):
        total = 0.0
        for s in range(2):
            part = got_ref[s, pl.ds(pl.multiple_of(start, 8), 8), :]
            total = total + part + shift[s] * part[4:5]
        return total

    common = []
    columns = []
    for base in (0, 32, 64):
        one = block(base + 16 * core)
        two = block(base + 16 * core + 8)
        common.append(jnp.where(upper, one, pltpu.roll(two, 4, 0)))
        columns += [one[4:5], two[4:5]]
    lane = iota((4, 128), 1)
    request = iota((4, 128), 0)
    stats = jnp.zeros((4, 128), F32)
    both = parts_of(column_of(center, 0, 4, (4, 128)), 3)
    both += parts_of(column_of(square, 0, 4, (4, 128)), 3)
    for k, part in enumerate(both):
        stats = jnp.where(lane == request + 16 * k, part, stats)
    columns.append(jnp.sum(stats, axis=0, keepdims=True))
    row = iota((8, 128), 0)
    tail = jnp.zeros((8, 128), F32)
    for k, column in enumerate(columns):
        tail = jnp.where(row == k, column, tail)
    shared = jnp.concatenate(common, axis=0)
    for m in range(8):
        last = block(96 + 64 * core + 8 * m)
        whole = jnp.concatenate([shared, jnp.where(row == 7, last[4:5], tail)], axis=0)
        for k in range(2):
            start = FLOW * (2 * m + k)
            wire[start : start + 32] = whole
            wire[start + 32 : start + 34] = last[2 * k : 2 * k + 2]
    out_ref[...] = wire[...].astype(BF16)


def pool(got):
    return call(
        pool_kernel,
        "pool",
        (near_out((16 * FLOW, 128), BF16),),
        [pltpu.VMEM((16 * FLOW, 128), F32)],
        (),
        got,
    )[0]


def finish_kernel(got_ref, factor_ref, out_ref, act_ref, wire):
    wire[...] = got_ref[...].astype(F32)
    stats = wire[pl.ds(30, 16, stride=FLOW), :]
    stats = stats + pltpu.roll(stats, 112, 1) + pltpu.roll(stats, 96, 1)
    average = jnp.sum(stats, axis=0, keepdims=True) * (1.0 / 16)
    offset = stats - average
    spread_sum = 128.0 * jnp.sum(offset * offset, axis=0, keepdims=True)
    square_sum = pltpu.roll(jnp.sum(stats, axis=0, keepdims=True), 80, 1)
    rstd = lax.rsqrt((square_sum + spread_sum) * (1.0 / D) + EPSILON)
    upper = iota((8, 128), 0) < 4
    pair = 2 * ((lax.axis_index("blk") // 2) % 2)
    sums = [0.0] * 4
    for z in range(16):
        base = FLOW * z
        move = offset[z : z + 1]
        mine = column_of(move, 0, 4, (8, 128))
        tail = wire[base + 24 : base + 32]
        for k in range(3):
            part = wire[base + 8 * k : base + 8 * k + 8]
            column = jnp.where(upper, tail[2 * k : 2 * k + 1], tail[2 * k + 1 : 2 * k + 2])
            sums[k] = sums[k] + part + mine * column
        part = wire[base + 32 : base + 34]
        sums[3] = sums[3] + part + column_of(move, pair, 2, (2, 128)) * tail[7:8]
    mine = column_of(rstd, 0, 4, (8, 128))
    factors = jnp.concatenate([factor_ref[...], factor_ref[...]], axis=0)
    packed = [rope(mine * sums[k], factors) for k in range(2)] + [mine * sums[2]]
    packed = jnp.concatenate(packed, axis=0).astype(BF16)
    for k in range(8):
        out_ref[k] = packed
    act_ref[...] = gelu(column_of(rstd, pair, 2, (2, 128)) * sums[3])


def finish(got, factors):
    return call(
        finish_kernel,
        "finish",
        (near_out((8, 24, 128), BF16), near_out((2, 128), F32)),
        [pltpu.VMEM((16 * FLOW, 128), F32)],
        (),
        got,
        factors,
    )


def attend_kernel(layer, meta_ref, got_ref, cache_ref, *refs):
    held, out_ref, kv = refs
    rep = lax.axis_index("rep")
    tiles = []
    for tile in range(4):
        core, rows = tile // 2, 4 * (tile % 2)
        parts = [got_ref[2 * r + core, :8].astype(F32)[rows : rows + 4] for r in range(4)]
        tiles.append(jnp.concatenate(parts, axis=0))
        new = got_ref[2 * rep + core].astype(F32)
        for side in range(2):
            start = 8 + 8 * side + rows
            kv[side, :, 128 * tile : 128 * tile + 128] = new[start : start + 4]
    queries = jnp.concatenate(tiles, axis=1)
    queries = [queries[i : i + 1] for i in range(16)]
    spot = iota((PAGE, 512), 0)
    for side in range(2):
        for page in range(8):
            home = jnp.clip(meta_ref[0, page] - rep * 4, 0, 3)
            place = jnp.where(meta_ref[3, page] == 1, meta_ref[2, page], -1)
            fresh = kv[side, pl.ds(home, 1), :]
            old = cache_ref[layer, side, page].astype(F32)
            held[side, page] = jnp.where(spot == place, fresh, old).astype(BF16)
    head_of = iota((8, 512), 1) // HD == iota((8, 512), 0)
    wide = jnp.concatenate(
        [jnp.where(head_of, jnp.broadcast_to(row, (8, 512)), 0.0) for row in queries], axis=0
    ).astype(BF16)
    keys = held[0].reshape(8 * PAGE, 512)
    values = held[1].reshape(8 * PAGE, 512)
    scores = dot_t(wide, keys) * HD ** (-0.5)
    page_of = iota((1, 256), 1) // PAGE
    owner = jnp.zeros((1, 256), jnp.int32)
    limit = jnp.zeros((1, 256), jnp.int32)
    for page in range(8):
        length = jnp.where(meta_ref[1, page] == 1, meta_ref[2, page] + meta_ref[3, page], 0)
        owner = jnp.where(page_of == page, meta_ref[0, page], owner)
        limit = jnp.where(page_of == page, length, limit)
    owner = jnp.where(iota((1, 256), 1) % PAGE < limit, owner, -1)
    allowed = iota((128, 256), 0) // 8 == owner
    scores = jnp.where(allowed, scores, LOWEST)
    high = jnp.max(scores, axis=1, keepdims=True)
    weights = jnp.where(allowed, jnp.exp(scores - high), 0.0)
    total = jnp.sum(weights, axis=1, keepdims=True)
    mixed = dot32(weights.astype(BF16), values)
    head = iota((128, 128), 0) % 8
    lane = iota((128, 128), 1)
    picked = mixed[:, :128]
    for k in range(1, 4):
        picked = jnp.where(head // 2 == k, mixed[:, 128 * k : 128 * k + 128], picked)
    picked = jnp.where(head % 2 == 1, pltpu.roll(picked, HD, 1), picked)
    out_ref[...] = jnp.where(
        lane < HD, picked, jnp.where(lane == HD, total, jnp.where(lane == HD + 1, high, 0.0))
    )


def attend(layer, meta, got, caches):
    return call(
        functools.partial(attend_kernel, layer),
        "attend",
        (near_out(caches.shape[1:], BF16), near_out((128, 128), F32)),
        [pltpu.VMEM((2, 4, 512), F32)],
        (meta,),
        got,
        caches,
    )


def join_kernel(got_ref, act_ref, out_ref, wire):
    got = got_ref[...]
    high = got[:, :, HD + 1 : HD + 2]
    top = jnp.max(high, axis=0)
    total = jnp.sum(got * jnp.exp(high - top[None]), axis=0)
    lane = iota((16, 128), 1)
    out = jnp.where(lane < HD, total, 0.0)
    extra = parts_of(total[:, HD : HD + 1], 3) + parts_of(top, 3)
    for k, part in enumerate(extra):
        out = jnp.where(lane == HD + k, part, out)
    act = act_ref[...]
    for z in range(16):
        wire[JOIN * z : JOIN * z + 16] = out
        wire[JOIN * z + 16 : JOIN * z + 18] = act
    out_ref[...] = wire[...].astype(BF16)


def join(got, act):
    return call(
        join_kernel,
        "join",
        (near_out((16 * JOIN, 128), BF16),),
        [pltpu.VMEM((16 * JOIN, 128), F32)],
        (),
        got,
        act,
    )[0]


def settle_kernel(layer, got_ref, held_ref, *refs):
    pages_ref, out_ref, wire, back, sem = refs[-5:]
    send = pltpu.make_async_copy(held_ref, pages_ref.at[layer], sem)
    send.start()
    wire[...] = got_ref[...].astype(F32)
    parts = [wire[JOIN * z : JOIN * z + 16] for z in range(16)]
    take = lambda part, k: part[:, HD + k : HD + k + 1]
    highs = [take(part, 3) + take(part, 4) + take(part, 5) for part in parts]
    top = functools.reduce(jnp.maximum, highs)
    total, mixed = 0.0, 0.0
    for part, high in zip(parts, highs):
        factor = jnp.exp(high - top)
        total = total + (take(part, 0) + take(part, 1) + take(part, 2)) * factor
        mixed = mixed + part * factor
    back[:16] = jnp.where(iota((16, 128), 1) < HD, mixed / total, 0.0)
    for k in range(2):
        back[pl.ds(16 + k, 16, stride=2), :] = wire[pl.ds(16 + k, 16, stride=JOIN), :]
    out_ref[...] = back[...].astype(BF16)
    send.wait()


def settle(layer, got, held, *pages):
    return call(
        functools.partial(settle_kernel, layer),
        "settle",
        (jax.ShapeDtypeStruct((LAYERS,) + held.shape, BF16), near_out((48, 128), BF16)),
        [
            pltpu.VMEM((16 * JOIN, 128), F32),
            pltpu.VMEM((48, 128), F32),
            pltpu.SemaphoreType.DMA,
        ],
        (),
        got,
        held,
        *pages,
        far=(2,),
        far_outs=(0,),
        aliases={2: 0} if pages else {},
    )


def output_kernel(layer, got_ref, wo_ref, wf_ref, out_ref):
    att = jnp.concatenate([got_ref[:16], got_ref[48:64]], axis=0).astype(F32)
    att = att + pltpu.roll(att, HD, 1)
    att = jnp.concatenate([att] * 4, axis=1)
    own = iota((32, 512), 1) // HD == iota((32, 512), 0) % 8
    by_head = dot_t(jnp.where(own, att, 0.0).astype(BF16), wo_ref[layer])
    tiles = []
    for core in range(2):
        act = got_ref[48 * core + 16 : 48 * core + 48].astype(F32)
        tiles += [act[4 * m : 4 * m + 4] for m in range(8)]
    mlp = dot_t(jnp.concatenate(tiles, axis=1).astype(BF16), wf_ref[layer])
    rows = [
        jnp.sum(by_head[8 * i : 8 * i + 8], axis=0, keepdims=True) + mlp[i : i + 1]
        for i in range(4)
    ]
    tile = jnp.concatenate(rows, axis=0)
    tile = jnp.concatenate([tile, jnp.zeros_like(tile)], axis=1)
    for k in range(4):
        out_ref[4 * k : 4 * k + 4] = tile


def output(layer, got, w_out, w_fc2):
    return call(
        functools.partial(output_kernel, layer),
        "output",
        (near_out((16, 128), F32),),
        [],
        (),
        got,
        w_out,
        w_fc2,
    )[0]


def per_device(
    hidden,
    ln_gain,
    w_qkv,
    w_fc1,
    w_out,
    w_fc2,
    caches,
    page_owner,
    page_used,
    page_fill,
    page_tail,
    positions,
):
    zs = [[2 * z + c for z in range(16)] for c in range(2)]
    pairs = [[2 * z, 2 * z + 1] for z in range(16)]
    rep_core = [[r * 32 + 2 * z + c for r in range(4) for c in range(2)] for z in range(16)]

    factors = rope_factors(positions)
    factors = jnp.concatenate([factors, factors], axis=1)
    meta = jnp.stack([page_owner, page_used, page_fill, page_tail])
    w_qkv = w_qkv.transpose(0, 2, 1, 3)
    w_out = w_out.transpose(0, 2, 1)
    w_fc2 = w_fc2.transpose(0, 2, 1)

    state, branch, pages = hidden, (), ()
    for layer in range(LAYERS):
        parts, state = project(layer, state, ln_gain, w_qkv, w_fc1, *branch)
        parts = lax.all_gather(parts, "blk", axis_index_groups=pairs)
        got = exchange(pool(parts).reshape(16, FLOW // 2, 2, 128), "blk", zs)
        packed, act = finish(got.reshape(16 * FLOW, 128), factors)
        got = exchange(packed, ("rep", "blk"), rep_core)
        held, parts = attend(layer, meta, got, caches)
        parts = exchange(parts.reshape(8, 16, 128), ("rep", "blk"), rep_core)
        got = exchange(join(parts, act).reshape(16, JOIN // 2, 2, 128), "blk", zs)
        fresh, got = settle(layer, got.reshape(16 * JOIN, 128), held, *pages)
        pages = (fresh,)
        got = lax.all_gather(got, "blk", axis_index_groups=pairs, tiled=True)
        out = output(layer, got, w_out, w_fc2).reshape(4, 4, 128)
        out = exchange(out, "tp")
        branch = (out.reshape(16, 128),)
    result = (state[:, :HD] + jnp.sum(out, axis=0)[:, :HD]).astype(BF16)
    return (result, fresh)


def solution(mesh):
    in_specs = (
        P("rep", "blk"),
        P(None, "blk"),
        P(None, "blk", None, "tp"),
        P(None, "blk", "tp"),
        P(None, "tp", "blk"),
        P(None, "tp", "blk"),
        P(None, None, ("rep", "blk"), None, "tp"),
        P(("rep", "blk")),
        P(("rep", "blk")),
        P(("rep", "blk")),
        P(("rep", "blk")),
        P("rep"),
    )
    out_specs = (P("rep", "blk"), P(None, None, ("rep", "blk"), None, "tp"))
    return jax.shard_map(
        per_device, mesh=mesh, in_specs=in_specs, out_specs=out_specs, check_vma=False
    )
```

```python
import functools
import math

import jax
import jax.numpy as jnp
import numpy as np
from jax import lax
from jax.experimental import pallas as pl
from jax.experimental.pallas import tpu as pltpu
from jax.sharding import PartitionSpec as P

D = 2048
HD = 64
ROT = 32
LAYERS = 2
PAGE = 32
EPSILON = 1e-05
LOWEST = -1e30
F32 = jnp.float32
BF16 = jnp.bfloat16
INVERSE = [float(np.float32(10000.0 ** (-2.0 * k / ROT))) for k in range(ROT // 2)]
TWO_PI_MIDDLE = float(np.floor((2.0 * math.pi - 6.28125) * 2.0**21) / 2.0**21)
TWO_PI_LAST = 2.0 * math.pi - 6.28125 - TWO_PI_MIDDLE
INTERPRET = False
HALF = 232
FLOW = 34
JOIN = 18


def exchange(value, axis, groups=None):
    return lax.all_to_all(value, axis, 0, 0, tiled=True, axis_index_groups=groups)


def rope_factors(positions):
    lane = iota((positions.shape[0], 128), 1) % HD
    inverse = jnp.zeros(lane.shape, F32)
    for k in range(ROT // 2):
        inverse = jnp.where(lane % (ROT // 2) == k, INVERSE[k], inverse)
    angles = positions * inverse
    turns = jnp.floor(angles * (1.0 / (2.0 * math.pi)) + 0.5)
    angles = angles - turns * 6.28125
    angles = angles - turns * TWO_PI_MIDDLE
    angles = angles - turns * TWO_PI_LAST
    sine = jnp.sin(angles)
    return jnp.where(lane < 32, jnp.cos(angles), jnp.where(lane < 48, -sine, sine))


def near(value):
    return value if INTERPRET else pltpu.with_memory_space_constraint(value, pltpu.VMEM)


def away(value):
    return value if INTERPRET else pltpu.with_memory_space_constraint(value, pltpu.HBM)


def near_out(shape, dtype):
    return jax.ShapeDtypeStruct(shape, dtype) if INTERPRET else pltpu.VMEM(shape, dtype)


def iota(shape, axis):
    return lax.broadcasted_iota(jnp.int32, shape, axis)


def dot32(left, right):
    return jnp.dot(left, right, preferred_element_type=F32)


def dot_t(left, right):
    return lax.dot_general(left, right, (((1,), (1,)), ((), ())), preferred_element_type=F32)


def parts_of(value, count):
    found = []
    for _ in range(count):
        part = value.astype(BF16).astype(F32)
        found.append(part)
        value = value - part
    return found


def rope(value, factors):
    lane = iota(value.shape, 1)
    left = lane < HD
    half = ROT // 2
    cosine = jnp.where(left, pltpu.roll(factors, 64, 1), factors)
    sine = jnp.where(left, pltpu.roll(factors, 32, 1), pltpu.roll(factors, 96, 1))
    other = jnp.where(
        lane % HD < half, pltpu.roll(value, 128 - half, 1), pltpu.roll(value, half, 1)
    )
    return jnp.where(lane % HD < ROT, value * cosine + other * sine, value)


def gelu(value):
    cubed = value * value * value
    return 0.5 * value * (1.0 + jnp.tanh(math.sqrt(2.0 / math.pi) * (value + 0.044715 * cubed)))


def column_of(row, first, period, shape):
    mine = iota(shape, 1) == first + iota(shape, 0) % period
    return jnp.sum(jnp.where(mine, row, 0.0), axis=1, keepdims=True)


def project_kernel(layer, x_ref, gain_ref, wq_ref, wf_ref, *refs):
    if layer == 0:
        pos_ref, out_ref, state_ref, gain_held, factor_ref, q_held, f_held = refs[:7]
        x_held, pos_held, sems = refs[7:]
        copies = [
            pltpu.make_async_copy(x_ref, x_held, sems.at[0]),
            pltpu.make_async_copy(gain_ref, gain_held, sems.at[1]),
            pltpu.make_async_copy(wq_ref.at[0], q_held, sems.at[2]),
            pltpu.make_async_copy(wf_ref.at[0], f_held, sems.at[3]),
            pltpu.make_async_copy(pos_ref, pos_held, sems.at[4]),
        ]
        for copy in copies:
            copy.start()
        copies[0].wait()
        copies[1].wait()
        x = x_held[...].astype(F32)
        gain_ref = gain_held
        copies[4].wait()
        places = jnp.broadcast_to(pos_held[...].astype(F32), (4, 4))
        mine = iota((4, 4), 0) == iota((4, 4), 1)
        places = jnp.sum(jnp.where(mine, places, 0.0), axis=1, keepdims=True)
        factor_ref[...] = rope_factors(places)
    else:
        branch_ref, out_ref, state_ref = refs
        x = x_ref[...] + branch_ref[0:4] + branch_ref[4:8] + branch_ref[8:12] + branch_ref[12:16]
        x = x.astype(BF16).astype(F32)[:, :HD]
    state_ref[...] = jnp.concatenate([x, jnp.zeros_like(x)], axis=1)
    gain = gain_ref[layer : layer + 1]
    mean = jnp.sum(x, axis=1, keepdims=True) * (1.0 / HD)
    centered = x - mean
    square = jnp.sum(centered * centered, axis=1, keepdims=True)
    rows = jnp.concatenate([centered * gain, jnp.broadcast_to(gain, (4, HD))], axis=0)
    high, low = parts_of(rows, 2)
    high, low = high.astype(BF16), low.astype(BF16)
    if layer == 0:
        copies[2].wait()
    for k in range(3):
        weights = q_held[k] if layer == 0 else wq_ref[layer, k]
        every = dot32(high, weights) + dot32(low, weights)
        for j in range(4):
            start = 8 * (4 * k + j)
            out_ref[start : start + 8] = every[:, 128 * j : 128 * j + 128]
    if layer == 0:
        copies[3].wait()
    weights = f_held[...] if layer == 0 else wf_ref[layer]
    every = dot32(high, weights) + dot32(low, weights)
    for j in range(16):
        out_ref[96 + 8 * j : 104 + 8 * j] = every[:, 128 * j : 128 * j + 128]
    lane = iota((4, 128), 1)
    request = iota((4, 128), 0)
    stats = jnp.where(lane == request, mean, jnp.where(lane == request + 16, square, 0.0))
    out_ref[224:232] = jnp.broadcast_to(jnp.sum(stats, axis=0, keepdims=True), (8, 128))


def call(kernel, name, outs, scratch, tables, *args, far=(), far_outs=(), aliases=None):
    near_spec = pl.BlockSpec(memory_space=pltpu.VMEM)
    far_spec = pl.BlockSpec(memory_space=pl.ANY)
    specs = [pl.BlockSpec(memory_space=pltpu.SMEM) for _ in tables]
    specs += [far_spec if k in far else near_spec for k in range(len(args))]
    args = [away(arg) if k in far else near(arg) for k, arg in enumerate(args)]
    return pl.pallas_call(
        kernel,
        in_specs=specs,
        out_specs=tuple(far_spec if k in far_outs else near_spec for k in range(len(outs))),
        out_shape=tuple(outs),
        scratch_shapes=scratch,
        input_output_aliases=aliases or {},
        compiler_params=pltpu.CompilerParams(vmem_limit_bytes=24 * 2**20),
        name=name,
        interpret=INTERPRET,
    )(*tables, *args)


def project(layer, x, gain, wq, wf, *more):
    outs = [near_out((HALF, 128), F32), near_out((4, 128), F32)]
    scratch = []
    if layer == 0:
        outs += [near_out(gain.shape, F32), near_out((4, 128), F32)]
        scratch = [
            pltpu.VMEM(wq.shape[1:], BF16),
            pltpu.VMEM(wf.shape[1:], BF16),
            pltpu.VMEM(x.shape, x.dtype),
            pltpu.VMEM((1, 4), jnp.int32),
            pltpu.SemaphoreType.DMA((5,)),
        ]
    return call(
        functools.partial(project_kernel, layer),
        "project",
        outs,
        scratch,
        (),
        x,
        gain,
        wq,
        wf,
        *more,
        far=(0, 1, 2, 3, 4) if layer == 0 else (),
    )


def pool_kernel(got_ref, out_ref, wire):
    core = lax.axis_index("blk") % 2
    means = [got_ref[s, 224:225] for s in range(2)]
    center = 0.5 * (means[0] + means[1])
    moves = [mean - center for mean in means]
    square = pltpu.roll(means[0] + means[1], 112, 1) + 64.0 * (
        moves[0] * moves[0] + moves[1] * moves[1]
    )
    upper = iota((8, 1), 0) < 4
    shift = [jnp.where(upper, column_of(move, 0, 4, (8, 128)), 0.0) for move in moves]

    def block(start):
        total = 0.0
        for s in range(2):
            part = got_ref[s, pl.ds(pl.multiple_of(start, 8), 8), :]
            total = total + part + shift[s] * part[4:5]
        return total

    common = []
    columns = []
    for base in (0, 32, 64):
        one = block(base + 16 * core)
        two = block(base + 16 * core + 8)
        common.append(jnp.where(upper, one, pltpu.roll(two, 4, 0)))
        columns += [one[4:5], two[4:5]]
    lane = iota((4, 128), 1)
    request = iota((4, 128), 0)
    stats = jnp.zeros((4, 128), F32)
    both = parts_of(column_of(center, 0, 4, (4, 128)), 3)
    both += parts_of(column_of(square, 0, 4, (4, 128)), 3)
    for k, part in enumerate(both):
        stats = jnp.where(lane == request + 16 * k, part, stats)
    columns.append(jnp.sum(stats, axis=0, keepdims=True))
    row = iota((8, 128), 0)
    tail = jnp.zeros((8, 128), F32)
    for k, column in enumerate(columns):
        tail = jnp.where(row == k, column, tail)
    shared = jnp.concatenate(common, axis=0)
    for m in range(8):
        last = block(96 + 64 * core + 8 * m)
        whole = jnp.concatenate([shared, jnp.where(row == 7, last[4:5], tail)], axis=0)
        for k in range(2):
            start = FLOW * (2 * m + k)
            wire[start : start + 32] = whole
            wire[start + 32 : start + 34] = last[2 * k : 2 * k + 2]
    out_ref[...] = wire[...].astype(BF16)


def pool(got):
    return call(
        pool_kernel,
        "pool",
        (near_out((16 * FLOW, 128), BF16),),
        [pltpu.VMEM((16 * FLOW, 128), F32)],
        (),
        got,
    )[0]


def finish_kernel(got_ref, factor_ref, out_ref, act_ref, wire):
    wire[...] = got_ref[...].astype(F32)
    stats = wire[pl.ds(30, 16, stride=FLOW), :]
    stats = stats + pltpu.roll(stats, 112, 1) + pltpu.roll(stats, 96, 1)
    average = jnp.sum(stats, axis=0, keepdims=True) * (1.0 / 16)
    offset = stats - average
    spread_sum = 128.0 * jnp.sum(offset * offset, axis=0, keepdims=True)
    square_sum = pltpu.roll(jnp.sum(stats, axis=0, keepdims=True), 80, 1)
    rstd = lax.rsqrt((square_sum + spread_sum) * (1.0 / D) + EPSILON)
    upper = iota((8, 128), 0) < 4
    pair = 2 * ((lax.axis_index("blk") // 2) % 2)
    sums = [0.0] * 4
    for z in range(16):
        base = FLOW * z
        move = offset[z : z + 1]
        mine = column_of(move, 0, 4, (8, 128))
        tail = wire[base + 24 : base + 32]
        for k in range(3):
            part = wire[base + 8 * k : base + 8 * k + 8]
            column = jnp.where(upper, tail[2 * k : 2 * k + 1], tail[2 * k + 1 : 2 * k + 2])
            sums[k] = sums[k] + part + mine * column
        part = wire[base + 32 : base + 34]
        sums[3] = sums[3] + part + column_of(move, pair, 2, (2, 128)) * tail[7:8]
    mine = column_of(rstd, 0, 4, (8, 128))
    factors = jnp.concatenate([factor_ref[...], factor_ref[...]], axis=0)
    packed = [rope(mine * sums[k], factors) for k in range(2)] + [mine * sums[2]]
    packed = jnp.concatenate(packed, axis=0).astype(BF16)
    for k in range(8):
        out_ref[k] = packed
    act_ref[...] = gelu(column_of(rstd, pair, 2, (2, 128)) * sums[3])


def finish(got, factors):
    return call(
        finish_kernel,
        "finish",
        (near_out((8, 24, 128), BF16), near_out((2, 128), F32)),
        [pltpu.VMEM((16 * FLOW, 128), F32)],
        (),
        got,
        factors,
    )


def attend_kernel(layer, owner_ref, used_ref, fill_ref, tail_ref, got_ref, cache_ref, *refs):
    pages_ref, held, out_ref, kv, sem = refs[-5:]
    rep = lax.axis_index("rep")
    tiles = []
    for tile in range(4):
        core, rows = tile // 2, 4 * (tile % 2)
        parts = [got_ref[2 * r + core, :8].astype(F32)[rows : rows + 4] for r in range(4)]
        tiles.append(jnp.concatenate(parts, axis=0))
        new = got_ref[2 * rep + core].astype(F32)
        for side in range(2):
            start = 8 + 8 * side + rows
            kv[side, :, 128 * tile : 128 * tile + 128] = new[start : start + 4]
    queries = jnp.concatenate(tiles, axis=1)
    queries = [queries[i : i + 1] for i in range(16)]
    spot = iota((PAGE, 512), 0)
    send = pltpu.make_async_copy(held.at[0], pages_ref.at[layer, 0], sem)
    for side in range(2):
        for page in range(8):
            home = jnp.clip(owner_ref[page] - rep * 4, 0, 3)
            place = jnp.where(tail_ref[page] == 1, fill_ref[page], -1)
            fresh = kv[side, pl.ds(home, 1), :]
            old = cache_ref[layer, side, page].astype(F32)
            held[side, page] = jnp.where(spot == place, fresh, old).astype(BF16)
        if side == 0:
            send.start()
    head_of = iota((8, 512), 1) // HD == iota((8, 512), 0)
    wide = jnp.concatenate(
        [jnp.where(head_of, jnp.broadcast_to(row, (8, 512)), 0.0) for row in queries], axis=0
    ).astype(BF16)
    keys = held[0].reshape(8 * PAGE, 512)
    values = held[1].reshape(8 * PAGE, 512)
    scores = dot_t(wide, keys) * HD ** (-0.5)
    page_of = iota((1, 256), 1) // PAGE
    owner = jnp.zeros((1, 256), jnp.int32)
    limit = jnp.zeros((1, 256), jnp.int32)
    for page in range(8):
        length = jnp.where(used_ref[page] == 1, fill_ref[page] + tail_ref[page], 0)
        owner = jnp.where(page_of == page, owner_ref[page], owner)
        limit = jnp.where(page_of == page, length, limit)
    owner = jnp.where(iota((1, 256), 1) % PAGE < limit, owner, -1)
    allowed = iota((128, 256), 0) // 8 == owner
    scores = jnp.where(allowed, scores, LOWEST)
    high = jnp.max(scores, axis=1, keepdims=True)
    weights = jnp.where(allowed, jnp.exp(scores - high), 0.0)
    total = jnp.sum(weights, axis=1, keepdims=True)
    mixed = dot32(weights.astype(BF16), values)
    head = iota((128, 128), 0) % 8
    lane = iota((128, 128), 1)
    picked = mixed[:, :128]
    for k in range(1, 4):
        picked = jnp.where(head // 2 == k, mixed[:, 128 * k : 128 * k + 128], picked)
    picked = jnp.where(head % 2 == 1, pltpu.roll(picked, HD, 1), picked)
    out_ref[...] = jnp.where(
        lane < HD, picked, jnp.where(lane == HD, total, jnp.where(lane == HD + 1, high, 0.0))
    )
    send.wait()


def attend(layer, tables, got, caches, *pages):
    return call(
        functools.partial(attend_kernel, layer),
        "attend",
        (
            jax.ShapeDtypeStruct(caches.shape, BF16),
            near_out(caches.shape[1:], BF16),
            near_out((128, 128), F32),
        ),
        [pltpu.VMEM((2, 4, 512), F32), pltpu.SemaphoreType.DMA],
        tables,
        got,
        caches,
        *pages,
        far=(2,),
        far_outs=(0,),
        aliases={6: 0} if pages else {},
    )


def join_kernel(got_ref, act_ref, out_ref, wire):
    got = got_ref[...]
    high = got[:, :, HD + 1 : HD + 2]
    top = jnp.max(high, axis=0)
    total = jnp.sum(got * jnp.exp(high - top[None]), axis=0)
    lane = iota((16, 128), 1)
    out = jnp.where(lane < HD, total, 0.0)
    extra = parts_of(total[:, HD : HD + 1], 3) + parts_of(top, 3)
    for k, part in enumerate(extra):
        out = jnp.where(lane == HD + k, part, out)
    act = act_ref[...]
    for z in range(16):
        wire[JOIN * z : JOIN * z + 16] = out
        wire[JOIN * z + 16 : JOIN * z + 18] = act
    out_ref[...] = wire[...].astype(BF16)


def join(got, act):
    return call(
        join_kernel,
        "join",
        (near_out((16 * JOIN, 128), BF16),),
        [pltpu.VMEM((16 * JOIN, 128), F32)],
        (),
        got,
        act,
    )[0]


def settle_kernel(layer, got_ref, held_ref, *refs):
    pages_ref, out_ref, wire, back, sem = refs[-5:]
    send = pltpu.make_async_copy(held_ref.at[1], pages_ref.at[layer, 1], sem)
    send.start()
    wire[...] = got_ref[...].astype(F32)
    parts = [wire[JOIN * z : JOIN * z + 16] for z in range(16)]
    take = lambda part, k: part[:, HD + k : HD + k + 1]
    highs = [take(part, 3) + take(part, 4) + take(part, 5) for part in parts]
    top = functools.reduce(jnp.maximum, highs)
    total, mixed = 0.0, 0.0
    for part, high in zip(parts, highs):
        factor = jnp.exp(high - top)
        total = total + (take(part, 0) + take(part, 1) + take(part, 2)) * factor
        mixed = mixed + part * factor
    back[:16] = jnp.where(iota((16, 128), 1) < HD, mixed / total, 0.0)
    for k in range(2):
        back[pl.ds(16 + k, 16, stride=2), :] = wire[pl.ds(16 + k, 16, stride=JOIN), :]
    out_ref[...] = back[...].astype(BF16)
    send.wait()


def settle(layer, got, held, pages):
    return call(
        functools.partial(settle_kernel, layer),
        "settle",
        (jax.ShapeDtypeStruct((LAYERS,) + held.shape, BF16), near_out((48, 128), BF16)),
        [
            pltpu.VMEM((16 * JOIN, 128), F32),
            pltpu.VMEM((48, 128), F32),
            pltpu.SemaphoreType.DMA,
        ],
        (),
        got,
        held,
        pages,
        far=(2,),
        far_outs=(0,),
        aliases={2: 0},
    )


def output_kernel(layer, got_ref, wo_ref, wf_ref, out_ref):
    att = jnp.concatenate([got_ref[:16], got_ref[48:64]], axis=0).astype(F32)
    att = att + pltpu.roll(att, HD, 1)
    att = jnp.concatenate([att] * 4, axis=1)
    own = iota((32, 512), 1) // HD == iota((32, 512), 0) % 8
    by_head = dot_t(jnp.where(own, att, 0.0).astype(BF16), wo_ref[layer])
    tiles = []
    for core in range(2):
        act = got_ref[48 * core + 16 : 48 * core + 48].astype(F32)
        tiles += [act[4 * m : 4 * m + 4] for m in range(8)]
    mlp = dot_t(jnp.concatenate(tiles, axis=1).astype(BF16), wf_ref[layer])
    rows = [
        jnp.sum(by_head[8 * i : 8 * i + 8], axis=0, keepdims=True) + mlp[i : i + 1]
        for i in range(4)
    ]
    tile = jnp.concatenate(rows, axis=0)
    tile = jnp.concatenate([tile, jnp.zeros_like(tile)], axis=1)
    for k in range(4):
        out_ref[4 * k : 4 * k + 4] = tile


def output(layer, got, w_out, w_fc2):
    return call(
        functools.partial(output_kernel, layer),
        "output",
        (near_out((16, 128), F32),),
        [],
        (),
        got,
        w_out,
        w_fc2,
    )[0]


def per_device(
    hidden,
    ln_gain,
    w_qkv,
    w_fc1,
    w_out,
    w_fc2,
    caches,
    page_owner,
    page_used,
    page_fill,
    page_tail,
    positions,
):
    zs = [[2 * z + c for z in range(16)] for c in range(2)]
    pairs = [[2 * z, 2 * z + 1] for z in range(16)]
    rep_core = [[r * 32 + 2 * z + c for r in range(4) for c in range(2)] for z in range(16)]

    tables = (page_owner, page_used, page_fill, page_tail)
    more = (positions.reshape(1, 4),)
    w_qkv = w_qkv.transpose(0, 2, 1, 3)
    w_out = w_out.transpose(0, 2, 1)
    w_fc2 = w_fc2.transpose(0, 2, 1)

    state, gain, pages = hidden, ln_gain, ()
    for layer in range(LAYERS):
        parts, state, *kept = project(layer, state, gain, w_qkv, w_fc1, *more)
        if layer == 0:
            gain, factors = kept
        parts = lax.all_gather(parts, "blk", axis_index_groups=pairs)
        got = exchange(pool(parts).reshape(16, FLOW // 2, 2, 128), "blk", zs)
        packed, act = finish(got.reshape(16 * FLOW, 128), factors)
        got = exchange(packed, ("rep", "blk"), rep_core)
        fresh, held, parts = attend(layer, tables, got, caches, *pages)
        parts = exchange(parts.reshape(8, 16, 128), ("rep", "blk"), rep_core)
        got = exchange(join(parts, act).reshape(16, JOIN // 2, 2, 128), "blk", zs)
        fresh, got = settle(layer, got.reshape(16 * JOIN, 128), held, fresh)
        pages = (fresh,)
        got = lax.all_gather(got, "blk", axis_index_groups=pairs, tiled=True)
        out = output(layer, got, w_out, w_fc2).reshape(4, 4, 128)
        out = exchange(out, "tp")
        more = (out.reshape(16, 128),)
    result = (state[:, :HD] + jnp.sum(out, axis=0)[:, :HD]).astype(BF16)
    return (result, fresh)


def solution(mesh):
    in_specs = (
        P("rep", "blk"),
        P(None, "blk"),
        P(None, "blk", None, "tp"),
        P(None, "blk", "tp"),
        P(None, "tp", "blk"),
        P(None, "tp", "blk"),
        P(None, None, ("rep", "blk"), None, "tp"),
        P(("rep", "blk")),
        P(("rep", "blk")),
        P(("rep", "blk")),
        P(("rep", "blk")),
        P("rep"),
    )
    out_specs = (P("rep", "blk"), P(None, None, ("rep", "blk"), None, "tp"))
    return jax.shard_map(
        per_device, mesh=mesh, in_specs=in_specs, out_specs=out_specs, check_vma=False
    )
```

```python
import functools
import math

import jax
import jax.numpy as jnp
import numpy as np
from jax import lax
from jax.experimental import pallas as pl
from jax.experimental.pallas import tpu as pltpu
from jax.sharding import PartitionSpec as P

D = 2048
HD = 64
ROT = 32
LAYERS = 2
PAGE = 32
EPSILON = 1e-05
LOWEST = -1e30
F32 = jnp.float32
BF16 = jnp.bfloat16
INVERSE = [float(np.float32(10000.0 ** (-2.0 * k / ROT))) for k in range(ROT // 2)]
TWO_PI_MIDDLE = float(np.floor((2.0 * math.pi - 6.28125) * 2.0**21) / 2.0**21)
TWO_PI_LAST = 2.0 * math.pi - 6.28125 - TWO_PI_MIDDLE
INTERPRET = False
HALF = 232
FLOW = 16
JOIN = 20


def exchange(value, axis, groups=None):
    return lax.all_to_all(value, axis, 0, 0, tiled=True, axis_index_groups=groups)


def rope_factors(positions):
    lane = iota((positions.shape[0], 128), 1) % HD
    inverse = jnp.zeros(lane.shape, F32)
    for k in range(ROT // 2):
        inverse = jnp.where(lane % (ROT // 2) == k, INVERSE[k], inverse)
    angles = positions * inverse
    turns = jnp.floor(angles * (1.0 / (2.0 * math.pi)) + 0.5)
    angles = angles - turns * 6.28125
    angles = angles - turns * TWO_PI_MIDDLE
    angles = angles - turns * TWO_PI_LAST
    sine = jnp.sin(angles)
    return jnp.where(lane < 32, jnp.cos(angles), jnp.where(lane < 48, -sine, sine))


def near(value):
    return value if INTERPRET else pltpu.with_memory_space_constraint(value, pltpu.VMEM)


def away(value):
    return value if INTERPRET else pltpu.with_memory_space_constraint(value, pltpu.HBM)


def near_out(shape, dtype):
    return jax.ShapeDtypeStruct(shape, dtype) if INTERPRET else pltpu.VMEM(shape, dtype)


def iota(shape, axis):
    return lax.broadcasted_iota(jnp.int32, shape, axis)


def dot32(left, right):
    return jnp.dot(left, right, preferred_element_type=F32)


def dot_t(left, right):
    return lax.dot_general(left, right, (((1,), (1,)), ((), ())), preferred_element_type=F32)


def parts_of(value, count):
    found = []
    for _ in range(count):
        part = value.astype(BF16).astype(F32)
        found.append(part)
        value = value - part
    return found


def rope(value, factors):
    lane = iota(value.shape, 1)
    left = lane < HD
    half = ROT // 2
    cosine = jnp.where(left, pltpu.roll(factors, 64, 1), factors)
    sine = jnp.where(left, pltpu.roll(factors, 32, 1), pltpu.roll(factors, 96, 1))
    other = jnp.where(
        lane % HD < half, pltpu.roll(value, 128 - half, 1), pltpu.roll(value, half, 1)
    )
    return jnp.where(lane % HD < ROT, value * cosine + other * sine, value)


def gelu(value):
    cubed = value * value * value
    return 0.5 * value * (1.0 + jnp.tanh(math.sqrt(2.0 / math.pi) * (value + 0.044715 * cubed)))


def column_of(row, first, period, shape):
    mine = iota(shape, 1) == first + iota(shape, 0) % period
    return jnp.sum(jnp.where(mine, row, 0.0), axis=1, keepdims=True)


def project_kernel(layer, x_ref, gain_ref, wq_ref, wf_ref, *refs):
    if layer == 0:
        pos_ref, out_ref, state_ref, gain_held, factor_ref, q_held, f_held = refs[:7]
        x_held, pos_held, sems = refs[7:]
        copies = [
            pltpu.make_async_copy(x_ref, x_held, sems.at[0]),
            pltpu.make_async_copy(gain_ref, gain_held, sems.at[1]),
            pltpu.make_async_copy(wq_ref.at[0], q_held, sems.at[2]),
            pltpu.make_async_copy(wf_ref.at[0], f_held, sems.at[3]),
            pltpu.make_async_copy(pos_ref, pos_held, sems.at[4]),
        ]
        for copy in copies:
            copy.start()
        copies[0].wait()
        copies[1].wait()
        x = x_held[...].astype(F32)
        gain_ref = gain_held
        copies[4].wait()
        places = jnp.broadcast_to(pos_held[...].astype(F32), (4, 4))
        mine = iota((4, 4), 0) == iota((4, 4), 1)
        places = jnp.sum(jnp.where(mine, places, 0.0), axis=1, keepdims=True)
        factor_ref[...] = rope_factors(places)
    else:
        branch_ref, out_ref, state_ref = refs
        x = x_ref[...] + branch_ref[0:4] + branch_ref[4:8] + branch_ref[8:12] + branch_ref[12:16]
        x = x.astype(BF16).astype(F32)[:, :HD]
    state_ref[...] = jnp.concatenate([x, jnp.zeros_like(x)], axis=1)
    gain = gain_ref[layer : layer + 1]
    mean = jnp.sum(x, axis=1, keepdims=True) * (1.0 / HD)
    centered = x - mean
    square = jnp.sum(centered * centered, axis=1, keepdims=True)
    rows = jnp.concatenate([centered * gain, jnp.broadcast_to(gain, (4, HD))], axis=0)
    high, low = parts_of(rows, 2)
    high, low = high.astype(BF16), low.astype(BF16)
    if layer == 0:
        copies[2].wait()
    for k in range(3):
        weights = q_held[k] if layer == 0 else wq_ref[layer, k]
        every = dot32(high, weights) + dot32(low, weights)
        for j in range(4):
            start = 8 * (4 * k + j)
            out_ref[start : start + 8] = every[:, 128 * j : 128 * j + 128]
    if layer == 0:
        copies[3].wait()
    weights = f_held[...] if layer == 0 else wf_ref[layer]
    every = dot32(high, weights) + dot32(low, weights)
    for j in range(16):
        out_ref[96 + 8 * j : 104 + 8 * j] = every[:, 128 * j : 128 * j + 128]
    lane = iota((4, 128), 1)
    request = iota((4, 128), 0)
    stats = jnp.where(lane == request, mean, jnp.where(lane == request + 16, square, 0.0))
    out_ref[224:232] = jnp.broadcast_to(jnp.sum(stats, axis=0, keepdims=True), (8, 128))


def call(kernel, name, outs, scratch, tables, *args, far=(), far_outs=(), aliases=None):
    near_spec = pl.BlockSpec(memory_space=pltpu.VMEM)
    far_spec = pl.BlockSpec(memory_space=pl.ANY)
    specs = [pl.BlockSpec(memory_space=pltpu.SMEM) for _ in tables]
    specs += [far_spec if k in far else near_spec for k in range(len(args))]
    args = [away(arg) if k in far else near(arg) for k, arg in enumerate(args)]
    return pl.pallas_call(
        kernel,
        in_specs=specs,
        out_specs=tuple(far_spec if k in far_outs else near_spec for k in range(len(outs))),
        out_shape=tuple(outs),
        scratch_shapes=scratch,
        input_output_aliases=aliases or {},
        compiler_params=pltpu.CompilerParams(vmem_limit_bytes=24 * 2**20),
        name=name,
        interpret=INTERPRET,
    )(*tables, *args)


def project(layer, x, gain, wq, wf, *more):
    outs = [near_out((HALF, 128), F32), near_out((4, 128), F32)]
    scratch = []
    if layer == 0:
        outs += [near_out(gain.shape, F32), near_out((4, 128), F32)]
        scratch = [
            pltpu.VMEM(wq.shape[1:], BF16),
            pltpu.VMEM(wf.shape[1:], BF16),
            pltpu.VMEM(x.shape, x.dtype),
            pltpu.VMEM((1, 4), jnp.int32),
            pltpu.SemaphoreType.DMA((5,)),
        ]
    return call(
        functools.partial(project_kernel, layer),
        "project",
        outs,
        scratch,
        (),
        x,
        gain,
        wq,
        wf,
        *more,
        far=(0, 1, 2, 3, 4) if layer == 0 else (),
    )


def pool_kernel(got_ref, out_ref):
    core = lax.axis_index("blk") % 2
    means = [got_ref[s, 224:225] for s in range(2)]
    center = 0.5 * (means[0] + means[1])
    moves = [mean - center for mean in means]
    square = pltpu.roll(means[0] + means[1], 112, 1) + 64.0 * (
        moves[0] * moves[0] + moves[1] * moves[1]
    )
    upper = iota((8, 1), 0) < 4
    shift = [jnp.where(upper, column_of(move, 0, 4, (8, 128)), 0.0) for move in moves]

    def block(start):
        total = 0.0
        for s in range(2):
            part = got_ref[s, pl.ds(pl.multiple_of(start, 8), 8), :]
            total = total + part + shift[s] * part[4:5]
        return total

    merged = []
    columns = []
    for base in (0, 32, 64):
        one = block(base + 16 * core)
        two = block(base + 16 * core + 8)
        merged.append(jnp.where(upper, one, pltpu.roll(two, 4, 0)))
        columns.append((one[4:5], two[4:5]))
    lane = iota((4, 128), 1)
    request = iota((4, 128), 0)
    stats = jnp.zeros((4, 128), F32)
    both = parts_of(column_of(center, 0, 4, (4, 128)), 3)
    both += parts_of(column_of(square, 0, 4, (4, 128)), 3)
    for k, part in enumerate(both):
        stats = jnp.where(lane == request + 16 * k, part, stats)
    stats = jnp.sum(stats, axis=0, keepdims=True)
    row = iota((8, 128), 0)
    base = jnp.where(row == 0, columns[0][0], jnp.where(row == 1, columns[0][1], stats))
    for m in range(8):
        last = block(96 + 64 * core + 8 * m)
        for k in range(2):
            z = 2 * m + k
            side, slot = 1 + z // 8, z % 8
            rows = (
                merged[side][slot : slot + 1],
                columns[side][slot // 4],
                last[4:5],
                last[2 * k : 2 * k + 1],
                last[2 * k + 1 : 2 * k + 2],
            )
            tail = base
            for j, value in enumerate(rows):
                tail = jnp.where(row == 3 + j, value, tail)
            whole = jnp.concatenate([merged[0], tail], axis=0)
            out_ref[FLOW * z : FLOW * z + FLOW] = whole.astype(BF16)


def pool(got):
    return call(
        pool_kernel,
        "pool",
        (near_out((16 * FLOW, 128), BF16),),
        [],
        (),
        got,
    )[0]


def finish_kernel(got_ref, factor_ref, out_ref, held_ref, extra_ref):
    blocks = [got_ref[FLOW * z : FLOW * z + FLOW].astype(F32) for z in range(16)]
    stats = jnp.concatenate([block[10:11] for block in blocks], axis=0)
    stats = stats + pltpu.roll(stats, 112, 1) + pltpu.roll(stats, 96, 1)
    average = jnp.sum(stats, axis=0, keepdims=True) * (1.0 / 16)
    offset = stats - average
    spread_sum = 128.0 * jnp.sum(offset * offset, axis=0, keepdims=True)
    square_sum = pltpu.roll(jnp.sum(stats, axis=0, keepdims=True), 80, 1)
    rstd = lax.rsqrt((square_sum + spread_sum) * (1.0 / D) + EPSILON)
    upper = iota((8, 128), 0) < 4
    here = lax.axis_index("blk") // 2
    pair, single = 2 * (here % 2), here % 4
    query, entry, inner = 0.0, 0.0, 0.0
    for z, block in enumerate(blocks):
        move = offset[z : z + 1]
        column = jnp.where(upper, block[8:9], block[9:10])
        query = query + block[:8] + column_of(move, 0, 4, (8, 128)) * column
        entry = entry + block[11:12] + column_of(move, single, 1, (1, 128)) * block[12:13]
        inner = inner + block[14:16] + column_of(move, pair, 2, (2, 128)) * block[13:14]
    query = column_of(rstd, 0, 4, (8, 128)) * query
    query = rope(query, jnp.concatenate([factor_ref[...], factor_ref[...]], axis=0)).astype(BF16)
    for k in range(8):
        out_ref[k] = query
    held_ref[...] = query.astype(F32)
    entry = column_of(rstd, single, 1, (1, 128)) * entry
    turned = rope(entry, factor_ref[pl.ds(single, 1), :])
    extra_ref[0:2] = gelu(column_of(rstd, pair, 2, (2, 128)) * inner)
    extra_ref[2:3] = jnp.where(jnp.full((1, 128), here) < 8, turned, entry)
    extra_ref[3:4] = jnp.zeros((1, 128), F32)


def finish(got, factors):
    return call(
        finish_kernel,
        "finish",
        (near_out((8, 8, 128), BF16), near_out((8, 128), F32), near_out((4, 128), F32)),
        [],
        (),
        got,
        factors,
    )


def attend_kernel(layer, owner_ref, used_ref, fill_ref, got_ref, cache_ref, out_ref):
    tiles = []
    for tile in range(4):
        core, rows = tile // 2, 4 * (tile % 2)
        parts = [got_ref[2 * r + core].astype(F32)[rows : rows + 4] for r in range(4)]
        tiles.append(jnp.concatenate(parts, axis=0))
    queries = jnp.concatenate(tiles, axis=1)
    place = iota((8, 512), 0)
    wide = []
    for rep in range(4):
        for core in range(2):
            for i in (0, 2):
                row = 4 * rep + i
                both = jnp.where(place < 4, queries[row : row + 1], queries[row + 1 : row + 2])
                mine = iota((8, 512), 1) // HD == 4 * core + place % 4
                wide.append(jnp.where(mine, both, 0.0))
    wide = jnp.concatenate(wide, axis=0).astype(BF16)
    keys = cache_ref[layer, 0].reshape(8 * PAGE, 512)
    values = cache_ref[layer, 1].reshape(8 * PAGE, 512)
    scores = dot_t(wide, keys) * HD ** (-0.5)
    page_of = iota((1, 256), 1) // PAGE
    owner = jnp.zeros((1, 256), jnp.int32)
    limit = jnp.zeros((1, 256), jnp.int32)
    for page in range(8):
        length = jnp.where(used_ref[page] == 1, fill_ref[page], 0)
        owner = jnp.where(page_of == page, owner_ref[page], owner)
        limit = jnp.where(page_of == page, length, limit)
    owner = jnp.where(iota((1, 256), 1) % PAGE < limit, owner, -1)
    pair = iota((128, 256), 0)
    allowed = 4 * (pair // 32) + pair % 16 // 4 == owner
    scores = jnp.where(allowed, scores, LOWEST)
    high = jnp.max(scores, axis=1, keepdims=True)
    weights = jnp.where(allowed, jnp.exp(scores - high), 0.0)
    total = jnp.sum(weights, axis=1, keepdims=True)
    mixed = dot32(weights.astype(BF16), values)
    head = iota((128, 128), 0) // 16 % 2 * 4 + iota((128, 128), 0) % 4
    lane = iota((128, 128), 1)
    picked = mixed[:, :128]
    for k in range(1, 4):
        picked = jnp.where(head // 2 == k, mixed[:, 128 * k : 128 * k + 128], picked)
    picked = jnp.where(head % 2 == 1, pltpu.roll(picked, HD, 1), picked)
    out_ref[...] = jnp.where(
        lane < HD, picked, jnp.where(lane == HD, total, jnp.where(lane == HD + 1, high, 0.0))
    )


def attend(layer, tables, got, caches):
    return call(
        functools.partial(attend_kernel, layer),
        "attend",
        (near_out((128, 128), F32),),
        [],
        tables,
        got,
        caches,
    )[0]


def join_kernel(got_ref, act_ref, out_ref, wire):
    got = got_ref[...]
    high = got[:, :, HD + 1 : HD + 2]
    top = jnp.max(high, axis=0)
    total = jnp.sum(got * jnp.exp(high - top[None]), axis=0)
    lane = iota((16, 128), 1)
    out = jnp.where(lane < HD, total, 0.0)
    extra = parts_of(total[:, HD : HD + 1], 3) + parts_of(top, 3)
    for k, part in enumerate(extra):
        out = jnp.where(lane == HD + k, part, out)
    act = act_ref[...]
    for z in range(16):
        wire[JOIN * z : JOIN * z + 16] = out
        wire[JOIN * z + 16 : JOIN * z + 20] = act
    out_ref[...] = wire[...].astype(BF16)


def join(got, act):
    return call(
        join_kernel,
        "join",
        (near_out((16 * JOIN, 128), BF16),),
        [pltpu.VMEM((16 * JOIN, 128), F32)],
        (),
        got,
        act,
    )[0]


def settle_kernel(got_ref, query_ref, out_ref, wire, back, score, fresh):
    wire[...] = got_ref[...].astype(F32)
    entries = wire[pl.ds(18, 16, stride=JOIN), :]
    product = query_ref[...] * entries[:8]
    left = iota((8, 128), 1) < HD
    for half in range(2):
        summed = jnp.sum(jnp.where(left == (half == 0), product, 0.0), axis=1, keepdims=True)
        summed = jnp.broadcast_to(summed * HD ** (-0.5), (8, 128))
        value = entries[8:] if half == 0 else pltpu.roll(entries[8:], HD, 1)
        for j in range(2):
            score[pl.ds(2 * j + half, 4, stride=4), :] = summed[4 * j : 4 * j + 4]
            fresh[pl.ds(2 * j + half, 4, stride=4), :] = value[4 * j : 4 * j + 4]
    parts = [wire[JOIN * z : JOIN * z + 16] for z in range(16)]
    take = lambda part, k: part[:, HD + k : HD + k + 1]
    highs = [take(part, 3) + take(part, 4) + take(part, 5) for part in parts]
    own = score[:, 0:1]
    top = functools.reduce(jnp.maximum, highs, own)
    total = jnp.exp(own - top)
    mixed = fresh[...] * total
    for part, high in zip(parts, highs):
        factor = jnp.exp(high - top)
        total = total + (take(part, 0) + take(part, 1) + take(part, 2)) * factor
        mixed = mixed + part * factor
    back[:16] = jnp.where(iota((16, 128), 1) < HD, mixed / total, 0.0)
    for k in range(2):
        back[pl.ds(16 + k, 16, stride=2), :] = wire[pl.ds(16 + k, 16, stride=JOIN), :]
    back[48:] = entries
    out_ref[...] = back[...].astype(BF16)


def settle(got, query):
    return call(
        settle_kernel,
        "settle",
        (near_out((64, 128), BF16),),
        [
            pltpu.VMEM((16 * JOIN, 128), F32),
            pltpu.VMEM((64, 128), F32),
            pltpu.VMEM((16, 128), F32),
            pltpu.VMEM((16, 128), F32),
        ],
        (),
        got,
        query,
    )[0]


def renew_kernel(owner_ref, fill_ref, tail_ref, one_ref, two_ref, cache_ref, pages_ref, held, kv, sems):
    rep = lax.axis_index("rep")
    spot = iota((PAGE, 512), 0)
    sends = []
    for layer, got_ref in enumerate((one_ref, two_ref)):
        for tile in range(4):
            start = 64 * (tile // 2) + 48
            new = got_ref[start : start + 16].astype(F32)
            for side in range(2):
                rows = 8 * side + 4 * (tile % 2)
                kv[side, :, 128 * tile : 128 * tile + 128] = new[rows : rows + 4]
        for side in range(2):
            for page in range(8):
                home = jnp.clip(owner_ref[page] - rep * 4, 0, 3)
                place = jnp.where(tail_ref[page] == 1, fill_ref[page], -1)
                fresh = kv[side, pl.ds(home, 1), :]
                old = cache_ref[layer, side, page].astype(F32)
                held[layer, side, page] = jnp.where(spot == place, fresh, old).astype(BF16)
        sends.append(
            pltpu.make_async_copy(held.at[layer], pages_ref.at[layer], sems.at[layer])
        )
        sends[-1].start()
    for send in sends:
        send.wait()


def renew(tables, one, two, caches):
    return call(
        renew_kernel,
        "renew",
        (jax.ShapeDtypeStruct(caches.shape, BF16),),
        [
            pltpu.VMEM(caches.shape, BF16),
            pltpu.VMEM((2, 4, 512), F32),
            pltpu.SemaphoreType.DMA((2,)),
        ],
        tables,
        one,
        two,
        caches,
        far_outs=(0,),
    )[0]


def output_kernel(layer, got_ref, wo_ref, wf_ref, out_ref):
    att = jnp.concatenate([got_ref[:16], got_ref[64:80]], axis=0).astype(F32)
    att = att + pltpu.roll(att, HD, 1)
    att = jnp.concatenate([att] * 4, axis=1)
    own = iota((32, 512), 1) // HD == iota((32, 512), 0) // 16 * 4 + iota((32, 512), 0) % 4
    by_head = dot_t(jnp.where(own, att, 0.0).astype(BF16), wo_ref[layer])
    tiles = []
    for core in range(2):
        act = got_ref[64 * core + 16 : 64 * core + 48].astype(F32)
        tiles += [act[4 * m : 4 * m + 4] for m in range(8)]
    mlp = dot_t(jnp.concatenate(tiles, axis=1).astype(BF16), wf_ref[layer])
    rows = [
        jnp.sum(by_head[4 * i : 4 * i + 4] + by_head[16 + 4 * i : 20 + 4 * i], axis=0, keepdims=True)
        + mlp[i : i + 1]
        for i in range(4)
    ]
    tile = jnp.concatenate(rows, axis=0)
    tile = jnp.concatenate([tile, jnp.zeros_like(tile)], axis=1)
    for k in range(4):
        out_ref[4 * k : 4 * k + 4] = tile


def output(layer, got, w_out, w_fc2):
    return call(
        functools.partial(output_kernel, layer),
        "output",
        (near_out((16, 128), F32),),
        [],
        (),
        got,
        w_out,
        w_fc2,
    )[0]


def per_device(
    hidden,
    ln_gain,
    w_qkv,
    w_fc1,
    w_out,
    w_fc2,
    caches,
    page_owner,
    page_used,
    page_fill,
    page_tail,
    positions,
):
    zs = [[2 * z + c for z in range(16)] for c in range(2)]
    pairs = [[2 * z, 2 * z + 1] for z in range(16)]
    rep_core = [[r * 32 + 2 * z + c for r in range(4) for c in range(2)] for z in range(16)]

    more = (positions.reshape(1, 4),)
    w_qkv = w_qkv.transpose(0, 2, 1, 3)
    w_out = w_out.transpose(0, 2, 1)
    w_fc2 = w_fc2.transpose(0, 2, 1)

    state, gain, joined = hidden, ln_gain, []
    for layer in range(LAYERS):
        parts, state, *kept = project(layer, state, gain, w_qkv, w_fc1, *more)
        if layer == 0:
            gain, factors = kept
        parts = lax.all_gather(parts, "blk", axis_index_groups=pairs)
        got = exchange(pool(parts).reshape(16, FLOW // 2, 2, 128), "blk", zs)
        packed, query, extra = finish(got.reshape(16 * FLOW, 128), factors)
        got = exchange(packed, ("rep", "blk"), rep_core)
        parts = attend(layer, (page_owner, page_used, page_fill), got, caches)
        parts = exchange(parts.reshape(8, 16, 128), ("rep", "blk"), rep_core)
        got = exchange(join(parts, extra).reshape(16, JOIN // 2, 2, 128), "blk", zs)
        got = settle(got.reshape(16 * JOIN, 128), query)
        got = lax.all_gather(got, "blk", axis_index_groups=pairs, tiled=True)
        joined.append(got)
        out = output(layer, got, w_out, w_fc2).reshape(4, 4, 128)
        out = exchange(out, "tp")
        more = (out.reshape(16, 128),)
    result = (state[:, :HD] + jnp.sum(out, axis=0)[:, :HD]).astype(BF16)
    return (result, renew((page_owner, page_fill, page_tail), *joined, caches))


def solution(mesh):
    in_specs = (
        P("rep", "blk"),
        P(None, "blk"),
        P(None, "blk", None, "tp"),
        P(None, "blk", "tp"),
        P(None, "tp", "blk"),
        P(None, "tp", "blk"),
        P(None, None, ("rep", "blk"), None, "tp"),
        P(("rep", "blk")),
        P(("rep", "blk")),
        P(("rep", "blk")),
        P(("rep", "blk")),
        P("rep"),
    )
    out_specs = (P("rep", "blk"), P(None, None, ("rep", "blk"), None, "tp"))
    return jax.shard_map(
        per_device, mesh=mesh, in_specs=in_specs, out_specs=out_specs, check_vma=False
    )
```

```python
import functools
import math

import jax
import jax.numpy as jnp
import numpy as np
from jax import lax
from jax.experimental import pallas as pl
from jax.experimental.pallas import tpu as pltpu
from jax.sharding import PartitionSpec as P

D = 2048
HD = 64
ROT = 32
LAYERS = 2
PAGE = 32
EPSILON = 1e-05
LOWEST = -1e30
F32 = jnp.float32
BF16 = jnp.bfloat16
INVERSE = [float(np.float32(10000.0 ** (-2.0 * k / ROT))) for k in range(ROT // 2)]
TWO_PI_MIDDLE = float(np.floor((2.0 * math.pi - 6.28125) * 2.0**21) / 2.0**21)
TWO_PI_LAST = 2.0 * math.pi - 6.28125 - TWO_PI_MIDDLE
INTERPRET = False
HALF = 232
FLOW = 16
JOIN = 20


def exchange(value, axis, groups=None):
    return lax.all_to_all(value, axis, 0, 0, tiled=True, axis_index_groups=groups)


def rope_factors(positions):
    lane = iota((positions.shape[0], 128), 1) % HD
    inverse = jnp.zeros(lane.shape, F32)
    for k in range(ROT // 2):
        inverse = jnp.where(lane % (ROT // 2) == k, INVERSE[k], inverse)
    angles = positions * inverse
    turns = jnp.floor(angles * (1.0 / (2.0 * math.pi)) + 0.5)
    angles = angles - turns * 6.28125
    angles = angles - turns * TWO_PI_MIDDLE
    angles = angles - turns * TWO_PI_LAST
    sine = jnp.sin(angles)
    return jnp.where(lane < 32, jnp.cos(angles), jnp.where(lane < 48, -sine, sine))


def near(value):
    return value if INTERPRET else pltpu.with_memory_space_constraint(value, pltpu.VMEM)


def away(value):
    return value if INTERPRET else pltpu.with_memory_space_constraint(value, pltpu.HBM)


def near_out(shape, dtype):
    return jax.ShapeDtypeStruct(shape, dtype) if INTERPRET else pltpu.VMEM(shape, dtype)


def iota(shape, axis):
    return lax.broadcasted_iota(jnp.int32, shape, axis)


def dot32(left, right):
    return jnp.dot(left, right, preferred_element_type=F32)


def dot_t(left, right):
    return lax.dot_general(left, right, (((1,), (1,)), ((), ())), preferred_element_type=F32)


def parts_of(value, count):
    found = []
    for _ in range(count):
        part = value.astype(BF16).astype(F32)
        found.append(part)
        value = value - part
    return found


def rope(value, factors):
    lane = iota(value.shape, 1)
    left = lane < HD
    half = ROT // 2
    cosine = jnp.where(left, pltpu.roll(factors, 64, 1), factors)
    sine = jnp.where(left, pltpu.roll(factors, 32, 1), pltpu.roll(factors, 96, 1))
    other = jnp.where(
        lane % HD < half, pltpu.roll(value, 128 - half, 1), pltpu.roll(value, half, 1)
    )
    return jnp.where(lane % HD < ROT, value * cosine + other * sine, value)


def gelu(value):
    cubed = value * value * value
    return 0.5 * value * (1.0 + jnp.tanh(math.sqrt(2.0 / math.pi) * (value + 0.044715 * cubed)))


def column_of(row, first, period, shape):
    mine = iota(shape, 1) == first + iota(shape, 0) % period
    return jnp.sum(jnp.where(mine, row, 0.0), axis=1, keepdims=True)


def page_holders(owners, used, fills):
    page_of = iota((1, 256), 1) // PAGE
    owner = jnp.zeros((1, 256), jnp.int32)
    limit = jnp.zeros((1, 256), jnp.int32)
    for page in range(8):
        length = jnp.where(used[page] == 1, fills[page], 0)
        owner = jnp.where(page_of == page, owners[page], owner)
        limit = jnp.where(page_of == page, length, limit)
    return jnp.where(iota((1, 256), 1) % PAGE < limit, owner, -1)


def project_kernel(layer, x_ref, gain_ref, wq_ref, wf_ref, *refs):
    if layer == 0:
        pos_ref, *table_refs = refs[:4]
        out_ref, state_ref, gain_held, factor_ref, holder_ref = refs[4:9]
        q_held, f_held, x_held, pos_held, *tables, sems = refs[9:]
        copies = [
            pltpu.make_async_copy(x_ref, x_held, sems.at[0]),
            pltpu.make_async_copy(gain_ref, gain_held, sems.at[1]),
            pltpu.make_async_copy(wq_ref.at[0], q_held, sems.at[2]),
            pltpu.make_async_copy(wf_ref.at[0], f_held, sems.at[3]),
            pltpu.make_async_copy(pos_ref, pos_held, sems.at[4]),
        ]
        copies += [
            pltpu.make_async_copy(table_refs[k], tables[k], sems.at[5 + k]) for k in range(3)
        ]
        for copy in copies:
            copy.start()
        copies[0].wait()
        copies[1].wait()
        x = x_held[...].astype(F32)
        gain_ref = gain_held
        copies[4].wait()
        places = jnp.broadcast_to(pos_held[...].astype(F32), (4, 4))
        mine = iota((4, 4), 0) == iota((4, 4), 1)
        places = jnp.sum(jnp.where(mine, places, 0.0), axis=1, keepdims=True)
        factor_ref[...] = rope_factors(places)
        for copy in copies[5:]:
            copy.wait()
        holder_ref[...] = page_holders(*tables)
    else:
        branch_ref, out_ref, state_ref = refs
        x = x_ref[...] + branch_ref[0:4] + branch_ref[4:8] + branch_ref[8:12] + branch_ref[12:16]
        x = x.astype(BF16).astype(F32)[:, :HD]
    state_ref[...] = jnp.concatenate([x, jnp.zeros_like(x)], axis=1)
    gain = gain_ref[layer : layer + 1]
    mean = jnp.sum(x, axis=1, keepdims=True) * (1.0 / HD)
    centered = x - mean
    square = jnp.sum(centered * centered, axis=1, keepdims=True)
    rows = jnp.concatenate([centered * gain, jnp.broadcast_to(gain, (4, HD))], axis=0)
    high, low = parts_of(rows, 2)
    high, low = high.astype(BF16), low.astype(BF16)
    if layer == 0:
        copies[2].wait()
    for k in range(3):
        weights = q_held[k] if layer == 0 else wq_ref[layer, k]
        every = dot32(high, weights) + dot32(low, weights)
        for j in range(4):
            start = 8 * (4 * k + j)
            out_ref[start : start + 8] = every[:, 128 * j : 128 * j + 128]
    if layer == 0:
        copies[3].wait()
    weights = f_held[...] if layer == 0 else wf_ref[layer]
    every = dot32(high, weights) + dot32(low, weights)
    for j in range(16):
        out_ref[96 + 8 * j : 104 + 8 * j] = every[:, 128 * j : 128 * j + 128]
    lane = iota((4, 128), 1)
    request = iota((4, 128), 0)
    stats = jnp.where(lane == request, mean, jnp.where(lane == request + 16, square, 0.0))
    out_ref[224:232] = jnp.broadcast_to(jnp.sum(stats, axis=0, keepdims=True), (8, 128))


def call(kernel, name, outs, scratch, tables, *args, far=(), far_outs=(), aliases=None):
    near_spec = pl.BlockSpec(memory_space=pltpu.VMEM)
    far_spec = pl.BlockSpec(memory_space=pl.ANY)
    specs = [pl.BlockSpec(memory_space=pltpu.SMEM) for _ in tables]
    specs += [far_spec if k in far else near_spec for k in range(len(args))]
    args = [away(arg) if k in far else near(arg) for k, arg in enumerate(args)]
    return pl.pallas_call(
        kernel,
        in_specs=specs,
        out_specs=tuple(far_spec if k in far_outs else near_spec for k in range(len(outs))),
        out_shape=tuple(outs),
        scratch_shapes=scratch,
        input_output_aliases=aliases or {},
        compiler_params=pltpu.CompilerParams(vmem_limit_bytes=24 * 2**20),
        name=name,
        interpret=INTERPRET,
    )(*tables, *args)


def project(layer, x, gain, wq, wf, *more):
    outs = [near_out((HALF, 128), F32), near_out((4, 128), F32)]
    scratch = []
    if layer == 0:
        outs += [near_out(gain.shape, F32), near_out((4, 128), F32)]
        outs += [near_out((1, 256), jnp.int32)]
        scratch = [
            pltpu.VMEM(wq.shape[1:], BF16),
            pltpu.VMEM(wf.shape[1:], BF16),
            pltpu.VMEM(x.shape, x.dtype),
            pltpu.VMEM((1, 4), jnp.int32),
            *[pltpu.SMEM((8,), jnp.int32) for _ in range(3)],
            pltpu.SemaphoreType.DMA((8,)),
        ]
    return call(
        functools.partial(project_kernel, layer),
        "project",
        outs,
        scratch,
        (),
        x,
        gain,
        wq,
        wf,
        *more,
        far=range(8) if layer == 0 else (),
    )


def pool_kernel(got_ref, out_ref):
    core = lax.axis_index("blk") % 2
    means = [got_ref[s, 224:225] for s in range(2)]
    center = 0.5 * (means[0] + means[1])
    moves = [mean - center for mean in means]
    square = pltpu.roll(means[0] + means[1], 112, 1) + 64.0 * (
        moves[0] * moves[0] + moves[1] * moves[1]
    )
    upper = iota((8, 1), 0) < 4
    shift = [jnp.where(upper, column_of(move, 0, 4, (8, 128)), 0.0) for move in moves]

    def block(start):
        total = 0.0
        for s in range(2):
            part = got_ref[s, pl.ds(pl.multiple_of(start, 8), 8), :]
            total = total + part + shift[s] * part[4:5]
        return total

    merged = []
    columns = []
    for base in (0, 32, 64):
        one = block(base + 16 * core)
        two = block(base + 16 * core + 8)
        merged.append(jnp.where(upper, one, pltpu.roll(two, 4, 0)))
        columns.append((one[4:5], two[4:5]))
    lane = iota((4, 128), 1)
    request = iota((4, 128), 0)
    stats = jnp.zeros((4, 128), F32)
    both = parts_of(column_of(center, 0, 4, (4, 128)), 3)
    both += parts_of(column_of(square, 0, 4, (4, 128)), 3)
    for k, part in enumerate(both):
        stats = jnp.where(lane == request + 16 * k, part, stats)
    stats = jnp.sum(stats, axis=0, keepdims=True)
    row = iota((8, 128), 0)
    base = jnp.where(row == 0, columns[0][0], jnp.where(row == 1, columns[0][1], stats))
    for m in range(8):
        last = block(96 + 64 * core + 8 * m)
        for k in range(2):
            z = 2 * m + k
            side, slot = 1 + z // 8, z % 8
            rows = (
                merged[side][slot : slot + 1],
                columns[side][slot // 4],
                last[4:5],
                last[2 * k : 2 * k + 1],
                last[2 * k + 1 : 2 * k + 2],
            )
            tail = base
            for j, value in enumerate(rows):
                tail = jnp.where(row == 3 + j, value, tail)
            whole = jnp.concatenate([merged[0], tail], axis=0)
            out_ref[FLOW * z : FLOW * z + FLOW] = whole.astype(BF16)


def pool(got):
    return call(
        pool_kernel,
        "pool",
        (near_out((16 * FLOW, 128), BF16),),
        [],
        (),
        got,
    )[0]


def finish_kernel(got_ref, factor_ref, out_ref, held_ref, extra_ref):
    blocks = [got_ref[FLOW * z : FLOW * z + FLOW].astype(F32) for z in range(16)]
    stats = jnp.concatenate([block[10:11] for block in blocks], axis=0)
    stats = stats + pltpu.roll(stats, 112, 1) + pltpu.roll(stats, 96, 1)
    average = jnp.sum(stats, axis=0, keepdims=True) * (1.0 / 16)
    offset = stats - average
    spread_sum = 128.0 * jnp.sum(offset * offset, axis=0, keepdims=True)
    square_sum = pltpu.roll(jnp.sum(stats, axis=0, keepdims=True), 80, 1)
    rstd = lax.rsqrt((square_sum + spread_sum) * (1.0 / D) + EPSILON)
    upper = iota((8, 128), 0) < 4
    here = lax.axis_index("blk") // 2
    pair, single = 2 * (here % 2), here % 4
    query, entry, inner = 0.0, 0.0, 0.0
    for z, block in enumerate(blocks):
        move = offset[z : z + 1]
        column = jnp.where(upper, block[8:9], block[9:10])
        query = query + block[:8] + column_of(move, 0, 4, (8, 128)) * column
        entry = entry + block[11:12] + column_of(move, single, 1, (1, 128)) * block[12:13]
        inner = inner + block[14:16] + column_of(move, pair, 2, (2, 128)) * block[13:14]
    query = column_of(rstd, 0, 4, (8, 128)) * query
    query = rope(query, jnp.concatenate([factor_ref[...], factor_ref[...]], axis=0)).astype(BF16)
    for k in range(8):
        out_ref[k] = query
    held_ref[...] = query.astype(F32)
    entry = column_of(rstd, single, 1, (1, 128)) * entry
    turned = rope(entry, factor_ref[pl.ds(single, 1), :])
    extra_ref[0:2] = gelu(column_of(rstd, pair, 2, (2, 128)) * inner)
    extra_ref[2:3] = jnp.where(jnp.full((1, 128), here) < 8, turned, entry)
    extra_ref[3:4] = jnp.zeros((1, 128), F32)


def finish(got, factors):
    return call(
        finish_kernel,
        "finish",
        (near_out((8, 8, 128), BF16), near_out((8, 128), F32), near_out((4, 128), F32)),
        [],
        (),
        got,
        factors,
    )


def attend_kernel(layer, got_ref, cache_ref, holder_ref, out_ref):
    tiles = []
    for tile in range(4):
        core, rows = tile // 2, 4 * (tile % 2)
        parts = [got_ref[2 * r + core].astype(F32)[rows : rows + 4] for r in range(4)]
        tiles.append(jnp.concatenate(parts, axis=0))
    queries = jnp.concatenate(tiles, axis=1)
    place = iota((8, 512), 0)
    wide = []
    for rep in range(4):
        for core in range(2):
            for i in (0, 2):
                row = 4 * rep + i
                both = jnp.where(place < 4, queries[row : row + 1], queries[row + 1 : row + 2])
                mine = iota((8, 512), 1) // HD == 4 * core + place % 4
                wide.append(jnp.where(mine, both, 0.0))
    wide = jnp.concatenate(wide, axis=0).astype(BF16)
    keys = cache_ref[layer, 0].reshape(8 * PAGE, 512)
    values = cache_ref[layer, 1].reshape(8 * PAGE, 512)
    scores = dot_t(wide, keys) * HD ** (-0.5)
    pair = iota((128, 256), 0)
    allowed = 4 * (pair // 32) + pair % 16 // 4 == holder_ref[...]
    scores = jnp.where(allowed, scores, LOWEST)
    high = jnp.max(scores, axis=1, keepdims=True)
    weights = jnp.where(allowed, jnp.exp(scores - high), 0.0)
    total = jnp.sum(weights, axis=1, keepdims=True)
    mixed = dot32(weights.astype(BF16), values)
    head = iota((128, 128), 0) // 16 % 2 * 4 + iota((128, 128), 0) % 4
    lane = iota((128, 128), 1)
    picked = mixed[:, :128]
    for k in range(1, 4):
        picked = jnp.where(head // 2 == k, mixed[:, 128 * k : 128 * k + 128], picked)
    picked = jnp.where(head % 2 == 1, pltpu.roll(picked, HD, 1), picked)
    out_ref[...] = jnp.where(
        lane < HD, picked, jnp.where(lane == HD, total, jnp.where(lane == HD + 1, high, 0.0))
    )


def attend(layer, got, caches, holders):
    return call(
        functools.partial(attend_kernel, layer),
        "attend",
        (near_out((128, 128), F32),),
        [],
        (),
        got,
        caches,
        holders,
    )[0]


def join_kernel(got_ref, act_ref, out_ref, wire):
    got = got_ref[...]
    high = got[:, :, HD + 1 : HD + 2]
    top = jnp.max(high, axis=0)
    total = jnp.sum(got * jnp.exp(high - top[None]), axis=0)
    lane = iota((16, 128), 1)
    out = jnp.where(lane < HD, total, 0.0)
    extra = parts_of(total[:, HD : HD + 1], 3) + parts_of(top, 3)
    for k, part in enumerate(extra):
        out = jnp.where(lane == HD + k, part, out)
    act = act_ref[...]
    for z in range(16):
        wire[JOIN * z : JOIN * z + 16] = out
        wire[JOIN * z + 16 : JOIN * z + 20] = act
    out_ref[...] = wire[...].astype(BF16)


def join(got, act):
    return call(
        join_kernel,
        "join",
        (near_out((16 * JOIN, 128), BF16),),
        [pltpu.VMEM((16 * JOIN, 128), F32)],
        (),
        got,
        act,
    )[0]


def settle_kernel(got_ref, query_ref, out_ref, wire, back, score, fresh):
    wire[...] = got_ref[...].astype(F32)
    entries = wire[pl.ds(18, 16, stride=JOIN), :]
    product = query_ref[...] * entries[:8]
    left = iota((8, 128), 1) < HD
    for half in range(2):
        summed = jnp.sum(jnp.where(left == (half == 0), product, 0.0), axis=1, keepdims=True)
        summed = jnp.broadcast_to(summed * HD ** (-0.5), (8, 128))
        value = entries[8:] if half == 0 else pltpu.roll(entries[8:], HD, 1)
        for j in range(2):
            score[pl.ds(2 * j + half, 4, stride=4), :] = summed[4 * j : 4 * j + 4]
            fresh[pl.ds(2 * j + half, 4, stride=4), :] = value[4 * j : 4 * j + 4]
    parts = [wire[JOIN * z : JOIN * z + 16] for z in range(16)]
    take = lambda part, k: part[:, HD + k : HD + k + 1]
    highs = [take(part, 3) + take(part, 4) + take(part, 5) for part in parts]
    own = score[:, 0:1]
    top = functools.reduce(jnp.maximum, highs, own)
    total = jnp.exp(own - top)
    mixed = fresh[...] * total
    for part, high in zip(parts, highs):
        factor = jnp.exp(high - top)
        total = total + (take(part, 0) + take(part, 1) + take(part, 2)) * factor
        mixed = mixed + part * factor
    back[:16] = jnp.where(iota((16, 128), 1) < HD, mixed / total, 0.0)
    for k in range(2):
        back[pl.ds(16 + k, 16, stride=2), :] = wire[pl.ds(16 + k, 16, stride=JOIN), :]
    back[48:] = entries
    out_ref[...] = back[...].astype(BF16)


def settle(got, query):
    return call(
        settle_kernel,
        "settle",
        (near_out((64, 128), BF16),),
        [
            pltpu.VMEM((16 * JOIN, 128), F32),
            pltpu.VMEM((64, 128), F32),
            pltpu.VMEM((16, 128), F32),
            pltpu.VMEM((16, 128), F32),
        ],
        (),
        got,
        query,
    )[0]


def renew_kernel(owner_ref, fill_ref, tail_ref, one_ref, two_ref, cache_ref, pages_ref, held, kv, sems):
    rep = lax.axis_index("rep")
    spot = iota((PAGE, 512), 0)
    sends = []
    for layer, got_ref in enumerate((one_ref, two_ref)):
        for tile in range(4):
            start = 64 * (tile // 2) + 48
            new = got_ref[start : start + 16].astype(F32)
            for side in range(2):
                rows = 8 * side + 4 * (tile % 2)
                kv[side, :, 128 * tile : 128 * tile + 128] = new[rows : rows + 4]
        for side in range(2):
            for page in range(8):
                home = jnp.clip(owner_ref[page] - rep * 4, 0, 3)
                place = jnp.where(tail_ref[page] == 1, fill_ref[page], -1)
                fresh = kv[side, pl.ds(home, 1), :]
                old = cache_ref[layer, side, page].astype(F32)
                held[layer, side, page] = jnp.where(spot == place, fresh, old).astype(BF16)
        sends.append(
            pltpu.make_async_copy(held.at[layer], pages_ref.at[layer], sems.at[layer])
        )
        sends[-1].start()
    for send in sends:
        send.wait()


def renew(tables, one, two, caches):
    return call(
        renew_kernel,
        "renew",
        (jax.ShapeDtypeStruct(caches.shape, BF16),),
        [
            pltpu.VMEM(caches.shape, BF16),
            pltpu.VMEM((2, 4, 512), F32),
            pltpu.SemaphoreType.DMA((2,)),
        ],
        tables,
        one,
        two,
        caches,
        far_outs=(0,),
    )[0]


def output_kernel(layer, got_ref, wo_ref, wf_ref, out_ref):
    att = jnp.concatenate([got_ref[:16], got_ref[64:80]], axis=0).astype(F32)
    att = att + pltpu.roll(att, HD, 1)
    att = jnp.concatenate([att] * 4, axis=1)
    own = iota((32, 512), 1) // HD == iota((32, 512), 0) // 16 * 4 + iota((32, 512), 0) % 4
    by_head = dot_t(jnp.where(own, att, 0.0).astype(BF16), wo_ref[layer])
    tiles = []
    for core in range(2):
        act = got_ref[64 * core + 16 : 64 * core + 48].astype(F32)
        tiles += [act[4 * m : 4 * m + 4] for m in range(8)]
    mlp = dot_t(jnp.concatenate(tiles, axis=1).astype(BF16), wf_ref[layer])
    rows = [
        jnp.sum(by_head[4 * i : 4 * i + 4] + by_head[16 + 4 * i : 20 + 4 * i], axis=0, keepdims=True)
        + mlp[i : i + 1]
        for i in range(4)
    ]
    tile = jnp.concatenate(rows, axis=0)
    tile = jnp.concatenate([tile, jnp.zeros_like(tile)], axis=1)
    for k in range(4):
        out_ref[4 * k : 4 * k + 4] = tile


def output(layer, got, w_out, w_fc2):
    return call(
        functools.partial(output_kernel, layer),
        "output",
        (near_out((16, 128), F32),),
        [],
        (),
        got,
        w_out,
        w_fc2,
    )[0]


def per_device(
    hidden,
    ln_gain,
    w_qkv,
    w_fc1,
    w_out,
    w_fc2,
    caches,
    page_owner,
    page_used,
    page_fill,
    page_tail,
    positions,
):
    zs = [[2 * z + c for z in range(16)] for c in range(2)]
    pairs = [[2 * z, 2 * z + 1] for z in range(16)]
    rep_core = [[r * 32 + 2 * z + c for r in range(4) for c in range(2)] for z in range(16)]

    more = (positions.reshape(1, 4), page_owner, page_used, page_fill)
    w_qkv = w_qkv.transpose(0, 2, 1, 3)
    w_out = w_out.transpose(0, 2, 1)
    w_fc2 = w_fc2.transpose(0, 2, 1)

    state, gain, joined = hidden, ln_gain, []
    for layer in range(LAYERS):
        parts, state, *kept = project(layer, state, gain, w_qkv, w_fc1, *more)
        if layer == 0:
            gain, factors, holders = kept
        parts = lax.all_gather(parts, "blk", axis_index_groups=pairs)
        got = exchange(pool(parts).reshape(16, FLOW // 2, 2, 128), "blk", zs)
        packed, query, extra = finish(got.reshape(16 * FLOW, 128), factors)
        got = exchange(packed, ("rep", "blk"), rep_core)
        parts = attend(layer, got, caches, holders)
        parts = exchange(parts.reshape(8, 16, 128), ("rep", "blk"), rep_core)
        got = exchange(join(parts, extra).reshape(16, JOIN // 2, 2, 128), "blk", zs)
        got = settle(got.reshape(16 * JOIN, 128), query)
        got = lax.all_gather(got, "blk", axis_index_groups=pairs, tiled=True)
        joined.append(got)
        out = output(layer, got, w_out, w_fc2).reshape(4, 4, 128)
        out = exchange(out, "tp")
        more = (out.reshape(16, 128),)
    out, joined[1] = lax.optimization_barrier((out, joined[1]))
    result = (state[:, :HD] + jnp.sum(out, axis=0)[:, :HD]).astype(BF16)
    return (result, renew((page_owner, page_fill, page_tail), *joined, caches))


def solution(mesh):
    in_specs = (
        P("rep", "blk"),
        P(None, "blk"),
        P(None, "blk", None, "tp"),
        P(None, "blk", "tp"),
        P(None, "tp", "blk"),
        P(None, "tp", "blk"),
        P(None, None, ("rep", "blk"), None, "tp"),
        P(("rep", "blk")),
        P(("rep", "blk")),
        P(("rep", "blk")),
        P(("rep", "blk")),
        P("rep"),
    )
    out_specs = (P("rep", "blk"), P(None, None, ("rep", "blk"), None, "tp"))
    return jax.shard_map(
        per_device, mesh=mesh, in_specs=in_specs, out_specs=out_specs, check_vma=False
    )
```
